32 devices in a mesh: grp: 2 (over x), lat: 16 (over z, y, core).
Axes of the slice: x: 2, y: 2, z: 4, core: 2. Of those that a mesh axis runs over, the one named last changes fastest.
Arguments:
- coarse: bfloat16 [80, 64, 512], P(None, ('grp', 'lat')), parts along dimension 1, may hold values from -6 to 6
- reg_gain: float32 [2, 80], replicated, may hold values from 0.25 to 1.75
- reg_weight: bfloat16 [2, 3, 3, 80, 80], replicated, may hold values from -0.21875 to 0.21875
- reg_bias: float32 [2, 80], replicated, may hold values from -1.5 to 1.5
- noisy: bfloat16 [32, 4, 32, 512], P(('grp', 'lat')), parts along dimension 0, may hold values from -6 to 6
- lift_weight: bfloat16 [3, 3, 192, 84], replicated, may hold values from -0.21875 to 0.21875
- lift_bias: float32 [192], replicated, may hold values from -1.5 to 1.5
- mid_gain: float32 [192], replicated, may hold values from 0.25 to 1.75
- mid_weight: bfloat16 [3, 3, 192, 192], replicated, may hold values from -0.15625 to 0.15625
- mid_bias: float32 [192], replicated, may hold values from -1.5 to 1.5
Outputs:
- fine_level: bfloat16 [32, 192, 32, 512], P(('grp', 'lat')), parts along dimension 0
The draws below stay inside these ranges and needn't reach their ends.
There are 2 independent parts, one for each index of `grp`. The reference program is written for one: setup_inputs(seed, part) draws one part's arguments, and reference() takes and returns one part's arrays. A program takes and returns all parts, laid end to end along the dimension named above; an argument that names none is the same for every part. Nothing has to cross between parts.
All inputs are finite; a program needn't handle non-finite values.
Results may differ from the reference program's by a relative error of at most 0.007.
Values may be sent and summed in bfloat16 or wider, within the bound.
A program may use at most 320 MiB of HBM per device.

```python
import jax
import jax.numpy as jnp
from jax import lax

CIN = 80
CH = 192
NOUT = 4
REG_BLOCKS = 2
CLON = 512
TILE_COLS = 4
LAT_UP = 4
LON_UP = 4
NCR = 32
TILE_ROWS = 4
FT_ROWS = 32
FT_LON = 512
FLAT = 128
FLON = 2048
N_LAT = 16


def shard_levels(own_key, extent, cuts, least, top_value):
    def one(dim, blocks):
        draws = jax.random.uniform(jax.random.fold_in(jax.random.fold_in(own_key, 6), dim), (blocks,), jnp.float32, least / len(cuts), top_value / len(cuts))
        return jnp.repeat(jnp.exp(draws), extent[dim] // blocks).reshape((-1,) + (1,) * (len(extent) - dim - 1))

    level = one(*cuts[0])
    for cut in cuts[1:]:
        level = level * one(*cut)
    return level


def gaussian(key, shape, width, bound, shards=(), kind=jnp.bfloat16):
    level = shard_levels(key, shape, shards, -0.22, 0.18) if shards else 1.0
    entries = jax.random.normal(key, shape, jnp.float32) * width * level
    return jnp.minimum(jnp.maximum(entries, -bound), bound).astype(kind)


def setup_inputs(seed: int = 0, part: int = 0) -> dict:
    arg_keys = jax.random.split(jax.random.key(seed), 11)
    part_splits = jax.random.split(jax.random.fold_in(arg_keys[10], part), 11)
    coarse = gaussian(part_splits[0], (CIN, NCR, CLON), 1.0, 6.0, ((1, 16),))
    reg_gain = jnp.clip(1.0 + 0.15 * jax.random.normal(arg_keys[1], (REG_BLOCKS, CIN), jnp.float32), 0.25, 1.75)
    reg_weight = gaussian(arg_keys[2], (REG_BLOCKS, 3, 3, CIN, CIN), (9 * CIN) ** -0.5, 0.21875)
    reg_bias = gaussian(arg_keys[3], (REG_BLOCKS, CIN), 0.3, 1.5, (), jnp.float32)
    noisy = gaussian(part_splits[4], (N_LAT, NOUT, FT_ROWS, FT_LON), 1.0, 6.0, ((0, 16),))
    lift_weight = gaussian(arg_keys[5], (3, 3, CH, CIN + NOUT), (9 * (CIN + NOUT)) ** -0.5, 0.21875)
    lift_bias = gaussian(arg_keys[6], (CH,), 0.3, 1.5, (), jnp.float32)
    mid_gain = jnp.clip(1.0 + 0.15 * jax.random.normal(arg_keys[7], (CH,), jnp.float32), 0.25, 1.75)
    mid_weight = gaussian(arg_keys[8], (3, 3, CH, CH), (9 * CH) ** -0.5, 0.15625)
    mid_bias = gaussian(arg_keys[9], (CH,), 0.3, 1.5, (), jnp.float32)
    return dict(coarse=coarse, reg_gain=reg_gain, reg_weight=reg_weight, reg_bias=reg_bias, noisy=noisy, lift_weight=lift_weight, lift_bias=lift_bias, mid_gain=mid_gain, mid_weight=mid_weight, mid_bias=mid_bias)


EPSILON = 1e-06
HIGHEST = lax.Precision.HIGHEST

def activate(field_in, gain_row):
    values = field_in.astype(jnp.float32)
    inverse = lax.rsqrt(lax.optimization_barrier(jnp.mean(values * values, axis=0, keepdims=True)) + EPSILON)
    return jax.nn.silu(values * inverse * gain_row[:, None, None]).astype(jnp.bfloat16)

def wrap_cols(field_in):
    return jnp.concatenate([field_in[:, :, -1:], field_in, field_in[:, :, :1]], axis=2)

def pad_rows(field_in):
    return jnp.pad(field_in, ((0, 0), (1, 1), (0, 0)))

def conv_taps(padded, weight):
    channels = padded.shape[0]
    height = padded.shape[1] - 2
    breadth = padded.shape[2] - 2
    summed = jnp.zeros((weight.shape[2], height * breadth), jnp.float32)
    for row_shift in range(3):
        for col_shift in range(3):
            window = padded[:, row_shift:row_shift + height, col_shift:col_shift + breadth].reshape(channels, height * breadth)
            summed = summed + jnp.dot(weight[row_shift, col_shift], window, preferred_element_type=jnp.float32)
    return summed.reshape(weight.shape[2], height, breadth)

def blend_matrix(fine_count, coarse_count, factor, clamped):
    fine_index = jnp.arange(fine_count, dtype=jnp.int32)
    numerator = 2 * fine_index + 1 - factor
    lower_cell = numerator // (2 * factor)
    fraction = (numerator - 2 * factor * lower_cell).astype(jnp.float32) / (2.0 * factor)
    if clamped:
        low_side = numerator < 0
        high_side = lower_cell >= coarse_count - 1
        lower_cell = jnp.where(low_side, 0, jnp.where(high_side, coarse_count - 1, lower_cell))
        fraction = jnp.where(low_side | high_side, 0.0, fraction)
        upper_cell = lower_cell + 1
    else:
        lower_cell = lower_cell % coarse_count
        upper_cell = (lower_cell + 1) % coarse_count
    columns = jnp.arange(coarse_count, dtype=jnp.int32)[None, :]
    first_part = jnp.where(columns == lower_cell[:, None], 1.0 - fraction[:, None], 0.0)
    second_part = jnp.where(columns == upper_cell[:, None], fraction[:, None], 0.0)
    return (first_part + second_part).astype(jnp.float32)

def reference(coarse, reg_gain, reg_weight, reg_bias, noisy, lift_weight, lift_bias, mid_gain, mid_weight, mid_bias):
    current = coarse
    for block_index in range(REG_BLOCKS):
        activated = activate(current, reg_gain[block_index])
        update = conv_taps(wrap_cols(pad_rows(activated)), reg_weight[block_index])
        updated = current.astype(jnp.float32) + update + reg_bias[block_index][:, None, None]
        current = lax.optimization_barrier(updated.astype(jnp.bfloat16))
    lat_blend = blend_matrix(FLAT, NCR, LAT_UP, True)
    lon_blend = blend_matrix(FLON, CLON, LON_UP, False)
    halfway = jnp.einsum('yi,cij->cyj', lat_blend, current.astype(jnp.float32), precision=HIGHEST)
    upsampled = jnp.einsum('cyj,xj->cyx', halfway, lon_blend, precision=HIGHEST).astype(jnp.bfloat16)
    noise_field = noisy.reshape(TILE_ROWS, TILE_COLS, NOUT, FT_ROWS, FT_LON).transpose(2, 0, 3, 1, 4).reshape(NOUT, FLAT, FLON)
    lift_input = jnp.concatenate([upsampled, noise_field], axis=0)
    lifted = conv_taps(wrap_cols(pad_rows(lift_input)), lift_weight) + lift_bias[:, None, None]
    lifted = lax.optimization_barrier(lifted.astype(jnp.bfloat16))
    activated = activate(lifted, mid_gain)
    summed = lifted.astype(jnp.float32) + conv_taps(wrap_cols(pad_rows(activated)), mid_weight) + mid_bias[:, None, None]
    fine_level = summed.astype(jnp.bfloat16)
    return fine_level.reshape(CH, TILE_ROWS, FT_ROWS, TILE_COLS, FT_LON).transpose(1, 3, 0, 2, 4).reshape(N_LAT, CH, FT_ROWS, FT_LON)
```

```python
import functools

import jax
import jax.numpy as jnp
from jax import lax
from jax.experimental import pallas as pl
from jax.experimental.pallas import tpu as pltpu
from jax.sharding import PartitionSpec as P

TILE_COLS = 4
LAT_UP = 4
LON_UP = 4
EPSILON = 1e-06
F32 = jnp.float32
BF16 = jnp.bfloat16
MESH = pl.DeviceIdType.MESH
HALF = 64


def activate(values, half_gain):
    inverse = lax.rsqrt(jnp.mean(values * values, axis=0, keepdims=True) + EPSILON)
    half = values * inverse * half_gain
    return half + half * jnp.tanh(half)


def split(numerator, factor):
    lower = numerator // (2 * factor)
    return lower, (numerator - 2 * factor * lower).astype(F32) / (2.0 * factor)


def column(row):
    n = row.shape[1]
    here = lax.broadcasted_iota(jnp.int32, (n, n), 0) == lax.broadcasted_iota(jnp.int32, (n, n), 1)
    return jnp.broadcast_to(jnp.sum(jnp.where(here, row, 0.0), axis=1, keepdims=True), (n, 128))


def nt_dot(a, b):
    return lax.dot_general(a, b, (((1,), (1,)), ((), ())), preferred_element_type=F32)


def first_kernel(
    coarse, noisy, gain, regb, regs, lifts, mids,
    field, ring, got_rows, liftw, midw, lon,
    band, pieces, got, tile, cols, rows, got_cols, far_rows, regv, liftv, midv, regw, liftt, held, part,
    send, recv, nsend, nrecv, local,
):
    me = lax.axis_index("lat")
    tile_rows = lax.axis_size("lat") // TILE_COLS
    r = me // TILE_COLS
    c = me % TILE_COLS
    north, south = r > 0, r < tile_rows - 1
    top, bottom = r == 0, r == tile_rows - 1
    cin, band_rows, clon = band.shape
    ch = midv.shape[1]
    nout, fr, fl = tile.shape
    blocks = regw.shape[0]
    halo = blocks + 1
    span = 2 * halo * TILE_COLS
    cw = held.shape[2]
    lines_n = held.shape[0]
    spare = (lines_n - band_rows * TILE_COLS) // 2

    barrier = pltpu.get_barrier_semaphore()

    def greet(target):
        pl.semaphore_signal(barrier, inc=1, device_id={"lat": target}, device_id_type=MESH)

    for k in range(1, TILE_COLS):
        greet(r * TILE_COLS + (c + k) % TILE_COLS)

    @pl.when(north)
    def _():
        for k in range(TILE_COLS):
            greet((r - 1) * TILE_COLS + k)

    @pl.when(south)
    def _():
        for k in range(TILE_COLS):
            greet((r + 1) * TILE_COLS + k)

    loads = [
        pltpu.make_async_copy(coarse, band, local.at[0]),
        pltpu.make_async_copy(noisy.at[0], tile, local.at[1]),
        pltpu.make_async_copy(regs, regv, local.at[2]),
        pltpu.make_async_copy(mids, midv, local.at[3]),
        pltpu.make_async_copy(lifts, liftv, local.at[4]),
    ]
    for load in loads:
        load.start()

    lane = lax.broadcasted_iota(jnp.int32, (1, 128), 1)
    loads[0].wait()
    for sub in range(band_rows):
        row = band[:, sub, :].astype(F32)
        parts = [row[:, b * 128:(b + 1) * 128] for b in range(TILE_COLS)]
        for b in range(TILE_COLS):
            pieces[b, sub, :cin, :] = parts[b].astype(BF16)
        side = jnp.zeros((16, 128), F32)
        for b in range(TILE_COLS):
            seam = jnp.where(lane < 64, parts[b], parts[(b + TILE_COLS - 1) % TILE_COLS])
            for g in range(cin // 16):
                at = g * span + 2 * halo * b
                moved = pltpu.roll(seam[g * 16:(g + 1) * 16], at + halo, 1)
                side = jnp.where(jnp.logical_and(lane >= at, lane < at + 2 * halo), moved, side)
        for b in range(TILE_COLS):
            pieces[b, sub, cin:, :] = side.astype(BF16)

    loads[1].wait()
    ends = []
    for n in range(nout):
        ends += [tile[n, :2, :].astype(F32), tile[n, fr - 2:, :].astype(F32)]
    rows[...] = jnp.concatenate(ends, axis=0).astype(BF16)
    pick_row = lax.broadcasted_iota(jnp.int32, (4 * nout, 128), 0)
    pick_lane = lax.broadcasted_iota(jnp.int32, (4 * nout, 128), 1)
    packed = jnp.zeros((4 * nout, fr), F32)
    for n in range(nout):
        for s, (lo, at) in enumerate(((0, 0), (0, 1), (fl - 128, 126), (fl - 128, 127))):
            if s % 2 == 0:
                hit = jnp.zeros(pick_row.shape, jnp.bool_)
            hit = jnp.logical_or(hit, jnp.logical_and(pick_row == s * nout + n, pick_lane == at))
            if s % 2:
                packed = packed + nt_dot(jnp.where(hit, 1.0, 0.0).astype(BF16), tile[n, :, lo:lo + 128])
    cols[...] = jnp.concatenate([packed, jnp.zeros((4 * nout, 128 - fr), F32)], axis=1).astype(BF16)

    peers = TILE_COLS - 1 + jnp.where(north, TILE_COLS, 0) + jnp.where(south, TILE_COLS, 0)
    pl.semaphore_wait(barrier, peers)

    def remote(src, dst, ssem, rsem, target):
        return pltpu.make_async_remote_copy(
            src_ref=src, dst_ref=dst, send_sem=ssem, recv_sem=rsem,
            device_id={"lat": target}, device_id_type=MESH)

    whole, upper, lower = (0, 2), (0, 1), (1, 1)

    def landing(slot, span_rows):
        return got.at[pl.ds(2 * slot + span_rows[0], span_rows[1])]

    def band_copy(k, row, slot, ssem, span_rows=whole):
        col = (c + k) % TILE_COLS
        return remote(pieces.at[col, pl.ds(*span_rows)], landing(slot, span_rows), send.at[ssem], recv.at[slot],
                      row * TILE_COLS + col)

    west, east = (c + TILE_COLS - 1) % TILE_COLS, (c + 1) % TILE_COLS

    def col_copy(slot, row, col):
        return remote(cols, got_cols.at[slot], nsend.at[slot], nrecv.at[slot], row * TILE_COLS + col)

    def row_copy(slot, row):
        return remote(rows, far_rows.at[slot], nsend.at[8 + slot], nrecv.at[8 + slot], row * TILE_COLS + c)

    def each_band(action):
        for col, side, row, slot, span_rows in (
            (2, south, r + 1, 0, lower), (3, south, r + 1, 1, whole),
            (0, north, r - 1, 6, whole), (1, north, r - 1, 7, upper),
        ):
            @pl.when(jnp.logical_and(side, c == col))
            def _():
                for k in range(TILE_COLS):
                    action(band_copy(k, row, slot, TILE_COLS + k, span_rows))

        for k in range(1, TILE_COLS):
            action(band_copy(k, r, 2 + c, k))

    def each_edge(action):
        action(col_copy(0, r, east))
        action(col_copy(1, r, west))

        @pl.when(south)
        def _():
            action(row_copy(0, r + 1))
            action(col_copy(6, r + 1, c))
            action(col_copy(2, r + 1, east))
            action(col_copy(3, r + 1, west))

        @pl.when(north)
        def _():
            action(row_copy(1, r - 1))
            action(col_copy(7, r - 1, c))
            action(col_copy(4, r - 1, east))
            action(col_copy(5, r - 1, west))

    each_band(lambda copy: copy.start())
    own = pltpu.make_async_copy(pieces.at[c], landing(2 + c, whole), local.at[5])
    own.start()

    loads[2].wait()
    for k in range(blocks):
        for p in range(3):
            for q in range(3):
                regw[k, p * cin:(p + 1) * cin, q * cin:(q + 1) * cin] = regv[9 * k + 3 * p + q]
    each_edge(lambda copy: copy.start())

    loads[3].wait()
    for tap in range(9):
        midw[:, tap * ch:(tap + 1) * ch] = midv[tap]
    loads[4].wait()
    slab = liftt.shape[0] // 3
    for p in range(3):
        noise = []
        for q in range(3):
            base = p * slab + q * cin
            liftt[base:base + cin, :] = liftv[3 * p + q, :cin, :]
            noise.append(liftv[3 * p + q, cin:, :].astype(F32))
        noise.append(jnp.zeros((slab - 3 * (cin + nout), ch), F32))
        liftt[p * slab + 3 * cin:(p + 1) * slab, :] = jnp.concatenate(noise, axis=0).astype(BF16)
    eye = jnp.where(lax.broadcasted_iota(jnp.int32, (ch, ch), 0) == lax.broadcasted_iota(jnp.int32, (ch, ch), 1), 1.0, 0.0)
    liftw[...] = nt_dot(eye.astype(BF16), liftt[...]).astype(BF16)

    position = lax.broadcasted_iota(jnp.int32, (1, 3 * fl), 1)
    shift = jnp.where(position >= 2 * fl, 2, jnp.where(position >= fl, 1, 0))
    low, weight = lon_split(position - shift * fl + shift - 1)
    low_lane = jnp.where(low < 0, low + cw, low)
    high_lane = jnp.where(low + 1 < 0, low + 1 + cw, low + 1)
    coarse_lane = lax.broadcasted_iota(jnp.int32, (cw, 3 * fl), 0)
    lon[...] = jnp.where(coarse_lane == low_lane, 1.0 - weight,
                         jnp.where(coarse_lane == high_lane, weight, 0.0)).astype(BF16)

    own.wait()

    def arrived(slot, span_rows=whole):
        remote(pieces.at[0, pl.ds(*span_rows)], landing(slot, span_rows), send.at[0], recv.at[slot], me).wait_recv()

    def edge(slot):
        if slot < 8:
            remote(cols, got_cols.at[slot], nsend.at[slot], nrecv.at[slot], me).wait_recv()
        else:
            remote(rows, far_rows.at[slot - 8], nsend.at[slot], nrecv.at[slot], me).wait_recv()

    for k in range(1, TILE_COLS):
        arrived(2 + (c + k) % TILE_COLS)

    @pl.when(north)
    def _():
        arrived(0, lower)
        arrived(1)

    @pl.when(south)
    def _():
        arrived(6)
        arrived(7, upper)

    def real(i):
        row = r * (lines_n - 2 * spare) - spare + i
        return jnp.logical_and(row >= 0, row < (lines_n - 2 * spare) * tile_rows)

    half_gains = [column(gain[k:k + 1, :])[:, :1] * 0.5 for k in range(blocks)]
    biases = [column(regb[k:k + 1, :])[:, :1] for k in range(blocks)]

    def spread(k, i, values):
        values = activate(values, half_gains[k])
        taps = jnp.concatenate(
            [pltpu.roll(values, 1, 1).astype(BF16), values.astype(BF16), pltpu.roll(values, cw - 1, 1).astype(BF16)],
            axis=0)
        part[k % 2, i] = jnp.dot(regw[k], taps, preferred_element_type=F32)

    def enter(i, _):
        own_cols = got[i, :cin, :].astype(F32)
        side = got[i, cin:, :].astype(F32)
        outer = []
        for g in range(cin // 16):
            after = pltpu.roll(side, 128 - halo - g * span - 2 * halo * east, 1)
            before = pltpu.roll(side, 128 - halo - g * span - 2 * halo * c, 1)
            outer.append(jnp.where(lane < halo, after, jnp.where(lane >= 128 - halo, before, 0.0)))
        values = jnp.concatenate([own_cols, jnp.concatenate(outer, axis=0)], axis=1)
        values = jnp.where(real(i), values, 0.0)
        held[i] = values
        spread(0, i, values)
        return 0

    lax.fori_loop(1, lines_n - 1, enter, 0, unroll=2)

    def update(k, i):
        values = held[i] + part[k % 2, i - 1, :cin, :] + part[k % 2, i, cin:2 * cin, :] + part[k % 2, i + 1, 2 * cin:, :]
        values = (values + biases[k]).astype(BF16)
        return jnp.where(real(i), values.astype(F32), 0.0)

    for k in range(1, blocks):
        def follow(i, _, k=k):
            values = update(k - 1, i)
            held[i] = values
            spread(k, i, values)
            return 0

        lax.fori_loop(1 + k, lines_n - 1 - k, follow, 0, unroll=2)

    def leave(i, _):
        field[i - halo] = update(blocks - 1, i).astype(BF16)
        return 0

    lax.fori_loop(halo, lines_n - halo, leave, 0, unroll=2)

    edge(0)
    edge(1)

    @pl.when(north)
    def _():
        for slot in (2, 3, 6, 8):
            edge(slot)

    @pl.when(south)
    def _():
        for slot in (4, 5, 7, 9):
            edge(slot)

    def along(middle, above, below):
        above = jnp.where(top, 0.0, pltpu.roll(above.astype(F32), 128 - (fr - 2), 1))
        below = jnp.where(bottom, 0.0, pltpu.roll(below.astype(F32), fr + 2, 1))
        middle = pltpu.roll(middle.astype(F32), 2, 1)
        return jnp.where(lane < 2, above, jnp.where(lane < fr + 2, middle, below))

    ring[0] = along(got_cols[0], got_cols[2], got_cols[4])
    ring[1] = along(got_cols[1], got_cols[3], got_cols[5])
    ring[2] = along(cols[...], got_cols[6], got_cols[7])
    got_rows[...] = far_rows[...]
    each_band(lambda copy: copy.wait_send())
    each_edge(lambda copy: copy.wait_send())


def lon_split(fine_col):
    lower, part = split(2 * fine_col + 1 - LON_UP + 2 * LON_UP, LON_UP)
    return lower - 1, part


def first_program(coarse, noisy, gain, regb, regs, lifts, mids):
    any_space = pl.BlockSpec(memory_space=pl.ANY)
    vmem = pl.BlockSpec(memory_space=pltpu.VMEM)
    dma = pltpu.SemaphoreType.DMA
    cin, band_rows, clon = coarse.shape
    nout, fr, fl = noisy.shape[1:]
    ch = mids.shape[1]
    blocks = regs.shape[0] // 9
    slab = 3 * cin + -(-3 * nout // 16) * 16
    lines_n = band_rows * (TILE_COLS + 4)
    count = lines_n - 2 * (blocks + 1)
    ct_lon = clon // TILE_COLS
    cw = 2 * ct_lon
    assert ct_lon == 128 and cin % 16 == 0 and band_rows == 2
    assert (cin // 16) * 2 * (blocks + 1) * TILE_COLS <= 128
    shape = jax.ShapeDtypeStruct
    return pl.pallas_call(
        first_kernel,
        out_shape=(
            shape((count, cin, cw), BF16),
            shape((3, 4 * nout, 128), F32),
            shape((2, 4 * nout, fl), BF16),
            shape((ch, 3 * slab), BF16),
            shape((ch, 9 * ch), BF16),
            shape((cw, 3 * fl), BF16),
        ),
        in_specs=[any_space] * 2 + [vmem] * 2 + [any_space] * 3,
        out_specs=(vmem,) * 6,
        scratch_shapes=[
            pltpu.VMEM((cin, band_rows, clon), BF16),
            pltpu.VMEM((TILE_COLS, band_rows, cin + 16, 128), BF16),
            pltpu.VMEM((lines_n, cin + 16, 128), BF16),
            pltpu.VMEM((nout, fr, fl), BF16),
            pltpu.VMEM((4 * nout, 128), BF16),
            pltpu.VMEM((4 * nout, fl), BF16),
            pltpu.VMEM((8, 4 * nout, 128), BF16),
            pltpu.VMEM((2, 4 * nout, fl), BF16),
            pltpu.VMEM(regs.shape, BF16),
            pltpu.VMEM(lifts.shape, BF16),
            pltpu.VMEM(mids.shape, BF16),
            pltpu.VMEM((blocks, 3 * cin, 3 * cin), BF16),
            pltpu.VMEM((3 * slab, ch), BF16),
            pltpu.VMEM((lines_n, cin, cw), F32),
            pltpu.VMEM((2, lines_n, 3 * cin, cw), F32),
            dma((2 * TILE_COLS,)), dma((8,)), dma((10,)), dma((10,)), dma((6,)),
        ],
        compiler_params=pltpu.CompilerParams(
            collective_id=0, has_side_effects=True, vmem_limit_bytes=24_000_000),
    )(coarse, noisy, gain, regb, regs, lifts, mids)


def tile_kernel(
    dims, field, tile, ring, got_rows, liftw, liftb, midg, midw, midb, lon, out,
    grid, lines, upper, sides, bands, keep, raw, prod, edges, cols, rows_out, stage, sems,
):
    cin, ch, fr, fl = dims
    count, cw = field.shape[0], field.shape[2]
    tile_row, tile_rows = lax.axis_index("lat") // TILE_COLS, lax.axis_size("lat") // TILE_COLS
    nout = tile.shape[1]
    top, bottom = tile_row == 0, tile_row == tile_rows - 1
    steps = bands.shape[0]
    wide = fl // 128

    cols[0] = column(liftb[...])
    cols[1] = column(midg[...]) * 0.5
    cols[2] = column(midb[...])

    for q in range(3):
        lines[:, q * cin:(q + 1) * cin, :] = jnp.dot(
            field[...].reshape(count * cin, cw), lon[:, q * fl:(q + 1) * fl],
            preferred_element_type=F32).reshape(count, cin, fl)

    low_line = jnp.where(top, 1, 0)
    high_line = jnp.where(bottom, count - 2, count - 1)
    fine_total = fr * tile_rows

    def inside(t):
        row = tile_row * fr + t - 2
        return jnp.logical_and(row >= 0, row < fine_total)

    def lat_split(t):
        lower, part = split(2 * (t - 2) + 1 - LAT_UP + 2 * LAT_UP, LAT_UP)
        return jnp.clip(lower, low_line, high_line), jnp.clip(lower + 1, low_line, high_line), part

    slab = upper.shape[1]
    lane = lax.broadcasted_iota(jnp.int32, (1, 128), 1)
    lane_first, lane_last = lane == 0, lane == 127

    tall = fr + 4
    for n in range(nout):
        for j in range(wide):
            at = slice(j * 128, (j + 1) * 128)
            base = n * tall
            grid[j, base + 2:base + 2 + fr, :] = tile[0, n, :, at].astype(F32)
            above = got_rows[0, :, at].astype(F32)[4 * n + 2:4 * n + 4]
            below = got_rows[1, :, at].astype(F32)[4 * n:4 * n + 2]
            grid[j, base:base + 2, :] = jnp.where(top, 0.0, above)
            grid[j, base + 2 + fr:base + tall, :] = jnp.where(bottom, 0.0, below)

    west, east, here = ring[0], ring[1], ring[2]
    none = jnp.zeros((slab - 3 * (cin + nout), 128), F32)
    left_cols = jnp.concatenate([west[2 * nout:], here[:nout], none], axis=0)
    right_cols = jnp.concatenate([here[3 * nout:], east[:2 * nout], none], axis=0)
    west_col, east_col = west[3 * nout:], east[:nout]

    def noise_rows(t):
        rows = [grid[j, pl.ds(t, nout, stride=tall), :] for j in range(wide)]
        onward = [pltpu.roll(v, 1, 1) for v in rows]
        back = [pltpu.roll(v, 127, 1) for v in rows]
        edge_l = pltpu.roll(west_col, (128 - t) % 128 if isinstance(t, int) else 128 - t, 1)
        edge_r = pltpu.roll(east_col, 127 - t, 1)
        pieces = []
        for j in range(wide):
            lo = jnp.where(lane_first, onward[j - 1] if j else edge_l, onward[j])
            hi = jnp.where(lane_last, back[j + 1] if j < wide - 1 else edge_r, back[j])
            pieces.append(jnp.concatenate([lo, rows[j], hi, none], axis=0))
        return jnp.concatenate(pieces, axis=1).astype(BF16)

    def raise_row(t, slot):
        a, b, part = lat_split(jnp.int32(t))
        ok = inside(t)
        wa = jnp.where(ok, 1.0 - part, 0.0)
        wb = jnp.where(ok, part, 0.0)
        for o in range(0, 3 * cin, 16):
            upper[slot, o:o + 16, :] = (wa * lines[a, o:o + 16, :] + wb * lines[b, o:o + 16, :]).astype(BF16)
        upper[slot, 3 * cin:slab, :] = noise_rows(t)

    edge_row = jnp.where(lane < HALF, lane, lane - HALF)
    near = fl // LON_UP
    picked_cols = [-1, 0, near - 1, near]
    select_lane = lax.broadcasted_iota(jnp.int32, (cw, 128), 0)
    select_pos = lax.broadcasted_iota(jnp.int32, (cw, 128), 1)
    hits = jnp.zeros((cw, 128), jnp.bool_)
    for s, col in enumerate(picked_cols):
        hits = jnp.logical_or(hits, jnp.logical_and(select_pos == s, select_lane == col % cw))
    chosen = jnp.where(hits, 1.0, 0.0).astype(BF16)
    packed = jnp.zeros((cin, 128), F32)
    for i in range(count):
        narrow = jnp.dot(field[i], chosen, preferred_element_type=F32)
        packed = packed + (pltpu.roll(narrow, 4 * i, 1) if i else narrow)
    packed = packed.astype(BF16)
    key = lax.broadcasted_iota(jnp.int32, (128, 1), 0)
    key_line = key // 4
    key_pick = key - 4 * key_line
    key_col = jnp.where(key_pick == 0, picked_cols[0], jnp.where(
        key_pick == 1, picked_cols[1], jnp.where(key_pick == 2, picked_cols[2], picked_cols[3])))
    for p in range(3):
        t = edge_row + p
        a, b, part = lat_split(t)
        ok = inside(t)
        wa = jnp.where(ok, 1.0 - part, 0.0)
        wb = jnp.where(ok, part, 0.0)
        by_row = jnp.where(key_line == a, wa, 0.0) + jnp.where(key_line == b, wb, 0.0)
        for q in range(3):
            lower, part_m = lon_split(jnp.where(lane < HALF, q - 2, fl - 1 + q))
            by_col = jnp.where(key_col == lower, 1.0 - part_m, jnp.where(key_col == lower + 1, part_m, 0.0))
            base = p * slab + q * cin
            sides[base:base + cin, :] = jnp.dot(
                packed, (by_row * by_col).astype(BF16), preferred_element_type=F32).astype(BF16)
        sides[p * slab + 3 * cin:(p + 1) * slab, :] = jnp.where(
            lane < HALF, pltpu.roll(left_cols, (128 - p) % 128, 1), pltpu.roll(right_cols, HALF - p, 1)).astype(BF16)
    edge_lift = jnp.dot(liftw[...], sides[...], preferred_element_type=F32) + cols[0]
    edge_lift = edge_lift.astype(BF16).astype(F32)
    edges[...] = jnp.where(inside(edge_row + 1), activate(edge_lift, cols[1]), 0.0)

    def lift(slot):
        window = jnp.concatenate([upper[(slot + n) % steps] for n in range(3)], axis=0)
        raw[slot % 2] = jnp.dot(liftw[...], window, preferred_element_type=F32)

    def finish(l, slot):
        squares = jnp.zeros((8, fl), F32)
        for o in range(0, ch, 16):
            bias = jnp.concatenate([cols[0, o:o + 16, :]] * wide, axis=1)
            rounded = (raw[slot % 2, o:o + 16, :] + bias).astype(BF16)
            keep[slot, o:o + 16, :] = rounded
            values = rounded.astype(F32)
            values = values * values
            squares = squares + (values[:8] + values[8:])
        inverse = lax.rsqrt(jnp.sum(squares, axis=0, keepdims=True) * (1.0 / ch) + EPSILON)
        inverse = jnp.where(inside(l + 1), inverse, 0.0)
        for o in range(0, ch, 16):
            half_gain = jnp.concatenate([cols[1, o:o + 16, :]] * wide, axis=1)
            half = keep[slot, o:o + 16, :].astype(F32) * inverse * half_gain
            values = half + half * jnp.tanh(half)
            edge = edges[o:o + 16, :]
            parts = [values[:, j * 128:(j + 1) * 128] for j in range(wide)]
            east = [pltpu.roll(v, 1, 1) for v in parts]
            west = [pltpu.roll(v, 127, 1) for v in parts]
            edge_l = pltpu.roll(edge, 128 - l, 1)
            edge_r = pltpu.roll(edge, 128 + HALF - 1 - l, 1)
            bands[slot, ch + o:ch + o + 16, :] = values.astype(BF16)
            bands[slot, o:o + 16, :] = jnp.concatenate(
                [jnp.where(lane_first, east[j - 1] if j else edge_l, east[j]) for j in range(wide)],
                axis=1).astype(BF16)
            bands[slot, 2 * ch + o:2 * ch + o + 16, :] = jnp.concatenate(
                [jnp.where(lane_last, west[j + 1] if j < wide - 1 else edge_r, west[j]) for j in range(wide)],
                axis=1).astype(BF16)

    def mid(slot):
        window = jnp.concatenate([bands[(slot + n) % steps] for n in range(3)], axis=0)
        prod[slot % 2] = jnp.dot(midw[...], window, preferred_element_type=F32)

    group = stage.shape[2]

    def flush(part):
        slot = part % 2

        def copy(n):
            return pltpu.make_async_copy(
                stage.at[n % 2], out.at[0, :, pl.ds(pl.multiple_of(n * group, group), group), :], sems.at[n % 2])

        @pl.when(part >= 2)
        def _():
            copy(part - 2).wait()

        def shrink(o, _):
            for j in range(wide):
                block = rows_out[j, pl.ds(pl.multiple_of(o * 8 * group, 8 * group), 8 * group), :]
                stage[slot, pl.ds(o * 8, 8), :, j * 128:(j + 1) * 128] = block.reshape(8, group, 128).astype(BF16)
            return 0

        lax.fori_loop(0, ch // 8, shrink, 0)
        copy(part).start()

    def emit(y, slot):
        spot = y % group
        for o in range(0, ch, 16):
            bias = cols[2, o:o + 16, :]
            for j in range(wide):
                at = slice(j * 128, (j + 1) * 128)
                total = keep[(slot + 1) % steps, o:o + 16, at].astype(F32) + prod[slot % 2, o:o + 16, at] + bias
                rows_out[j, pl.ds(spot + o * group, 16, stride=group), :] = total

    for t in range(3):
        raise_row(t, t % steps)
    for l in range(3):
        lift(l % steps)
        raise_row(l + 3, (l + 3) % steps)
        finish(jnp.int32(l), l % steps)

    def trip(i, _):
        for j in range(steps):
            l = i * steps + j + 3
            slot = (j + 3) % steps
            lift(slot)
            mid(j)
            raise_row(jnp.minimum(l + 3, fr + 3), (j + 6) % steps)
            finish(l, slot)
            emit(l - 3, j)

        @pl.when((i + 1) % (group // steps) == 0)
        def _():
            flush(i // (group // steps))
        return 0

    lax.fori_loop(0, fr // steps, trip, 0)
    parts = fr // group
    for n in range(max(parts - 2, 0), parts):
        pltpu.make_async_copy(stage.at[n % 2], out.at[0, :, pl.ds(n * group, group), :], sems.at[n % 2]).wait()


def tile_program(field, noisy, ring, got_rows, liftw, liftb, midg, midw, midb, lon):
    count, cin, cw = field.shape
    ch = liftw.shape[0]
    nout, fr, fl = noisy.shape[1:]
    group = 16
    steps = 4
    vmem = pl.BlockSpec(memory_space=pltpu.VMEM)
    slab = liftw.shape[1] // 3
    return pl.pallas_call(
        functools.partial(tile_kernel, (cin, ch, fr, fl)),
        out_shape=jax.ShapeDtypeStruct((1, ch, fr, fl), BF16),
        in_specs=[vmem] * 10,
        out_specs=pl.BlockSpec(memory_space=pl.ANY),
        scratch_shapes=[
            pltpu.VMEM((fl // 128, nout * (fr + 4), 128), F32),
            pltpu.VMEM((count, 3 * cin, fl), F32),
            pltpu.VMEM((steps, slab, fl), BF16),
            pltpu.VMEM((3 * slab, 128), BF16),
            pltpu.VMEM((steps, 3 * ch, fl), BF16),
            pltpu.VMEM((steps, ch, fl), BF16),
            pltpu.VMEM((2, ch, fl), F32),
            pltpu.VMEM((2, ch, fl), F32),
            pltpu.VMEM((ch, 128), F32),
            pltpu.VMEM((3, ch, 128), F32),
            pltpu.VMEM((fl // 128, ch * group, 128), F32),
            pltpu.VMEM((2, ch, group, fl), BF16),
            pltpu.SemaphoreType.DMA((2,)),
        ],
        compiler_params=pltpu.CompilerParams(vmem_limit_bytes=40_000_000),
    )(field, noisy, ring, got_rows, liftw, liftb, midg, midw, midb, lon)


def per_device(
    coarse, reg_gain, reg_weight, reg_bias, noisy, lift_weight, lift_bias, mid_gain, mid_weight, mid_bias,
):
    lifts = lift_weight.transpose(0, 1, 3, 2)
    field, ring, got_rows, liftw, midw, lon = first_program(
        coarse, noisy, reg_gain, reg_bias, reg_weight.reshape((-1,) + reg_weight.shape[3:]),
        lifts.reshape((9,) + lifts.shape[2:]), mid_weight.reshape((9,) + mid_weight.shape[2:]))
    return tile_program(
        field, noisy, ring, got_rows, liftw, lift_bias[None], mid_gain[None], midw, mid_bias[None], lon)


def solution(mesh):
    placed = (
        P(None, ("grp", "lat"), None),
        P(),
        P(),
        P(),
        P(("grp", "lat"), None, None, None),
        P(),
        P(),
        P(),
        P(),
        P(),
    )
    return jax.shard_map(
        per_device,
        mesh=mesh,
        in_specs=placed,
        out_specs=P(("grp", "lat"), None, None, None),
        check_vma=False,
    )
```

```python
import functools

import jax
import jax.numpy as jnp
from jax import lax
from jax.experimental import pallas as pl
from jax.experimental.pallas import tpu as pltpu
from jax.sharding import PartitionSpec as P

TILE_COLS = 4
LAT_UP = 4
LON_UP = 4
EPSILON = 1e-06
F32 = jnp.float32
BF16 = jnp.bfloat16
MESH = pl.DeviceIdType.MESH
HALF = 64


def activate(values, half_gain):
    inverse = lax.rsqrt(jnp.mean(values * values, axis=0, keepdims=True) + EPSILON)
    half = values * inverse * half_gain
    return half + half * jnp.tanh(half)


def split(numerator, factor):
    lower = numerator // (2 * factor)
    return lower, (numerator - 2 * factor * lower).astype(F32) / (2.0 * factor)


def column(row):
    n = row.shape[1]
    here = lax.broadcasted_iota(jnp.int32, (n, n), 0) == lax.broadcasted_iota(jnp.int32, (n, n), 1)
    return jnp.broadcast_to(jnp.sum(jnp.where(here, row, 0.0), axis=1, keepdims=True), (n, 128))


def nt_dot(a, b):
    return lax.dot_general(a, b, (((1,), (1,)), ((), ())), preferred_element_type=F32)


def lon_split(fine_col):
    lower, part = split(2 * fine_col + 1 - LON_UP + 2 * LON_UP, LON_UP)
    return lower - 1, part


def lat_split(t, top, bottom, count, start, total):
    lower, part = split(2 * (t - 2) + 1 - LAT_UP + 2 * LAT_UP, LAT_UP)
    low_line = jnp.where(top, 1, 0)
    high_line = jnp.where(bottom, count - 2, count - 1)
    row = start + t - 2
    ok = jnp.logical_and(row >= 0, row < total)
    return jnp.clip(lower, low_line, high_line), jnp.clip(lower + 1, low_line, high_line), part, ok


def first_kernel(
    coarse, noisy, gain, regb, regs, liftb, midg, midb, lifts, mids,
    got, got_cols, cols, grid, regw, regc, liftw, liftc, midw, lon, sidew, chosen,
    band, pieces, tile, rows, far_rows, gainv, regbv, vecs, regv, liftv, midv, liftt,
    send, recv, nsend, nrecv, local,
):
    me = lax.axis_index("lat")
    tile_rows = lax.axis_size("lat") // TILE_COLS
    r = me // TILE_COLS
    c = me % TILE_COLS
    north, south = r > 0, r < tile_rows - 1
    top, bottom = r == 0, r == tile_rows - 1
    cin, band_rows, clon = band.shape
    ch = midv.shape[1]
    nout, fr, fl = tile.shape
    blocks = regw.shape[0]
    halo = blocks + 1
    span = 2 * halo * TILE_COLS
    cw = chosen.shape[0]
    count = got.shape[0] - 2 * halo

    barrier = pltpu.get_barrier_semaphore()

    def greet(target):
        pl.semaphore_signal(barrier, inc=1, device_id={"lat": target}, device_id_type=MESH)

    for k in range(1, TILE_COLS):
        greet(r * TILE_COLS + (c + k) % TILE_COLS)

    @pl.when(north)
    def _():
        for k in range(TILE_COLS):
            greet((r - 1) * TILE_COLS + k)

    @pl.when(south)
    def _():
        for k in range(TILE_COLS):
            greet((r + 1) * TILE_COLS + k)

    loads = [
        pltpu.make_async_copy(coarse, band, local.at[0]),
        pltpu.make_async_copy(noisy.at[0], tile, local.at[1]),
        pltpu.make_async_copy(regs, regv, local.at[2]),
        pltpu.make_async_copy(mids, midv, local.at[3]),
        pltpu.make_async_copy(lifts, liftv, local.at[4]),
        pltpu.make_async_copy(gain, gainv, local.at[6]),
        pltpu.make_async_copy(regb, regbv, local.at[7]),
        pltpu.make_async_copy(liftb, vecs.at[0], local.at[8]),
        pltpu.make_async_copy(midg, vecs.at[1], local.at[9]),
        pltpu.make_async_copy(midb, vecs.at[2], local.at[10]),
    ]
    for load in loads:
        load.start()

    lane = lax.broadcasted_iota(jnp.int32, (1, 128), 1)
    both = band_rows * cin
    row_id = lax.broadcasted_iota(jnp.int32, (both, both), 0)
    sub_id = jnp.where(row_id >= cin, 1, 0)
    order = lax.broadcasted_iota(jnp.int32, (both, both), 1) == band_rows * (row_id - sub_id * cin) + sub_id
    order = jnp.where(order, 1.0, 0.0).astype(BF16)
    loads[0].wait()
    sorted_rows = jnp.dot(order, band[...].reshape(both, clon), preferred_element_type=F32)
    for sub in range(band_rows):
        row = sorted_rows[sub * cin:(sub + 1) * cin]
        parts = [row[:, b * 128:(b + 1) * 128] for b in range(TILE_COLS)]
        for b in range(TILE_COLS):
            pieces[b, sub, :cin, :] = parts[b].astype(BF16)
        side = jnp.zeros((16, 128), F32)
        for b in range(TILE_COLS):
            seam = jnp.where(lane < 64, parts[b], parts[(b + TILE_COLS - 1) % TILE_COLS])
            for g in range(cin // 16):
                at = g * span + 2 * halo * b
                moved = pltpu.roll(seam[g * 16:(g + 1) * 16], at + halo, 1)
                side = jnp.where(jnp.logical_and(lane >= at, lane < at + 2 * halo), moved, side)
        for b in range(TILE_COLS):
            pieces[b, sub, cin:, :] = side.astype(BF16)

    loads[1].wait()
    ends = []
    for n in range(nout):
        ends += [tile[n, :2, :].astype(F32), tile[n, fr - 2:, :].astype(F32)]
    rows[...] = jnp.concatenate(ends, axis=0).astype(BF16)
    pick_row = lax.broadcasted_iota(jnp.int32, (4 * nout, 128), 0)
    pick_lane = lax.broadcasted_iota(jnp.int32, (4 * nout, 128), 1)
    packed = jnp.zeros((4 * nout, fr), F32)
    for n in range(nout):
        for s, (lo, at) in enumerate(((0, 0), (0, 1), (fl - 128, 126), (fl - 128, 127))):
            if s % 2 == 0:
                hit = jnp.zeros(pick_row.shape, jnp.bool_)
            hit = jnp.logical_or(hit, jnp.logical_and(pick_row == s * nout + n, pick_lane == at))
            if s % 2:
                packed = packed + nt_dot(jnp.where(hit, 1.0, 0.0).astype(BF16), tile[n, :, lo:lo + 128])
    cols[...] = jnp.concatenate([packed, jnp.zeros((4 * nout, 128 - fr), F32)], axis=1).astype(BF16)

    peers = TILE_COLS - 1 + jnp.where(north, TILE_COLS, 0) + jnp.where(south, TILE_COLS, 0)
    pl.semaphore_wait(barrier, peers)

    def remote(src, dst, ssem, rsem, target):
        return pltpu.make_async_remote_copy(
            src_ref=src, dst_ref=dst, send_sem=ssem, recv_sem=rsem,
            device_id={"lat": target}, device_id_type=MESH)

    whole, upper, lower = (0, 2), (0, 1), (1, 1)

    def landing(slot, span_rows):
        return got.at[pl.ds(2 * slot + span_rows[0], span_rows[1])]

    def band_copy(k, row, slot, ssem, span_rows=whole):
        col = (c + k) % TILE_COLS
        return remote(pieces.at[col, pl.ds(*span_rows)], landing(slot, span_rows), send.at[ssem], recv.at[slot],
                      row * TILE_COLS + col)

    west, east = (c + TILE_COLS - 1) % TILE_COLS, (c + 1) % TILE_COLS

    def col_copy(slot, row, col):
        return remote(cols, got_cols.at[slot], nsend.at[slot], nrecv.at[slot], row * TILE_COLS + col)

    def row_copy(slot, row):
        return remote(rows, far_rows.at[slot], nsend.at[8 + slot], nrecv.at[8 + slot], row * TILE_COLS + c)

    def each_band(action):
        for col, side, row, slot, span_rows in (
            (2, south, r + 1, 0, lower), (3, south, r + 1, 1, whole),
            (0, north, r - 1, 6, whole), (1, north, r - 1, 7, upper),
        ):
            @pl.when(jnp.logical_and(side, c == col))
            def _():
                for k in range(TILE_COLS):
                    action(band_copy(k, row, slot, TILE_COLS + k, span_rows))

        for k in range(1, TILE_COLS):
            action(band_copy(k, r, 2 + c, k))

    def each_edge(action):
        action(col_copy(0, r, east))
        action(col_copy(1, r, west))

        @pl.when(south)
        def _():
            action(row_copy(0, r + 1))
            action(col_copy(6, r + 1, c))
            action(col_copy(2, r + 1, east))
            action(col_copy(3, r + 1, west))

        @pl.when(north)
        def _():
            action(row_copy(1, r - 1))
            action(col_copy(7, r - 1, c))
            action(col_copy(4, r - 1, east))
            action(col_copy(5, r - 1, west))

    each_band(lambda copy: copy.start())
    own = pltpu.make_async_copy(pieces.at[c], landing(2 + c, whole), local.at[5])
    own.start()

    loads[2].wait()
    for k in range(blocks):
        for p in range(3):
            for q in range(3):
                regw[k, p * cin:(p + 1) * cin, q * cin:(q + 1) * cin] = regv[9 * k + 3 * p + q]
    each_edge(lambda copy: copy.start())

    loads[3].wait()
    for tap in range(9):
        midw[:, tap * ch:(tap + 1) * ch] = midv[tap]
    loads[4].wait()
    slab = liftt.shape[0] // 3
    for p in range(3):
        noise = []
        for q in range(3):
            base = p * slab + q * cin
            liftt[base:base + cin, :] = liftv[3 * p + q, :cin, :]
            noise.append(liftv[3 * p + q, cin:, :].astype(F32))
        noise.append(jnp.zeros((slab - 3 * (cin + nout), ch), F32))
        liftt[p * slab + 3 * cin:(p + 1) * slab, :] = jnp.concatenate(noise, axis=0).astype(BF16)
    eye = jnp.where(lax.broadcasted_iota(jnp.int32, (ch, ch), 0) == lax.broadcasted_iota(jnp.int32, (ch, ch), 1), 1.0, 0.0)
    liftw[...] = nt_dot(eye.astype(BF16), liftt[...]).astype(BF16)

    position = lax.broadcasted_iota(jnp.int32, (1, 3 * fl), 1)
    shift = jnp.where(position >= 2 * fl, 2, jnp.where(position >= fl, 1, 0))
    low, weight = lon_split(position - shift * fl + shift - 1)
    low_lane = jnp.where(low < 0, low + cw, low)
    high_lane = jnp.where(low + 1 < 0, low + 1 + cw, low + 1)
    coarse_lane = lax.broadcasted_iota(jnp.int32, (cw, 3 * fl), 0)
    lon[...] = jnp.where(coarse_lane == low_lane, 1.0 - weight,
                         jnp.where(coarse_lane == high_lane, weight, 0.0)).astype(BF16)

    for load in loads[5:]:
        load.wait()
    for k in range(blocks):
        regc[2 * k] = column(gainv[k:k + 1, :]) * 0.5
        regc[2 * k + 1] = column(regbv[k:k + 1, :])
    liftc[0] = column(vecs[0])
    liftc[1] = column(vecs[1]) * 0.5
    liftc[2] = column(vecs[2])

    tall = fr + 4
    wide = fl // 128
    for n in range(nout):
        for j in range(wide):
            grid[j, n * tall + 2:n * tall + 2 + fr, :] = tile[n, :, j * 128:(j + 1) * 128].astype(F32)

    near = fl // LON_UP
    picked_cols = [-1, 0, near - 1, near]
    select_lane = lax.broadcasted_iota(jnp.int32, (cw, 128), 0)
    select_pos = lax.broadcasted_iota(jnp.int32, (cw, 128), 1)
    hits = jnp.zeros((cw, 128), jnp.bool_)
    for s, col in enumerate(picked_cols):
        hits = jnp.logical_or(hits, jnp.logical_and(select_pos == s, select_lane == col % cw))
    chosen[...] = jnp.where(hits, 1.0, 0.0).astype(BF16)
    key = lax.broadcasted_iota(jnp.int32, (128, 1), 0)
    key_line = key // 4
    key_pick = key - 4 * key_line
    key_col = jnp.where(key_pick == 0, picked_cols[0], jnp.where(
        key_pick == 1, picked_cols[1], jnp.where(key_pick == 2, picked_cols[2], picked_cols[3])))
    edge_row = jnp.where(lane < HALF, lane, lane - HALF)
    for p in range(3):
        a, b, share, ok = lat_split(edge_row + p, top, bottom, count, r * fr, fr * tile_rows)
        wa = jnp.where(ok, 1.0 - share, 0.0)
        wb = jnp.where(ok, share, 0.0)
        by_row = jnp.where(key_line == a, wa, 0.0) + jnp.where(key_line == b, wb, 0.0)
        for q in range(3):
            lower_col, share_m = lon_split(jnp.where(lane < HALF, q - 2, fl - 1 + q))
            by_col = jnp.where(key_col == lower_col, 1.0 - share_m, jnp.where(key_col == lower_col + 1, share_m, 0.0))
            sidew[3 * p + q] = (by_row * by_col).astype(BF16)

    own.wait()

    def arrived(slot, span_rows=whole):
        remote(pieces.at[0, pl.ds(*span_rows)], landing(slot, span_rows), send.at[0], recv.at[slot], me).wait_recv()

    def edge(slot):
        if slot < 8:
            remote(cols, got_cols.at[slot], nsend.at[slot], nrecv.at[slot], me).wait_recv()
        else:
            remote(rows, far_rows.at[slot - 8], nsend.at[slot], nrecv.at[slot], me).wait_recv()

    for k in range(1, TILE_COLS):
        arrived(2 + (c + k) % TILE_COLS)

    @pl.when(north)
    def _():
        arrived(0, lower)
        arrived(1)

    @pl.when(south)
    def _():
        arrived(6)
        arrived(7, upper)

    edge(0)
    edge(1)

    @pl.when(north)
    def _():
        for slot in (2, 3, 6, 8):
            edge(slot)

    @pl.when(south)
    def _():
        for slot in (4, 5, 7, 9):
            edge(slot)

    for n in range(nout):
        for j in range(wide):
            at = slice(j * 128, (j + 1) * 128)
            above = far_rows[0, :, at].astype(F32)[4 * n + 2:4 * n + 4]
            below = far_rows[1, :, at].astype(F32)[4 * n:4 * n + 2]
            grid[j, n * tall:n * tall + 2, :] = jnp.where(top, 0.0, above)
            grid[j, n * tall + 2 + fr:(n + 1) * tall, :] = jnp.where(bottom, 0.0, below)

    each_band(lambda copy: copy.wait_send())
    each_edge(lambda copy: copy.wait_send())


def first_program(coarse, noisy, gain, regb, regs, liftb, midg, midb, lifts, mids):
    hbm = pl.BlockSpec(memory_space=pltpu.HBM)
    vmem = pl.BlockSpec(memory_space=pltpu.VMEM)
    dma = pltpu.SemaphoreType.DMA
    cin, band_rows, clon = coarse.shape
    nout, fr, fl = noisy.shape[1:]
    ch = mids.shape[1]
    blocks = regs.shape[0] // 9
    slab = 3 * cin + -(-3 * nout // 16) * 16
    lines_n = band_rows * (TILE_COLS + 4)
    ct_lon = clon // TILE_COLS
    cw = 2 * ct_lon
    assert ct_lon == 128 and cin % 16 == 0 and band_rows == 2
    assert (cin // 16) * 2 * (blocks + 1) * TILE_COLS <= 128
    shape = jax.ShapeDtypeStruct
    return pl.pallas_call(
        first_kernel,
        out_shape=(
            shape((lines_n, cin + 16, 128), BF16),
            shape((8, 4 * nout, 128), BF16),
            shape((4 * nout, 128), BF16),
            shape((fl // 128, nout * (fr + 4), 128), F32),
            shape((blocks, 3 * cin, 3 * cin), BF16),
            shape((2 * blocks, cin, 128), F32),
            shape((ch, 3 * slab), BF16),
            shape((3, ch, 128), F32),
            shape((ch, 9 * ch), BF16),
            shape((cw, 3 * fl), BF16),
            shape((9, 128, 128), BF16),
            shape((cw, 128), BF16),
        ),
        in_specs=[hbm] * 10,
        out_specs=(vmem,) * 12,
        scratch_shapes=[
            pltpu.VMEM((cin, band_rows, clon), BF16),
            pltpu.VMEM((TILE_COLS, band_rows, cin + 16, 128), BF16),
            pltpu.VMEM((nout, fr, fl), BF16),
            pltpu.VMEM((4 * nout, fl), BF16),
            pltpu.VMEM((2, 4 * nout, fl), BF16),
            pltpu.VMEM(gain.shape, F32),
            pltpu.VMEM(regb.shape, F32),
            pltpu.VMEM((3, 1, ch), F32),
            pltpu.VMEM(regs.shape, BF16),
            pltpu.VMEM(lifts.shape, BF16),
            pltpu.VMEM(mids.shape, BF16),
            pltpu.VMEM((3 * slab, ch), BF16),
            dma((2 * TILE_COLS,)), dma((8,)), dma((10,)), dma((10,)), dma((11,)),
        ],
        compiler_params=pltpu.CompilerParams(
            collective_id=0, has_side_effects=True, vmem_limit_bytes=20_000_000),
    )(*[pltpu.with_memory_space_constraint(x, pltpu.HBM) for x in (
        coarse, noisy, gain, regb, regs, liftb, midg, midb, lifts, mids)])


def tile_kernel(
    dims, got, got_cols, own_cols, grid, regw, regc, liftw, cols, midw, lon, sidew, chosen, out,
    held, part, field, lines, upper, sides, bands, keep, raw, prod, edges, rows_out, stage, sems,
):
    cin, ch, nout, fr, fl = dims
    lines_n, count, cw = got.shape[0], field.shape[0], field.shape[2]
    blocks = regw.shape[0]
    halo = blocks + 1
    span = 2 * halo * TILE_COLS
    me = lax.axis_index("lat")
    tile_row, tile_rows = me // TILE_COLS, lax.axis_size("lat") // TILE_COLS
    c = me % TILE_COLS
    after_seam = (c + 1) % TILE_COLS
    top, bottom = tile_row == 0, tile_row == tile_rows - 1
    steps = bands.shape[0]
    wide = fl // 128
    lane = lax.broadcasted_iota(jnp.int32, (1, 128), 1)
    lane_first, lane_last = lane == 0, lane == 127
    spare = lines_n // 4

    def known(i, values):
        if i < spare:
            return jnp.where(top, 0.0, values)
        if i >= lines_n - spare:
            return jnp.where(bottom, 0.0, values)
        return values

    def spread(k, i, values):
        values = activate(values, regc[2 * k][:, :1])
        taps = jnp.concatenate(
            [pltpu.roll(values, 1, 1).astype(BF16), values.astype(BF16), pltpu.roll(values, cw - 1, 1).astype(BF16)],
            axis=0)
        part[k % 2, i] = jnp.dot(regw[k], taps, preferred_element_type=F32)

    for i in range(1, lines_n - 1):
        side = got[i, cin:, :].astype(F32)
        outer = []
        for g in range(cin // 16):
            after = pltpu.roll(side, 128 - halo - g * span - 2 * halo * after_seam, 1)
            before = pltpu.roll(side, 128 - halo - g * span - 2 * halo * c, 1)
            outer.append(jnp.where(lane < halo, after, jnp.where(lane >= 128 - halo, before, 0.0)))
        values = jnp.concatenate([got[i, :cin, :].astype(F32), jnp.concatenate(outer, axis=0)], axis=1)
        values = known(i, values)
        held[i] = values
        spread(0, i, values)

    def update(k, i):
        values = held[i] + part[k % 2, i - 1, :cin, :] + part[k % 2, i, cin:2 * cin, :] + part[k % 2, i + 1, 2 * cin:, :]
        values = (values + regc[2 * k + 1][:, :1]).astype(BF16)
        return known(i, values.astype(F32))

    for k in range(1, blocks):
        for i in range(1 + k, lines_n - 1 - k):
            values = update(k - 1, i)
            held[i] = values
            spread(k, i, values)

    for i in range(halo, lines_n - halo):
        field[i - halo] = update(blocks - 1, i).astype(BF16)

    for q in range(3):
        lines[:, q * cin:(q + 1) * cin, :] = jnp.dot(
            field[...].reshape(count * cin, cw), lon[:, q * fl:(q + 1) * fl],
            preferred_element_type=F32).reshape(count, cin, fl)

    def blend(t):
        return lat_split(t, top, bottom, count, tile_row * fr, fr * tile_rows)

    def inside(t):
        row = tile_row * fr + t - 2
        return jnp.logical_and(row >= 0, row < fr * tile_rows)

    tall = fr + 4
    slab = upper.shape[1]

    def along(middle, above, below):
        above = jnp.where(top, 0.0, pltpu.roll(above.astype(F32), 128 - (fr - 2), 1))
        below = jnp.where(bottom, 0.0, pltpu.roll(below.astype(F32), fr + 2, 1))
        middle = pltpu.roll(middle.astype(F32), 2, 1)
        return jnp.where(lane < 2, above, jnp.where(lane < fr + 2, middle, below))

    west = along(got_cols[0], got_cols[2], got_cols[4])
    east = along(got_cols[1], got_cols[3], got_cols[5])
    here = along(own_cols[...], got_cols[6], got_cols[7])
    none = jnp.zeros((slab - 3 * (cin + nout), 128), F32)
    left_cols = jnp.concatenate([west[2 * nout:], here[:nout], none], axis=0)
    right_cols = jnp.concatenate([here[3 * nout:], east[:2 * nout], none], axis=0)
    west_col, east_col = west[3 * nout:], east[:nout]

    def noise_rows(t):
        rows = [grid[j, pl.ds(t, nout, stride=tall), :] for j in range(wide)]
        onward = [pltpu.roll(v, 1, 1) for v in rows]
        back = [pltpu.roll(v, 127, 1) for v in rows]
        edge_l = pltpu.roll(west_col, (128 - t) % 128 if isinstance(t, int) else 128 - t, 1)
        edge_r = pltpu.roll(east_col, 127 - t, 1)
        pieces = []
        for j in range(wide):
            lo = jnp.where(lane_first, onward[j - 1] if j else edge_l, onward[j])
            hi = jnp.where(lane_last, back[j + 1] if j < wide - 1 else edge_r, back[j])
            pieces.append(jnp.concatenate([lo, rows[j], hi, none], axis=0))
        return jnp.concatenate(pieces, axis=1).astype(BF16)

    def raise_row(t, slot):
        a, b, share, ok = blend(jnp.int32(t))
        wa = jnp.where(ok, 1.0 - share, 0.0)
        wb = jnp.where(ok, share, 0.0)
        for o in range(0, 3 * cin, 16):
            upper[slot, o:o + 16, :] = (wa * lines[a, o:o + 16, :] + wb * lines[b, o:o + 16, :]).astype(BF16)
        upper[slot, 3 * cin:slab, :] = noise_rows(t)

    edge_row = jnp.where(lane < HALF, lane, lane - HALF)
    narrow = jnp.dot(field[...].reshape(count * cin, cw), chosen[...], preferred_element_type=F32)
    packed = narrow[:cin]
    for i in range(1, count):
        packed = packed + pltpu.roll(narrow[i * cin:(i + 1) * cin], 4 * i, 1)
    packed = packed.astype(BF16)
    for p in range(3):
        for q in range(3):
            base = p * slab + q * cin
            sides[base:base + cin, :] = jnp.dot(packed, sidew[3 * p + q], preferred_element_type=F32).astype(BF16)
        sides[p * slab + 3 * cin:(p + 1) * slab, :] = jnp.where(
            lane < HALF, pltpu.roll(left_cols, (128 - p) % 128, 1), pltpu.roll(right_cols, HALF - p, 1)).astype(BF16)
    edge_lift = jnp.dot(liftw[...], sides[...], preferred_element_type=F32) + cols[0]
    edge_lift = edge_lift.astype(BF16).astype(F32)
    edges[...] = jnp.where(inside(edge_row + 1), activate(edge_lift, cols[1]), 0.0)

    def lift(slot):
        window = jnp.concatenate([upper[(slot + n) % steps] for n in range(3)], axis=0)
        raw[slot % 2] = jnp.dot(liftw[...], window, preferred_element_type=F32)

    def finish(l, slot):
        squares = jnp.zeros((8, fl), F32)
        for o in range(0, ch, 16):
            bias = jnp.concatenate([cols[0, o:o + 16, :]] * wide, axis=1)
            rounded = (raw[slot % 2, o:o + 16, :] + bias).astype(BF16)
            keep[slot, o:o + 16, :] = rounded
            values = rounded.astype(F32)
            values = values * values
            squares = squares + (values[:8] + values[8:])
        inverse = lax.rsqrt(jnp.sum(squares, axis=0, keepdims=True) * (1.0 / ch) + EPSILON)
        inverse = jnp.where(inside(l + 1), inverse, 0.0)
        for o in range(0, ch, 16):
            half_gain = jnp.concatenate([cols[1, o:o + 16, :]] * wide, axis=1)
            half = keep[slot, o:o + 16, :].astype(F32) * inverse * half_gain
            values = half + half * jnp.tanh(half)
            edge = edges[o:o + 16, :]
            parts = [values[:, j * 128:(j + 1) * 128] for j in range(wide)]
            east = [pltpu.roll(v, 1, 1) for v in parts]
            west = [pltpu.roll(v, 127, 1) for v in parts]
            edge_l = pltpu.roll(edge, 128 - l, 1)
            edge_r = pltpu.roll(edge, 128 + HALF - 1 - l, 1)
            bands[slot, ch + o:ch + o + 16, :] = values.astype(BF16)
            bands[slot, o:o + 16, :] = jnp.concatenate(
                [jnp.where(lane_first, east[j - 1] if j else edge_l, east[j]) for j in range(wide)],
                axis=1).astype(BF16)
            bands[slot, 2 * ch + o:2 * ch + o + 16, :] = jnp.concatenate(
                [jnp.where(lane_last, west[j + 1] if j < wide - 1 else edge_r, west[j]) for j in range(wide)],
                axis=1).astype(BF16)

    def mid(slot):
        window = jnp.concatenate([bands[(slot + n) % steps] for n in range(3)], axis=0)
        prod[slot % 2] = jnp.dot(midw[...], window, preferred_element_type=F32)

    group = stage.shape[2]
    blocks_out = ch // 8

    def flushed(n):
        return pltpu.make_async_copy(
            stage.at[n % 2], out.at[0, :, pl.ds(pl.multiple_of(n * group, group), group), :], sems.at[n % 2])

    def shrink(n, o):
        for j in range(wide):
            block = rows_out[n % 2, j, pl.ds(pl.multiple_of(o * 8 * group, 8 * group), 8 * group), :]
            stage[n % 2, pl.ds(o * 8, 8), :, j * 128:(j + 1) * 128] = block.reshape(8, group, 128).astype(BF16)

    def emit(n, spot, slot):
        for o in range(0, ch, 16):
            bias = cols[2, o:o + 16, :]
            for j in range(wide):
                at = slice(j * 128, (j + 1) * 128)
                total = keep[(slot + 1) % steps, o:o + 16, at].astype(F32) + prod[slot % 2, o:o + 16, at] + bias
                rows_out[n % 2, j, pl.ds(spot + o * group, 16, stride=group), :] = total

    for t in range(3):
        raise_row(t, t % steps)
    for l in range(5):
        lift(l % steps)
        raise_row(l + 3, (l + 3) % steps)
        if l:
            finish(jnp.int32(l - 1), (l - 1) % steps)
    mid(0)

    halves = group // steps
    share_out = blocks_out // group

    def step(i, u, e, last):
        n = i // halves
        shrink_at = (i % halves) * (blocks_out // halves) + u * share_out
        for o in range(share_out):
            shrink(n + 1, shrink_at + o)
        emit(n, (i % halves) * steps + u, u)
        if last is None or last + 1 < fr:
            mid((u + 1) % steps)
        if last is None or last + 4 < fr + 2:
            finish(e + 4, (u + 4) % steps)
        if last is None or last + 5 < fr + 2:
            lift((u + 5) % steps)
        if last is None:
            raise_row(e + 8, u)

    trips = fr // steps

    def begin(i):
        @pl.when(jnp.logical_and(i % halves == 0, i >= 3 * halves))
        def _():
            flushed(i // halves - 3).wait()

    def finish_trip(i):
        @pl.when(jnp.logical_and(i % halves == halves - 1, i >= halves))
        def _():
            flushed(i // halves - 1).start()

    def trip(i, _):
        begin(i)
        for u in range(steps):
            step(i, u, i * steps + u, None)
        finish_trip(i)
        return 0

    lax.fori_loop(0, trips - 1, trip, 0)
    i = jnp.int32(trips - 1)
    begin(i)
    for u in range(steps):
        step(i, u, i * steps + u, fr - steps + u)
    finish_trip(i)
    groups = fr // group
    if groups >= 3:
        flushed(groups - 3).wait()
    for o in range(blocks_out):
        shrink(groups - 1, o)
    flushed(groups - 1).start()
    for n in range(max(groups - 2, 0), groups):
        flushed(n).wait()


def tile_program(dims, prepared):
    cin, ch, nout, fr, fl = dims
    got, lon, liftw = prepared[0], prepared[9], prepared[6]
    lines_n = got.shape[0]
    cw = lon.shape[0]
    blocks = prepared[4].shape[0]
    count = lines_n - 2 * (blocks + 1)
    group = 8
    steps = 4
    vmem = pl.BlockSpec(memory_space=pltpu.VMEM)
    slab = liftw.shape[1] // 3
    return pl.pallas_call(
        functools.partial(tile_kernel, dims),
        out_shape=jax.ShapeDtypeStruct((1, ch, fr, fl), BF16),
        in_specs=[vmem] * len(prepared),
        out_specs=pl.BlockSpec(memory_space=pl.ANY),
        scratch_shapes=[
            pltpu.VMEM((lines_n, cin, cw), F32),
            pltpu.VMEM((2, lines_n, 3 * cin, cw), F32),
            pltpu.VMEM((count, cin, cw), BF16),
            pltpu.VMEM((count, 3 * cin, fl), F32),
            pltpu.VMEM((steps, slab, fl), BF16),
            pltpu.VMEM((3 * slab, 128), BF16),
            pltpu.VMEM((steps, 3 * ch, fl), BF16),
            pltpu.VMEM((steps, ch, fl), BF16),
            pltpu.VMEM((2, ch, fl), F32),
            pltpu.VMEM((2, ch, fl), F32),
            pltpu.VMEM((ch, 128), F32),
            pltpu.VMEM((2, fl // 128, ch * group, 128), F32),
            pltpu.VMEM((2, ch, group, fl), BF16),
            pltpu.SemaphoreType.DMA((2,)),
        ],
        compiler_params=pltpu.CompilerParams(vmem_limit_bytes=44_000_000),
    )(*prepared)


def per_device(
    coarse, reg_gain, reg_weight, reg_bias, noisy, lift_weight, lift_bias, mid_gain, mid_weight, mid_bias,
):
    lifts = lift_weight.transpose(0, 1, 3, 2)
    prepared = first_program(
        coarse, noisy, reg_gain, reg_bias, reg_weight.reshape((-1,) + reg_weight.shape[3:]),
        lift_bias[None], mid_gain[None], mid_bias[None],
        lifts.reshape((9,) + lifts.shape[2:]), mid_weight.reshape((9,) + mid_weight.shape[2:]))
    return tile_program((coarse.shape[0], mid_weight.shape[2]) + noisy.shape[1:], prepared)


def solution(mesh):
    placed = (
        P(None, ("grp", "lat"), None),
        P(),
        P(),
        P(),
        P(("grp", "lat"), None, None, None),
        P(),
        P(),
        P(),
        P(),
        P(),
    )
    return jax.shard_map(
        per_device,
        mesh=mesh,
        in_specs=placed,
        out_specs=P(("grp", "lat"), None, None, None),
        check_vma=False,
    )
```

```python
import functools

import jax
import jax.numpy as jnp
from jax import lax
from jax.experimental import pallas as pl
from jax.experimental.pallas import tpu as pltpu
from jax.sharding import PartitionSpec as P

TILE_COLS = 4
LAT_UP = 4
LON_UP = 4
EPSILON = 1e-06
F32 = jnp.float32
BF16 = jnp.bfloat16
MESH = pl.DeviceIdType.MESH
HALF = 64


def activate(values, half_gain):
    inverse = lax.rsqrt(jnp.mean(values * values, axis=0, keepdims=True) + EPSILON)
    half = values * inverse * half_gain
    return half + half * jnp.tanh(half)


def split(numerator, factor):
    lower = numerator // (2 * factor)
    return lower, (numerator - 2 * factor * lower).astype(F32) / (2.0 * factor)


def column(row):
    n = row.shape[1]
    here = lax.broadcasted_iota(jnp.int32, (n, n), 0) == lax.broadcasted_iota(jnp.int32, (n, n), 1)
    return jnp.broadcast_to(jnp.sum(jnp.where(here, row, 0.0), axis=1, keepdims=True), (n, 128))


def thirds(values):
    high = values.astype(BF16).astype(F32)
    middle = (values - high).astype(BF16).astype(F32)
    return [high, middle, values - high - middle]


def nt_dot(a, b):
    return lax.dot_general(a, b, (((1,), (1,)), ((), ())), preferred_element_type=F32)


def lon_split(fine_col):
    lower, part = split(2 * fine_col + 1 - LON_UP + 2 * LON_UP, LON_UP)
    return lower - 1, part


def lat_split(t, top, bottom, count, start, total):
    lower, part = split(2 * (t - 2) + 1 - LAT_UP + 2 * LAT_UP, LAT_UP)
    low_line = jnp.where(top, 1, 0)
    high_line = jnp.where(bottom, count - 2, count - 1)
    row = start + t - 2
    ok = jnp.logical_and(row >= 0, row < total)
    return jnp.clip(lower, low_line, high_line), jnp.clip(lower + 1, low_line, high_line), part, ok


def first_kernel(
    coarse, noisy, gain, regb, regs, liftb, midg, midb, lifts, mids,
    got, got_cols, cols, grid, regw, regc, liftw, liftc, midw, lon, sidew, chosen,
    band, pieces, tile, rows, far_rows, gainv, regbv, vecs, regv, liftv, midv, liftt,
    send, recv, nsend, nrecv, local,
):
    me = lax.axis_index("lat")
    tile_rows = lax.axis_size("lat") // TILE_COLS
    r = me // TILE_COLS
    c = me % TILE_COLS
    north, south = r > 0, r < tile_rows - 1
    top, bottom = r == 0, r == tile_rows - 1
    cin, band_rows, clon = band.shape
    ch = midv.shape[1]
    nout, fr, fl = tile.shape
    blocks = regw.shape[0]
    halo = blocks + 1
    span = 2 * halo * TILE_COLS
    cw = chosen.shape[0]
    count = got.shape[0] - 2 * halo

    barrier = pltpu.get_barrier_semaphore()

    def greet(target):
        pl.semaphore_signal(barrier, inc=1, device_id={"lat": target}, device_id_type=MESH)

    for k in range(1, TILE_COLS):
        greet(r * TILE_COLS + (c + k) % TILE_COLS)

    @pl.when(north)
    def _():
        for k in range(TILE_COLS):
            greet((r - 1) * TILE_COLS + k)

    @pl.when(south)
    def _():
        for k in range(TILE_COLS):
            greet((r + 1) * TILE_COLS + k)

    loads = [
        pltpu.make_async_copy(coarse, band, local.at[0]),
        pltpu.make_async_copy(noisy.at[0], tile, local.at[1]),
        pltpu.make_async_copy(regs, regv, local.at[2]),
        pltpu.make_async_copy(mids, midv, local.at[3]),
        pltpu.make_async_copy(lifts, liftv, local.at[4]),
        pltpu.make_async_copy(gain, gainv, local.at[6]),
        pltpu.make_async_copy(regb, regbv, local.at[7]),
        pltpu.make_async_copy(liftb, vecs.at[0], local.at[8]),
        pltpu.make_async_copy(midg, vecs.at[1], local.at[9]),
        pltpu.make_async_copy(midb, vecs.at[2], local.at[10]),
    ]
    for load in loads:
        load.start()

    lane = lax.broadcasted_iota(jnp.int32, (1, 128), 1)
    both = band_rows * cin
    row_id = lax.broadcasted_iota(jnp.int32, (both, both), 0)
    sub_id = jnp.where(row_id >= cin, 1, 0)
    order = lax.broadcasted_iota(jnp.int32, (both, both), 1) == band_rows * (row_id - sub_id * cin) + sub_id
    order = jnp.where(order, 1.0, 0.0).astype(BF16)
    loads[0].wait()
    sorted_rows = jnp.dot(order, band[...].reshape(both, clon), preferred_element_type=F32)
    for sub in range(band_rows):
        row = sorted_rows[sub * cin:(sub + 1) * cin]
        parts = [row[:, b * 128:(b + 1) * 128] for b in range(TILE_COLS)]
        for b in range(TILE_COLS):
            pieces[b, sub, :cin, :] = parts[b].astype(BF16)
        side = jnp.zeros((16, 128), F32)
        for b in range(TILE_COLS):
            seam = jnp.where(lane < 64, parts[b], parts[(b + TILE_COLS - 1) % TILE_COLS])
            for g in range(cin // 16):
                at = g * span + 2 * halo * b
                moved = pltpu.roll(seam[g * 16:(g + 1) * 16], at + halo, 1)
                side = jnp.where(jnp.logical_and(lane >= at, lane < at + 2 * halo), moved, side)
        for b in range(TILE_COLS):
            pieces[b, sub, cin:, :] = side.astype(BF16)

    loads[1].wait()
    ends = []
    for n in range(nout):
        ends += [tile[n, :2, :].astype(F32), tile[n, fr - 2:, :].astype(F32)]
    rows[...] = jnp.concatenate(ends, axis=0).astype(BF16)
    pick_row = lax.broadcasted_iota(jnp.int32, (4 * nout, 128), 0)
    pick_lane = lax.broadcasted_iota(jnp.int32, (4 * nout, 128), 1)
    packed = jnp.zeros((4 * nout, fr), F32)
    for n in range(nout):
        for s, (lo, at) in enumerate(((0, 0), (0, 1), (fl - 128, 126), (fl - 128, 127))):
            if s % 2 == 0:
                hit = jnp.zeros(pick_row.shape, jnp.bool_)
            hit = jnp.logical_or(hit, jnp.logical_and(pick_row == s * nout + n, pick_lane == at))
            if s % 2:
                packed = packed + nt_dot(jnp.where(hit, 1.0, 0.0).astype(BF16), tile[n, :, lo:lo + 128])
    cols[...] = jnp.concatenate([packed, jnp.zeros((4 * nout, 128 - fr), F32)], axis=1).astype(BF16)

    peers = TILE_COLS - 1 + jnp.where(north, TILE_COLS, 0) + jnp.where(south, TILE_COLS, 0)
    pl.semaphore_wait(barrier, peers)

    def remote(src, dst, ssem, rsem, target):
        return pltpu.make_async_remote_copy(
            src_ref=src, dst_ref=dst, send_sem=ssem, recv_sem=rsem,
            device_id={"lat": target}, device_id_type=MESH)

    whole, upper, lower = (0, 2), (0, 1), (1, 1)

    def landing(slot, span_rows):
        return got.at[pl.ds(2 * slot + span_rows[0], span_rows[1])]

    def band_copy(k, row, slot, ssem, span_rows=whole):
        col = (c + k) % TILE_COLS
        return remote(pieces.at[col, pl.ds(*span_rows)], landing(slot, span_rows), send.at[ssem], recv.at[slot],
                      row * TILE_COLS + col)

    west, east = (c + TILE_COLS - 1) % TILE_COLS, (c + 1) % TILE_COLS

    def col_copy(slot, row, col):
        return remote(cols, got_cols.at[slot], nsend.at[slot], nrecv.at[slot], row * TILE_COLS + col)

    def row_copy(slot, row):
        return remote(rows, far_rows.at[slot], nsend.at[8 + slot], nrecv.at[8 + slot], row * TILE_COLS + c)

    def each_band(action):
        for col, side, row, slot, span_rows in (
            (2, south, r + 1, 0, lower), (3, south, r + 1, 1, whole),
            (0, north, r - 1, 6, whole), (1, north, r - 1, 7, upper),
        ):
            @pl.when(jnp.logical_and(side, c == col))
            def _():
                for k in range(TILE_COLS):
                    action(band_copy(k, row, slot, TILE_COLS + k, span_rows))

        for k in range(1, TILE_COLS):
            action(band_copy(k, r, 2 + c, k))

    def each_edge(action):
        action(col_copy(0, r, east))
        action(col_copy(1, r, west))

        @pl.when(south)
        def _():
            action(row_copy(0, r + 1))
            action(col_copy(6, r + 1, c))
            action(col_copy(2, r + 1, east))
            action(col_copy(3, r + 1, west))

        @pl.when(north)
        def _():
            action(row_copy(1, r - 1))
            action(col_copy(7, r - 1, c))
            action(col_copy(4, r - 1, east))
            action(col_copy(5, r - 1, west))

    each_band(lambda copy: copy.start())
    own = pltpu.make_async_copy(pieces.at[c], landing(2 + c, whole), local.at[5])
    own.start()

    loads[2].wait()
    for k in range(blocks):
        for p in range(3):
            for q in range(3):
                regw[k, p * cin:(p + 1) * cin, q * cin:(q + 1) * cin] = regv[9 * k + 3 * p + q]
    each_edge(lambda copy: copy.start())

    loads[3].wait()
    for tap in range(9):
        midw[:, tap * ch:(tap + 1) * ch] = midv[tap]
    for load in loads[4:]:
        load.wait()
    slab = liftt.shape[0] // 3
    for p in range(3):
        noise = []
        for q in range(3):
            base = p * slab + q * cin
            liftt[base:base + cin, :] = liftv[3 * p + q, :cin, :]
            noise.append(liftv[3 * p + q, cin:, :].astype(F32))
        spare_rows = slab - 3 * (cin + nout)
        if p == 1:
            noise += thirds(vecs[0]) + [jnp.zeros((spare_rows - 3, ch), F32)]
        else:
            noise.append(jnp.zeros((spare_rows, ch), F32))
        liftt[p * slab + 3 * cin:(p + 1) * slab, :] = jnp.concatenate(noise, axis=0).astype(BF16)
    eye = jnp.where(lax.broadcasted_iota(jnp.int32, (ch, ch), 0) == lax.broadcasted_iota(jnp.int32, (ch, ch), 1), 1.0, 0.0)
    liftw[...] = nt_dot(eye.astype(BF16), liftt[...]).astype(BF16)

    position = lax.broadcasted_iota(jnp.int32, (1, 3 * fl), 1)
    shift = jnp.where(position >= 2 * fl, 2, jnp.where(position >= fl, 1, 0))
    low, weight = lon_split(position - shift * fl + shift - 1)
    low_lane = jnp.where(low < 0, low + cw, low)
    high_lane = jnp.where(low + 1 < 0, low + 1 + cw, low + 1)
    coarse_lane = lax.broadcasted_iota(jnp.int32, (cw, 3 * fl), 0)
    lon[...] = jnp.where(coarse_lane == low_lane, 1.0 - weight,
                         jnp.where(coarse_lane == high_lane, weight, 0.0)).astype(BF16)

    for k in range(blocks):
        regc[2 * k] = column(gainv[k:k + 1, :]) * 0.5
        regc[2 * k + 1] = column(regbv[k:k + 1, :])
    liftc[...] = column(vecs[1]) * 0.5
    bias_cols = jnp.zeros((ch, 128), F32)
    for n, third in enumerate(thirds(column(vecs[2]))):
        bias_cols = jnp.where(lane == n, third, bias_cols)
    midw[:, 9 * ch:] = bias_cols[:, :16].astype(BF16)

    tall = fr + 4
    wide = fl // 128
    for n in range(nout):
        for j in range(wide):
            grid[j, n * tall + 2:n * tall + 2 + fr, :] = tile[n, :, j * 128:(j + 1) * 128].astype(F32)

    near = fl // LON_UP
    picked_cols = [-1, 0, near - 1, near]
    select_lane = lax.broadcasted_iota(jnp.int32, (cw, 128), 0)
    select_pos = lax.broadcasted_iota(jnp.int32, (cw, 128), 1)
    hits = jnp.zeros((cw, 128), jnp.bool_)
    for s, col in enumerate(picked_cols):
        hits = jnp.logical_or(hits, jnp.logical_and(select_pos == s, select_lane == col % cw))
    chosen[...] = jnp.where(hits, 1.0, 0.0).astype(BF16)
    key = lax.broadcasted_iota(jnp.int32, (128, 1), 0)
    key_line = key // 4
    key_pick = key - 4 * key_line
    key_col = jnp.where(key_pick == 0, picked_cols[0], jnp.where(
        key_pick == 1, picked_cols[1], jnp.where(key_pick == 2, picked_cols[2], picked_cols[3])))
    edge_row = jnp.where(lane < HALF, lane, lane - HALF)
    for p in range(3):
        a, b, share, ok = lat_split(edge_row + p, top, bottom, count, r * fr, fr * tile_rows)
        wa = jnp.where(ok, 1.0 - share, 0.0)
        wb = jnp.where(ok, share, 0.0)
        by_row = jnp.where(key_line == a, wa, 0.0) + jnp.where(key_line == b, wb, 0.0)
        for q in range(3):
            lower_col, share_m = lon_split(jnp.where(lane < HALF, q - 2, fl - 1 + q))
            by_col = jnp.where(key_col == lower_col, 1.0 - share_m, jnp.where(key_col == lower_col + 1, share_m, 0.0))
            sidew[3 * p + q] = (by_row * by_col).astype(BF16)

    own.wait()

    def arrived(slot, span_rows=whole):
        remote(pieces.at[0, pl.ds(*span_rows)], landing(slot, span_rows), send.at[0], recv.at[slot], me).wait_recv()

    def edge(slot):
        if slot < 8:
            remote(cols, got_cols.at[slot], nsend.at[slot], nrecv.at[slot], me).wait_recv()
        else:
            remote(rows, far_rows.at[slot - 8], nsend.at[slot], nrecv.at[slot], me).wait_recv()

    for k in range(1, TILE_COLS):
        arrived(2 + (c + k) % TILE_COLS)

    @pl.when(north)
    def _():
        arrived(0, lower)
        arrived(1)

    @pl.when(south)
    def _():
        arrived(6)
        arrived(7, upper)

    edge(0)
    edge(1)

    @pl.when(north)
    def _():
        for slot in (2, 3, 6, 8):
            edge(slot)

    @pl.when(south)
    def _():
        for slot in (4, 5, 7, 9):
            edge(slot)

    for n in range(nout):
        for j in range(wide):
            at = slice(j * 128, (j + 1) * 128)
            above = far_rows[0, :, at].astype(F32)[4 * n + 2:4 * n + 4]
            below = far_rows[1, :, at].astype(F32)[4 * n:4 * n + 2]
            grid[j, n * tall:n * tall + 2, :] = jnp.where(top, 0.0, above)
            grid[j, n * tall + 2 + fr:(n + 1) * tall, :] = jnp.where(bottom, 0.0, below)

    each_band(lambda copy: copy.wait_send())
    each_edge(lambda copy: copy.wait_send())


def first_program(coarse, noisy, gain, regb, regs, liftb, midg, midb, lifts, mids):
    hbm = pl.BlockSpec(memory_space=pltpu.HBM)
    vmem = pl.BlockSpec(memory_space=pltpu.VMEM)
    dma = pltpu.SemaphoreType.DMA
    cin, band_rows, clon = coarse.shape
    nout, fr, fl = noisy.shape[1:]
    ch = mids.shape[1]
    blocks = regs.shape[0] // 9
    slab = 3 * cin + -(-(3 * nout + 3) // 16) * 16
    lines_n = band_rows * (TILE_COLS + 4)
    ct_lon = clon // TILE_COLS
    cw = 2 * ct_lon
    assert ct_lon == 128 and cin % 16 == 0 and band_rows == 2
    assert (cin // 16) * 2 * (blocks + 1) * TILE_COLS <= 128
    shape = jax.ShapeDtypeStruct
    return pl.pallas_call(
        first_kernel,
        out_shape=(
            shape((lines_n, cin + 16, 128), BF16),
            shape((8, 4 * nout, 128), BF16),
            shape((4 * nout, 128), BF16),
            shape((fl // 128, nout * (fr + 4), 128), F32),
            shape((blocks, 3 * cin, 3 * cin), BF16),
            shape((2 * blocks, cin, 128), F32),
            shape((ch, 3 * slab), BF16),
            shape((ch, 128), F32),
            shape((ch, 9 * ch + 16), BF16),
            shape((cw, 3 * fl), BF16),
            shape((9, 128, 128), BF16),
            shape((cw, 128), BF16),
        ),
        in_specs=[hbm] * 10,
        out_specs=(vmem,) * 12,
        scratch_shapes=[
            pltpu.VMEM((cin, band_rows, clon), BF16),
            pltpu.VMEM((TILE_COLS, band_rows, cin + 16, 128), BF16),
            pltpu.VMEM((nout, fr, fl), BF16),
            pltpu.VMEM((4 * nout, fl), BF16),
            pltpu.VMEM((2, 4 * nout, fl), BF16),
            pltpu.VMEM(gain.shape, F32),
            pltpu.VMEM(regb.shape, F32),
            pltpu.VMEM((3, 1, ch), F32),
            pltpu.VMEM(regs.shape, BF16),
            pltpu.VMEM(lifts.shape, BF16),
            pltpu.VMEM(mids.shape, BF16),
            pltpu.VMEM((3 * slab, ch), BF16),
            dma((2 * TILE_COLS,)), dma((8,)), dma((10,)), dma((10,)), dma((11,)),
        ],
        compiler_params=pltpu.CompilerParams(
            collective_id=0, has_side_effects=True, vmem_limit_bytes=20_000_000),
    )(*[pltpu.with_memory_space_constraint(x, pltpu.HBM) for x in (
        coarse, noisy, gain, regb, regs, liftb, midg, midb, lifts, mids)])


def tile_kernel(
    dims, got, got_cols, own_cols, grid, regw, regc, liftw, gains, midw, lon, sidew, chosen, out,
    held, part, field, lines, upper, sides, bands, unit, raw, prod, edges, rows_out, stage, sems,
):
    cin, ch, nout, fr, fl = dims
    lines_n, count, cw = got.shape[0], field.shape[0], field.shape[2]
    blocks = regw.shape[0]
    halo = blocks + 1
    span = 2 * halo * TILE_COLS
    me = lax.axis_index("lat")
    tile_row, tile_rows = me // TILE_COLS, lax.axis_size("lat") // TILE_COLS
    c = me % TILE_COLS
    after_seam = (c + 1) % TILE_COLS
    top, bottom = tile_row == 0, tile_row == tile_rows - 1
    steps = bands.shape[0]
    wide = fl // 128
    lane = lax.broadcasted_iota(jnp.int32, (1, 128), 1)
    lane_first, lane_last = lane == 0, lane == 127
    spare = lines_n // 4

    def known(i, values):
        if i < spare:
            return jnp.where(top, 0.0, values)
        if i >= lines_n - spare:
            return jnp.where(bottom, 0.0, values)
        return values

    def spread(k, i, values):
        values = activate(values, regc[2 * k][:, :1])
        taps = jnp.concatenate(
            [pltpu.roll(values, 1, 1).astype(BF16), values.astype(BF16), pltpu.roll(values, cw - 1, 1).astype(BF16)],
            axis=0)
        part[k % 2, i] = jnp.dot(regw[k], taps, preferred_element_type=F32)

    def enter(i):
        side = got[i, cin:, :].astype(F32)
        outer = []
        for g in range(cin // 16):
            after = pltpu.roll(side, 128 - halo - g * span - 2 * halo * after_seam, 1)
            before = pltpu.roll(side, 128 - halo - g * span - 2 * halo * c, 1)
            outer.append(jnp.where(lane < halo, after, jnp.where(lane >= 128 - halo, before, 0.0)))
        values = jnp.concatenate([got[i, :cin, :].astype(F32), jnp.concatenate(outer, axis=0)], axis=1)
        values = known(i, values)
        held[i] = values
        spread(0, i, values)

    def update(k, i):
        values = held[i] + part[k % 2, i - 1, :cin, :] + part[k % 2, i, cin:2 * cin, :] + part[k % 2, i + 1, 2 * cin:, :]
        values = (values + regc[2 * k + 1][:, :1]).astype(BF16)
        return known(i, values.astype(F32))

    def follow(k, i):
        values = update(k - 1, i)
        held[i] = values
        spread(k, i, values)

    def widen(first, last):
        coarse = field[first:last].reshape((last - first) * cin, cw)
        for q in range(3):
            lines[first:last, q * cin:(q + 1) * cin, :] = jnp.dot(
                coarse, lon[:, q * fl:(q + 1) * fl], preferred_element_type=F32).reshape(last - first, cin, fl)

    def blend(t):
        return lat_split(t, top, bottom, count, tile_row * fr, fr * tile_rows)

    def inside(t):
        row = tile_row * fr + t - 2
        return jnp.logical_and(row >= 0, row < fr * tile_rows)

    tall = fr + 4
    slab = upper.shape[1]

    def along(middle, above, below):
        above = jnp.where(top, 0.0, pltpu.roll(above.astype(F32), 128 - (fr - 2), 1))
        below = jnp.where(bottom, 0.0, pltpu.roll(below.astype(F32), fr + 2, 1))
        middle = pltpu.roll(middle.astype(F32), 2, 1)
        return jnp.where(lane < 2, above, jnp.where(lane < fr + 2, middle, below))

    west = along(got_cols[0], got_cols[2], got_cols[4])
    east = along(got_cols[1], got_cols[3], got_cols[5])
    here = along(own_cols[...], got_cols[6], got_cols[7])
    none = jnp.ones((slab - 3 * (cin + nout), 128), F32)
    left_cols = jnp.concatenate([west[2 * nout:], here[:nout], none], axis=0)
    right_cols = jnp.concatenate([here[3 * nout:], east[:2 * nout], none], axis=0)
    west_col, east_col = west[3 * nout:], east[:nout]

    def noise_rows(t):
        rows = [grid[j, pl.ds(t, nout, stride=tall), :] for j in range(wide)]
        onward = [pltpu.roll(v, 1, 1) for v in rows]
        back = [pltpu.roll(v, 127, 1) for v in rows]
        edge_l = pltpu.roll(west_col, (128 - t) % 128 if isinstance(t, int) else 128 - t, 1)
        edge_r = pltpu.roll(east_col, 127 - t, 1)
        pieces = []
        for j in range(wide):
            lo = jnp.where(lane_first, onward[j - 1] if j else edge_l, onward[j])
            hi = jnp.where(lane_last, back[j + 1] if j < wide - 1 else edge_r, back[j])
            pieces.append(jnp.concatenate([lo, rows[j], hi, none], axis=0))
        return jnp.concatenate(pieces, axis=1).astype(BF16)

    def raise_row(t, slot):
        a, b, share, ok = blend(jnp.int32(t))
        wa = jnp.where(ok, 1.0 - share, 0.0)
        wb = jnp.where(ok, share, 0.0)
        for o in range(0, 3 * cin, 16):
            upper[slot, o:o + 16, :] = (wa * lines[a, o:o + 16, :] + wb * lines[b, o:o + 16, :]).astype(BF16)
        upper[slot, 3 * cin:slab, :] = noise_rows(t)

    edge_row = jnp.where(lane < HALF, lane, lane - HALF)

    def build_edges():
        narrow = jnp.dot(field[...].reshape(count * cin, cw), chosen[...], preferred_element_type=F32)
        packed = narrow[:cin]
        for i in range(1, count):
            packed = packed + pltpu.roll(narrow[i * cin:(i + 1) * cin], 4 * i, 1)
        packed = packed.astype(BF16)
        for p in range(3):
            for q in range(3):
                base = p * slab + q * cin
                sides[base:base + cin, :] = jnp.dot(packed, sidew[3 * p + q], preferred_element_type=F32).astype(BF16)
            sides[p * slab + 3 * cin:(p + 1) * slab, :] = jnp.where(
                lane < HALF, pltpu.roll(left_cols, (128 - p) % 128, 1), pltpu.roll(right_cols, HALF - p, 1)).astype(BF16)
        edge_lift = jnp.dot(liftw[...], sides[...], preferred_element_type=F32)
        edges[...] = jnp.where(inside(edge_row + 1), activate(edge_lift, gains[...]), 0.0).astype(BF16)

    def lift(slot, target):
        window = jnp.concatenate([upper[(slot + n) % steps] for n in range(3)], axis=0)
        raw[target % steps] = jnp.dot(liftw[...], window, preferred_element_type=F32)

    def finish(l, slot):
        squares = jnp.zeros((8, fl), F32)
        for o in range(0, ch, 16):
            values = raw[slot, o:o + 16, :]
            values = values * values
            squares = squares + (values[:8] + values[8:])
        inverse = lax.rsqrt(jnp.sum(squares, axis=0, keepdims=True) * (1.0 / ch) + EPSILON)
        inverse = jnp.where(inside(l + 1), inverse, 0.0)
        for o in range(0, ch, 16):
            half_gain = jnp.concatenate([gains[o:o + 16, :]] * wide, axis=1)
            half = raw[slot, o:o + 16, :] * inverse * half_gain
            values = (half + half * jnp.tanh(half)).astype(BF16)
            edge = edges[o:o + 16, :]
            parts = [values[:, j * 128:(j + 1) * 128] for j in range(wide)]
            onward = [pltpu.roll(v, 1, 1) for v in parts]
            back = [pltpu.roll(v, 127, 1) for v in parts]
            edge_l = pltpu.roll(edge, 128 - l, 1)
            edge_r = pltpu.roll(edge, 128 + HALF - 1 - l, 1)
            bands[slot, ch + o:ch + o + 16, :] = values
            bands[slot, o:o + 16, :] = jnp.concatenate(
                [jnp.where(lane_first, onward[j - 1] if j else edge_l, onward[j]) for j in range(wide)], axis=1)
            bands[slot, 2 * ch + o:2 * ch + o + 16, :] = jnp.concatenate(
                [jnp.where(lane_last, back[j + 1] if j < wide - 1 else edge_r, back[j]) for j in range(wide)], axis=1)

    def mid(slot):
        window = jnp.concatenate([bands[(slot + n) % steps] for n in range(3)] + [unit[...]], axis=0)
        prod[slot % 2] = jnp.dot(midw[...], window, preferred_element_type=F32)

    group = stage.shape[2]
    blocks_out = ch // 8

    def flushed(n):
        return pltpu.make_async_copy(
            stage.at[n % 2], out.at[0, :, pl.ds(pl.multiple_of(n * group, group), group), :], sems.at[n % 2])

    def shrink(n, o):
        for j in range(wide):
            block = rows_out[n % 2, j, pl.ds(pl.multiple_of(o * 8 * group, 8 * group), 8 * group), :]
            stage[n % 2, pl.ds(o * 8, 8), :, j * 128:(j + 1) * 128] = block.reshape(8, group, 128).astype(BF16)

    def emit(n, spot, slot):
        for o in range(0, ch, 16):
            for j in range(wide):
                at = slice(j * 128, (j + 1) * 128)
                total = raw[(slot + 1) % steps, o:o + 16, at] + prod[slot % 2, o:o + 16, at]
                rows_out[n % 2, j, pl.ds(spot + o * group, 16, stride=group), :] = total

    unit[...] = jnp.ones(unit.shape, BF16)

    def raised(t):
        raise_row(t, t % steps)

    def lifted(l):
        lift(l % steps, l)

    def finished(l):
        finish(jnp.int32(l), l % steps)

    early = [[(raised, 0), (raised, 1), (raised, 2)], [(lifted, 0), (raised, 3)], [(lifted, 1), (raised, 4)],
             [(lifted, 2), (raised, 5)], [(lifted, 3), (raised, 6)]]
    widened = 0
    for i in range(1, lines_n - 1):
        enter(i)
        for k in range(1, blocks):
            if 1 + k <= i - k < lines_n - 1 - k:
                follow(k, i - k)
        row = i - blocks
        if halo <= row < lines_n - halo:
            field[row - halo] = update(blocks - 1, row).astype(BF16)
            if (row - halo) % 2:
                widen(widened, row - halo + 1)
                widened = row - halo + 1
            if widened >= 2 and early and (widened >= 4 or len(early) > 2):
                for action, n in early.pop(0):
                    action(n)
    if widened < count:
        widen(widened, count)
    for actions in early:
        for action, n in actions:
            action(n)
    build_edges()
    finished(0)
    lifted(4)
    raised(7)
    finished(1)
    finished(2)
    mid(0)
    finished(3)

    halves = group // steps
    share_out = blocks_out // group

    def step(i, u, e, last):
        n = i // halves
        shrink_at = (i % halves) * (blocks_out // halves) + u * share_out
        for o in range(share_out):
            shrink(n + 1, shrink_at + o)
        emit(n, (i % halves) * steps + u, u)
        if last is None or last + 1 < fr:
            mid((u + 1) % steps)
        if last is None or last + 4 < fr + 2:
            finish(e + 4, (u + 4) % steps)
        if last is None or last + 5 < fr + 2:
            lift((u + 5) % steps, u + 5)
        if last is None:
            raise_row(e + 8, u)

    trips = fr // steps

    def begin(i):
        @pl.when(jnp.logical_and(i % halves == 0, i >= 3 * halves))
        def _():
            flushed(i // halves - 3).wait()

    def finish_trip(i):
        @pl.when(jnp.logical_and(i % halves == halves - 1, i >= halves))
        def _():
            flushed(i // halves - 1).start()

    def trip(i, _):
        begin(i)
        for u in range(steps):
            step(i, u, i * steps + u, None)
        finish_trip(i)
        return 0

    lax.fori_loop(0, trips - 1, trip, 0)
    i = jnp.int32(trips - 1)
    begin(i)
    for u in range(steps):
        step(i, u, i * steps + u, fr - steps + u)
    finish_trip(i)
    groups = fr // group
    if groups >= 3:
        flushed(groups - 3).wait()
    for o in range(blocks_out):
        shrink(groups - 1, o)
    flushed(groups - 1).start()
    for n in range(max(groups - 2, 0), groups):
        flushed(n).wait()


def tile_program(dims, prepared):
    cin, ch, nout, fr, fl = dims
    got, lon, liftw = prepared[0], prepared[9], prepared[6]
    lines_n = got.shape[0]
    cw = lon.shape[0]
    blocks = prepared[4].shape[0]
    count = lines_n - 2 * (blocks + 1)
    group = 8
    steps = 4
    vmem = pl.BlockSpec(memory_space=pltpu.VMEM)
    slab = liftw.shape[1] // 3
    return pl.pallas_call(
        functools.partial(tile_kernel, dims),
        out_shape=jax.ShapeDtypeStruct((1, ch, fr, fl), BF16),
        in_specs=[vmem] * len(prepared),
        out_specs=pl.BlockSpec(memory_space=pl.ANY),
        scratch_shapes=[
            pltpu.VMEM((lines_n, cin, cw), F32),
            pltpu.VMEM((2, lines_n, 3 * cin, cw), F32),
            pltpu.VMEM((count, cin, cw), BF16),
            pltpu.VMEM((count, 3 * cin, fl), F32),
            pltpu.VMEM((steps, slab, fl), BF16),
            pltpu.VMEM((3 * slab, 128), BF16),
            pltpu.VMEM((steps, 3 * ch, fl), BF16),
            pltpu.VMEM((16, fl), BF16),
            pltpu.VMEM((steps, ch, fl), F32),
            pltpu.VMEM((2, ch, fl), F32),
            pltpu.VMEM((ch, 128), BF16),
            pltpu.VMEM((2, fl // 128, ch * group, 128), F32),
            pltpu.VMEM((2, ch, group, fl), BF16),
            pltpu.SemaphoreType.DMA((2,)),
        ],
        compiler_params=pltpu.CompilerParams(vmem_limit_bytes=44_000_000),
    )(*prepared)


def per_device(
    coarse, reg_gain, reg_weight, reg_bias, noisy, lift_weight, lift_bias, mid_gain, mid_weight, mid_bias,
):
    lifts = lift_weight.transpose(0, 1, 3, 2)
    prepared = first_program(
        coarse, noisy, reg_gain, reg_bias, reg_weight.reshape((-1,) + reg_weight.shape[3:]),
        lift_bias[None], mid_gain[None], mid_bias[None],
        lifts.reshape((9,) + lifts.shape[2:]), mid_weight.reshape((9,) + mid_weight.shape[2:]))
    return tile_program((coarse.shape[0], mid_weight.shape[2]) + noisy.shape[1:], prepared)


def solution(mesh):
    placed = (
        P(None, ("grp", "lat"), None),
        P(),
        P(),
        P(),
        P(("grp", "lat"), None, None, None),
        P(),
        P(),
        P(),
        P(),
        P(),
    )
    return jax.shard_map(
        per_device,
        mesh=mesh,
        in_specs=placed,
        out_specs=P(("grp", "lat"), None, None, None),
        check_vma=False,
    )
```

```python
import functools

import jax
import jax.numpy as jnp
from jax import lax
from jax.experimental import pallas as pl
from jax.experimental.pallas import tpu as pltpu
from jax.sharding import PartitionSpec as P

TILE_COLS = 4
LAT_UP = 4
LON_UP = 4
EPSILON = 1e-06
F32 = jnp.float32
BF16 = jnp.bfloat16
MESH = pl.DeviceIdType.MESH
HALF = 64


def activate(values, half_gain):
    inverse = lax.rsqrt(jnp.mean(values * values, axis=0, keepdims=True) + EPSILON)
    half = values * inverse * half_gain
    return half + half * jnp.tanh(half)


def split(numerator, factor):
    lower = numerator // (2 * factor)
    return lower, (numerator - 2 * factor * lower).astype(F32) / (2.0 * factor)


def column(row):
    n = row.shape[1]
    here = lax.broadcasted_iota(jnp.int32, (n, n), 0) == lax.broadcasted_iota(jnp.int32, (n, n), 1)
    return jnp.broadcast_to(jnp.sum(jnp.where(here, row, 0.0), axis=1, keepdims=True), (n, 128))


def thirds(values):
    high = values.astype(BF16).astype(F32)
    middle = (values - high).astype(BF16).astype(F32)
    return [high, middle, values - high - middle]


def nt_dot(a, b):
    return lax.dot_general(a, b, (((1,), (1,)), ((), ())), preferred_element_type=F32)


def lon_split(fine_col):
    lower, part = split(2 * fine_col + 1 - LON_UP + 2 * LON_UP, LON_UP)
    return lower - 1, part


def lat_split(t, top, bottom, count, start, total):
    lower, part = split(2 * (t - 2) + 1 - LAT_UP + 2 * LAT_UP, LAT_UP)
    low_line = jnp.where(top, 1, 0)
    high_line = jnp.where(bottom, count - 2, count - 1)
    row = start + t - 2
    ok = jnp.logical_and(row >= 0, row < total)
    return jnp.clip(lower, low_line, high_line), jnp.clip(lower + 1, low_line, high_line), part, ok


def first_kernel(
    coarse, noisy, gain, regb, regs, liftb, midg, midb, lifts, mids,
    got, got_cols, cols, grid, regw, regc, liftw, liftc, midw, lon, sidew, chosen,
    band, pieces, tile, rows, far_rows, gainv, regbv, vecs, regv, liftv, midv, liftt,
    send, recv, nsend, nrecv, local,
):
    me = lax.axis_index("lat")
    tile_rows = lax.axis_size("lat") // TILE_COLS
    r = me // TILE_COLS
    c = me % TILE_COLS
    north, south = r > 0, r < tile_rows - 1
    top, bottom = r == 0, r == tile_rows - 1
    cin, band_rows, clon = band.shape
    ch = midv.shape[1]
    nout, fr, fl = tile.shape
    blocks = regw.shape[0]
    halo = blocks + 1
    span = 2 * halo * TILE_COLS
    cw = chosen.shape[0]
    count = got.shape[0] - 2 * halo

    barrier = pltpu.get_barrier_semaphore()

    def greet(target):
        pl.semaphore_signal(barrier, inc=1, device_id={"lat": target}, device_id_type=MESH)

    for k in range(1, TILE_COLS):
        greet(r * TILE_COLS + (c + k) % TILE_COLS)

    @pl.when(north)
    def _():
        for k in range(TILE_COLS):
            greet((r - 1) * TILE_COLS + k)

    @pl.when(south)
    def _():
        for k in range(TILE_COLS):
            greet((r + 1) * TILE_COLS + k)

    loads = [
        pltpu.make_async_copy(coarse, band, local.at[0]),
        pltpu.make_async_copy(noisy.at[0], tile, local.at[1]),
        pltpu.make_async_copy(regs, regv, local.at[2]),
        pltpu.make_async_copy(mids, midv, local.at[3]),
        pltpu.make_async_copy(lifts, liftv, local.at[4]),
        pltpu.make_async_copy(gain, gainv, local.at[6]),
        pltpu.make_async_copy(regb, regbv, local.at[7]),
        pltpu.make_async_copy(liftb, vecs.at[0], local.at[8]),
        pltpu.make_async_copy(midg, vecs.at[1], local.at[9]),
        pltpu.make_async_copy(midb, vecs.at[2], local.at[10]),
    ]
    for load in loads:
        load.start()

    lane = lax.broadcasted_iota(jnp.int32, (1, 128), 1)
    both = band_rows * cin
    row_id = lax.broadcasted_iota(jnp.int32, (both, both), 0)
    sub_id = jnp.where(row_id >= cin, 1, 0)
    order = lax.broadcasted_iota(jnp.int32, (both, both), 1) == band_rows * (row_id - sub_id * cin) + sub_id
    order = jnp.where(order, 1.0, 0.0).astype(BF16)
    loads[0].wait()
    sorted_rows = jnp.dot(order, band[...].reshape(both, clon), preferred_element_type=F32)
    for sub in range(band_rows):
        row = sorted_rows[sub * cin:(sub + 1) * cin]
        parts = [row[:, b * 128:(b + 1) * 128] for b in range(TILE_COLS)]
        for b in range(TILE_COLS):
            pieces[b, sub, :cin, :] = parts[b].astype(BF16)
        side = jnp.zeros((16, 128), F32)
        for b in range(TILE_COLS):
            seam = jnp.where(lane < 64, parts[b], parts[(b + TILE_COLS - 1) % TILE_COLS])
            for g in range(cin // 16):
                at = g * span + 2 * halo * b
                moved = pltpu.roll(seam[g * 16:(g + 1) * 16], at + halo, 1)
                side = jnp.where(jnp.logical_and(lane >= at, lane < at + 2 * halo), moved, side)
        for b in range(TILE_COLS):
            pieces[b, sub, cin:, :] = side.astype(BF16)

    loads[1].wait()
    ends = []
    for n in range(nout):
        ends += [tile[n, :2, :].astype(F32), tile[n, fr - 2:, :].astype(F32)]
    rows[...] = jnp.concatenate(ends, axis=0).astype(BF16)
    pick_row = lax.broadcasted_iota(jnp.int32, (4 * nout, 128), 0)
    pick_lane = lax.broadcasted_iota(jnp.int32, (4 * nout, 128), 1)
    packed = jnp.zeros((4 * nout, fr), F32)
    for n in range(nout):
        for s, (lo, at) in enumerate(((0, 0), (0, 1), (fl - 128, 126), (fl - 128, 127))):
            if s % 2 == 0:
                hit = jnp.zeros(pick_row.shape, jnp.bool_)
            hit = jnp.logical_or(hit, jnp.logical_and(pick_row == s * nout + n, pick_lane == at))
            if s % 2:
                packed = packed + nt_dot(jnp.where(hit, 1.0, 0.0).astype(BF16), tile[n, :, lo:lo + 128])
    cols[...] = jnp.concatenate([packed, jnp.zeros((4 * nout, 128 - fr), F32)], axis=1).astype(BF16)

    peers = TILE_COLS - 1 + jnp.where(north, TILE_COLS, 0) + jnp.where(south, TILE_COLS, 0)
    pl.semaphore_wait(barrier, peers)

    def remote(src, dst, ssem, rsem, target):
        return pltpu.make_async_remote_copy(
            src_ref=src, dst_ref=dst, send_sem=ssem, recv_sem=rsem,
            device_id={"lat": target}, device_id_type=MESH)

    whole, upper, lower = (0, 2), (0, 1), (1, 1)

    def landing(slot, span_rows):
        return got.at[pl.ds(2 * slot + span_rows[0], span_rows[1])]

    def band_copy(k, row, slot, ssem, span_rows=whole):
        col = (c + k) % TILE_COLS
        return remote(pieces.at[col, pl.ds(*span_rows)], landing(slot, span_rows), send.at[ssem], recv.at[slot],
                      row * TILE_COLS + col)

    west, east = (c + TILE_COLS - 1) % TILE_COLS, (c + 1) % TILE_COLS

    def col_copy(slot, row, col):
        return remote(cols, got_cols.at[slot], nsend.at[slot], nrecv.at[slot], row * TILE_COLS + col)

    def row_copy(slot, row):
        return remote(rows, far_rows.at[slot], nsend.at[8 + slot], nrecv.at[8 + slot], row * TILE_COLS + c)

    def each_band(action):
        for col, side, row, slot, span_rows in (
            (2, south, r + 1, 0, lower), (3, south, r + 1, 1, whole),
            (0, north, r - 1, 6, whole), (1, north, r - 1, 7, upper),
        ):
            @pl.when(jnp.logical_and(side, c == col))
            def _():
                for k in range(TILE_COLS):
                    action(band_copy(k, row, slot, TILE_COLS + k, span_rows))

        for k in range(1, TILE_COLS):
            action(band_copy(k, r, 2 + c, k))

    def each_edge(action):
        action(col_copy(0, r, east))
        action(col_copy(1, r, west))

        @pl.when(south)
        def _():
            action(row_copy(0, r + 1))
            action(col_copy(6, r + 1, c))
            action(col_copy(2, r + 1, east))
            action(col_copy(3, r + 1, west))

        @pl.when(north)
        def _():
            action(row_copy(1, r - 1))
            action(col_copy(7, r - 1, c))
            action(col_copy(4, r - 1, east))
            action(col_copy(5, r - 1, west))

    each_band(lambda copy: copy.start())
    own = pltpu.make_async_copy(pieces.at[c], landing(2 + c, whole), local.at[5])
    own.start()

    loads[2].wait()
    for k in range(blocks):
        for p in range(3):
            for q in range(3):
                regw[k, p * cin:(p + 1) * cin, q * cin:(q + 1) * cin] = regv[9 * k + 3 * p + q]
    each_edge(lambda copy: copy.start())

    loads[3].wait()
    for tap in range(9):
        midw[:, tap * ch:(tap + 1) * ch] = midv[tap]
    for load in loads[4:]:
        load.wait()
    slab = liftt.shape[0] // 3
    for p in range(3):
        noise = []
        for q in range(3):
            base = p * slab + q * cin
            liftt[base:base + cin, :] = liftv[3 * p + q, :cin, :]
            noise.append(liftv[3 * p + q, cin:, :].astype(F32))
        spare_rows = slab - 3 * (cin + nout)
        if p == 1:
            noise += thirds(vecs[0]) + [jnp.zeros((spare_rows - 3, ch), F32)]
        else:
            noise.append(jnp.zeros((spare_rows, ch), F32))
        liftt[p * slab + 3 * cin:(p + 1) * slab, :] = jnp.concatenate(noise, axis=0).astype(BF16)
    eye = jnp.where(lax.broadcasted_iota(jnp.int32, (ch, ch), 0) == lax.broadcasted_iota(jnp.int32, (ch, ch), 1), 1.0, 0.0)
    liftw[...] = nt_dot(eye.astype(BF16), liftt[...]).astype(BF16)

    position = lax.broadcasted_iota(jnp.int32, (1, 3 * fl), 1)
    shift = jnp.where(position >= 2 * fl, 2, jnp.where(position >= fl, 1, 0))
    low, weight = lon_split(position - shift * fl + shift - 1)
    low_lane = jnp.where(low < 0, low + cw, low)
    high_lane = jnp.where(low + 1 < 0, low + 1 + cw, low + 1)
    coarse_lane = lax.broadcasted_iota(jnp.int32, (cw, 3 * fl), 0)
    lon[...] = jnp.where(coarse_lane == low_lane, 1.0 - weight,
                         jnp.where(coarse_lane == high_lane, weight, 0.0)).astype(BF16)

    for k in range(blocks):
        regc[2 * k] = column(gainv[k:k + 1, :]) * 0.5
        regc[2 * k + 1] = column(regbv[k:k + 1, :])
    liftc[...] = column(vecs[1]) * 0.5
    bias_cols = jnp.zeros((ch, 128), F32)
    for n, third in enumerate(thirds(column(vecs[2]))):
        bias_cols = jnp.where(lane == n, third, bias_cols)
    midw[:, 9 * ch:] = bias_cols[:, :16].astype(BF16)

    tall = fr + 4
    wide = fl // 128
    for n in range(nout):
        for j in range(wide):
            grid[j, n * tall + 2:n * tall + 2 + fr, :] = tile[n, :, j * 128:(j + 1) * 128].astype(F32)

    near = fl // LON_UP
    picked_cols = [-1, 0, near - 1, near]
    select_lane = lax.broadcasted_iota(jnp.int32, (cw, 128), 0)
    select_pos = lax.broadcasted_iota(jnp.int32, (cw, 128), 1)
    hits = jnp.zeros((cw, 128), jnp.bool_)
    for s, col in enumerate(picked_cols):
        hits = jnp.logical_or(hits, jnp.logical_and(select_pos == s, select_lane == col % cw))
    chosen[...] = jnp.where(hits, 1.0, 0.0).astype(BF16)
    key = lax.broadcasted_iota(jnp.int32, (128, 1), 0)
    key_line = key // 4
    key_pick = key - 4 * key_line
    key_col = jnp.where(key_pick == 0, picked_cols[0], jnp.where(
        key_pick == 1, picked_cols[1], jnp.where(key_pick == 2, picked_cols[2], picked_cols[3])))
    edge_row = jnp.where(lane < HALF, lane, lane - HALF)
    for p in range(3):
        a, b, share, ok = lat_split(edge_row + p, top, bottom, count, r * fr, fr * tile_rows)
        wa = jnp.where(ok, 1.0 - share, 0.0)
        wb = jnp.where(ok, share, 0.0)
        by_row = jnp.where(key_line == a, wa, 0.0) + jnp.where(key_line == b, wb, 0.0)
        for q in range(3):
            lower_col, share_m = lon_split(jnp.where(lane < HALF, q - 2, fl - 1 + q))
            by_col = jnp.where(key_col == lower_col, 1.0 - share_m, jnp.where(key_col == lower_col + 1, share_m, 0.0))
            sidew[3 * p + q] = (by_row * by_col).astype(BF16)

    own.wait()

    def arrived(slot, span_rows=whole):
        remote(pieces.at[0, pl.ds(*span_rows)], landing(slot, span_rows), send.at[0], recv.at[slot], me).wait_recv()

    def edge(slot):
        if slot < 8:
            remote(cols, got_cols.at[slot], nsend.at[slot], nrecv.at[slot], me).wait_recv()
        else:
            remote(rows, far_rows.at[slot - 8], nsend.at[slot], nrecv.at[slot], me).wait_recv()

    for k in range(1, TILE_COLS):
        arrived(2 + (c + k) % TILE_COLS)

    @pl.when(north)
    def _():
        arrived(0, lower)
        arrived(1)

    @pl.when(south)
    def _():
        arrived(6)
        arrived(7, upper)

    edge(0)
    edge(1)

    @pl.when(north)
    def _():
        for slot in (2, 3, 6, 8):
            edge(slot)

    @pl.when(south)
    def _():
        for slot in (4, 5, 7, 9):
            edge(slot)

    for n in range(nout):
        for j in range(wide):
            at = slice(j * 128, (j + 1) * 128)
            above = far_rows[0, :, at].astype(F32)[4 * n + 2:4 * n + 4]
            below = far_rows[1, :, at].astype(F32)[4 * n:4 * n + 2]
            grid[j, n * tall:n * tall + 2, :] = jnp.where(top, 0.0, above)
            grid[j, n * tall + 2 + fr:(n + 1) * tall, :] = jnp.where(bottom, 0.0, below)

    each_band(lambda copy: copy.wait_send())
    each_edge(lambda copy: copy.wait_send())


def first_program(coarse, noisy, gain, regb, regs, liftb, midg, midb, lifts, mids):
    hbm = pl.BlockSpec(memory_space=pltpu.HBM)
    vmem = pl.BlockSpec(memory_space=pltpu.VMEM)
    dma = pltpu.SemaphoreType.DMA
    cin, band_rows, clon = coarse.shape
    nout, fr, fl = noisy.shape[1:]
    ch = mids.shape[1]
    blocks = regs.shape[0] // 9
    slab = 3 * cin + -(-(3 * nout + 3) // 16) * 16
    lines_n = band_rows * (TILE_COLS + 4)
    ct_lon = clon // TILE_COLS
    cw = 2 * ct_lon
    assert ct_lon == 128 and cin % 16 == 0 and band_rows == 2
    assert (cin // 16) * 2 * (blocks + 1) * TILE_COLS <= 128
    shape = jax.ShapeDtypeStruct
    return pl.pallas_call(
        first_kernel,
        out_shape=(
            shape((lines_n, cin + 16, 128), BF16),
            shape((8, 4 * nout, 128), BF16),
            shape((4 * nout, 128), BF16),
            shape((fl // 128, nout * (fr + 4), 128), F32),
            shape((blocks, 3 * cin, 3 * cin), BF16),
            shape((2 * blocks, cin, 128), F32),
            shape((ch, 3 * slab), BF16),
            shape((ch, 128), F32),
            shape((ch, 9 * ch + 16), BF16),
            shape((cw, 3 * fl), BF16),
            shape((9, 128, 128), BF16),
            shape((cw, 128), BF16),
        ),
        in_specs=[hbm] * 10,
        out_specs=(vmem,) * 12,
        scratch_shapes=[
            pltpu.VMEM((cin, band_rows, clon), BF16),
            pltpu.VMEM((TILE_COLS, band_rows, cin + 16, 128), BF16),
            pltpu.VMEM((nout, fr, fl), BF16),
            pltpu.VMEM((4 * nout, fl), BF16),
            pltpu.VMEM((2, 4 * nout, fl), BF16),
            pltpu.VMEM(gain.shape, F32),
            pltpu.VMEM(regb.shape, F32),
            pltpu.VMEM((3, 1, ch), F32),
            pltpu.VMEM(regs.shape, BF16),
            pltpu.VMEM(lifts.shape, BF16),
            pltpu.VMEM(mids.shape, BF16),
            pltpu.VMEM((3 * slab, ch), BF16),
            dma((2 * TILE_COLS,)), dma((8,)), dma((10,)), dma((10,)), dma((11,)),
        ],
        compiler_params=pltpu.CompilerParams(
            collective_id=0, has_side_effects=True, vmem_limit_bytes=20_000_000),
    )(*[pltpu.with_memory_space_constraint(x, pltpu.HBM) for x in (
        coarse, noisy, gain, regb, regs, liftb, midg, midb, lifts, mids)])


def tile_kernel(
    dims, got, got_cols, own_cols, grid, regw, regc, liftw, gains, midw, lon, sidew, chosen, out,
    held, part, field, lines, upper, sides, bands, unit, raw, prod, edges, rows_out, stage, sems,
):
    cin, ch, nout, fr, fl = dims
    lines_n, count, cw = got.shape[0], field.shape[0], field.shape[2]
    blocks = regw.shape[0]
    halo = blocks + 1
    span = 2 * halo * TILE_COLS
    me = lax.axis_index("lat")
    tile_row, tile_rows = me // TILE_COLS, lax.axis_size("lat") // TILE_COLS
    c = me % TILE_COLS
    after_seam = (c + 1) % TILE_COLS
    top, bottom = tile_row == 0, tile_row == tile_rows - 1
    steps = bands.shape[0]
    wide = fl // 128
    lane = lax.broadcasted_iota(jnp.int32, (1, 128), 1)
    lane_first, lane_last = lane == 0, lane == 127
    spare = lines_n // 4

    def known(i, values):
        if i < spare:
            return jnp.where(top, 0.0, values)
        if i >= lines_n - spare:
            return jnp.where(bottom, 0.0, values)
        return values

    def spread(k, i, values):
        values = activate(values, regc[2 * k][:, :1])
        taps = jnp.concatenate(
            [pltpu.roll(values, 1, 1).astype(BF16), values.astype(BF16), pltpu.roll(values, cw - 1, 1).astype(BF16)],
            axis=0)
        part[k % 2, i] = jnp.dot(regw[k], taps, preferred_element_type=F32)

    def enter(i):
        side = got[i, cin:, :].astype(F32)
        outer = []
        for g in range(cin // 16):
            after = pltpu.roll(side, 128 - halo - g * span - 2 * halo * after_seam, 1)
            before = pltpu.roll(side, 128 - halo - g * span - 2 * halo * c, 1)
            outer.append(jnp.where(lane < halo, after, jnp.where(lane >= 128 - halo, before, 0.0)))
        values = jnp.concatenate([got[i, :cin, :].astype(F32), jnp.concatenate(outer, axis=0)], axis=1)
        values = known(i, values)
        held[i] = values
        spread(0, i, values)

    def update(k, i):
        values = held[i] + part[k % 2, i - 1, :cin, :] + part[k % 2, i, cin:2 * cin, :] + part[k % 2, i + 1, 2 * cin:, :]
        values = (values + regc[2 * k + 1][:, :1]).astype(BF16)
        return known(i, values.astype(F32))

    def follow(k, i):
        values = update(k - 1, i)
        held[i] = values
        spread(k, i, values)

    def widen(first, last):
        coarse = field[first:last].reshape((last - first) * cin, cw)
        for q in range(3):
            lines[first:last, q * cin:(q + 1) * cin, :] = jnp.dot(
                coarse, lon[:, q * fl:(q + 1) * fl], preferred_element_type=F32).reshape(last - first, cin, fl)

    def blend(t):
        return lat_split(t, top, bottom, count, tile_row * fr, fr * tile_rows)

    def inside(t):
        row = tile_row * fr + t - 2
        return jnp.logical_and(row >= 0, row < fr * tile_rows)

    tall = fr + 4
    slab = upper.shape[1]

    def along(middle, above, below):
        above = jnp.where(top, 0.0, pltpu.roll(above.astype(F32), 128 - (fr - 2), 1))
        below = jnp.where(bottom, 0.0, pltpu.roll(below.astype(F32), fr + 2, 1))
        middle = pltpu.roll(middle.astype(F32), 2, 1)
        return jnp.where(lane < 2, above, jnp.where(lane < fr + 2, middle, below))

    west = along(got_cols[0], got_cols[2], got_cols[4])
    east = along(got_cols[1], got_cols[3], got_cols[5])
    here = along(own_cols[...], got_cols[6], got_cols[7])
    none = jnp.ones((slab - 3 * (cin + nout), 128), F32)
    left_cols = jnp.concatenate([west[2 * nout:], here[:nout], none], axis=0)
    right_cols = jnp.concatenate([here[3 * nout:], east[:2 * nout], none], axis=0)
    west_col, east_col = west[3 * nout:], east[:nout]

    def noise_rows(t):
        rows = [grid[j, pl.ds(t, nout, stride=tall), :] for j in range(wide)]
        onward = [pltpu.roll(v, 1, 1) for v in rows]
        back = [pltpu.roll(v, 127, 1) for v in rows]
        edge_l = pltpu.roll(west_col, (128 - t) % 128 if isinstance(t, int) else 128 - t, 1)
        edge_r = pltpu.roll(east_col, 127 - t, 1)
        pieces = []
        for j in range(wide):
            lo = jnp.where(lane_first, onward[j - 1] if j else edge_l, onward[j])
            hi = jnp.where(lane_last, back[j + 1] if j < wide - 1 else edge_r, back[j])
            pieces.append(jnp.concatenate([lo, rows[j], hi, none], axis=0))
        return jnp.concatenate(pieces, axis=1).astype(BF16)

    def raise_row(t, slot):
        a, b, share, ok = blend(jnp.int32(t))
        wa = jnp.where(ok, 1.0 - share, 0.0)
        wb = jnp.where(ok, share, 0.0)
        for o in range(0, 3 * cin, 16):
            upper[slot, o:o + 16, :] = (wa * lines[a, o:o + 16, :] + wb * lines[b, o:o + 16, :]).astype(BF16)
        upper[slot, 3 * cin:slab, :] = noise_rows(t)

    edge_row = jnp.where(lane < HALF, lane, lane - HALF)

    found = {}

    def edge_pick():
        found["narrow"] = jnp.dot(field[...].reshape(count * cin, cw), chosen[...], preferred_element_type=F32)

    def edge_pack():
        packed = found["narrow"][:cin]
        for i in range(1, count):
            packed = packed + pltpu.roll(found["narrow"][i * cin:(i + 1) * cin], 4 * i, 1)
        found["packed"] = packed.astype(BF16)

    def edge_blend(p):
        for q in range(3):
            base = p * slab + q * cin
            sides[base:base + cin, :] = jnp.dot(
                found["packed"], sidew[3 * p + q], preferred_element_type=F32).astype(BF16)
        sides[p * slab + 3 * cin:(p + 1) * slab, :] = jnp.where(
            lane < HALF, pltpu.roll(left_cols, (128 - p) % 128, 1), pltpu.roll(right_cols, HALF - p, 1)).astype(BF16)

    def edge_lift():
        found["lift"] = jnp.dot(liftw[...], sides[...], preferred_element_type=F32)

    def edge_finish():
        edges[...] = jnp.where(inside(edge_row + 1), activate(found["lift"], gains[...]), 0.0).astype(BF16)

    def lift(slot, target):
        window = jnp.concatenate([upper[(slot + n) % steps] for n in range(3)], axis=0)
        raw[target % steps] = jnp.dot(liftw[...], window, preferred_element_type=F32)

    def finish(l, slot):
        squares = jnp.zeros((8, fl), F32)
        for o in range(0, ch, 16):
            values = raw[slot, o:o + 16, :]
            values = values * values
            squares = squares + (values[:8] + values[8:])
        inverse = lax.rsqrt(jnp.sum(squares, axis=0, keepdims=True) * (1.0 / ch) + EPSILON)
        inverse = jnp.where(inside(l + 1), inverse, 0.0)
        for o in range(0, ch, 16):
            half_gain = jnp.concatenate([gains[o:o + 16, :]] * wide, axis=1)
            half = raw[slot, o:o + 16, :] * inverse * half_gain
            values = (half + half * jnp.tanh(half)).astype(BF16)
            edge = edges[o:o + 16, :]
            parts = [values[:, j * 128:(j + 1) * 128] for j in range(wide)]
            onward = [pltpu.roll(v, 1, 1) for v in parts]
            back = [pltpu.roll(v, 127, 1) for v in parts]
            edge_l = pltpu.roll(edge, 128 - l, 1)
            edge_r = pltpu.roll(edge, 128 + HALF - 1 - l, 1)
            bands[slot, ch + o:ch + o + 16, :] = values
            bands[slot, o:o + 16, :] = jnp.concatenate(
                [jnp.where(lane_first, onward[j - 1] if j else edge_l, onward[j]) for j in range(wide)], axis=1)
            bands[slot, 2 * ch + o:2 * ch + o + 16, :] = jnp.concatenate(
                [jnp.where(lane_last, back[j + 1] if j < wide - 1 else edge_r, back[j]) for j in range(wide)], axis=1)

    def mid(slot):
        window = jnp.concatenate([bands[(slot + n) % steps] for n in range(3)] + [unit[...]], axis=0)
        prod[slot % 2] = jnp.dot(midw[...], window, preferred_element_type=F32)

    group = stage.shape[2]
    blocks_out = ch // 8

    def flushed(n):
        return pltpu.make_async_copy(
            stage.at[n % 2], out.at[0, :, pl.ds(pl.multiple_of(n * group, group), group), :], sems.at[n % 2])

    def shrink(n, o):
        for j in range(wide):
            block = rows_out[n % 2, j, pl.ds(pl.multiple_of(o * 8 * group, 8 * group), 8 * group), :]
            stage[n % 2, pl.ds(o * 8, 8), :, j * 128:(j + 1) * 128] = block.reshape(8, group, 128).astype(BF16)

    def emit(n, spot, slot):
        for o in range(0, ch, 16):
            for j in range(wide):
                at = slice(j * 128, (j + 1) * 128)
                total = raw[(slot + 1) % steps, o:o + 16, at] + prod[slot % 2, o:o + 16, at]
                rows_out[n % 2, j, pl.ds(spot + o * group, 16, stride=group), :] = total

    unit[...] = jnp.ones(unit.shape, BF16)

    def raised(t):
        raise_row(t, t % steps)

    def lifted(l):
        lift(l % steps, l)

    def finished(l):
        finish(jnp.int32(l), l % steps)

    def settle(row):
        field[row - halo] = update(blocks - 1, row).astype(BF16)

    plan = []
    lag = 3
    for i in range(1, lines_n - 1 + lag * blocks):
        if i < lines_n - 1:
            plan.append((enter, i))
        for k in range(1, blocks):
            row = i - lag * k
            if 1 + k <= row < lines_n - 1 - k:
                plan.append((functools.partial(follow, k), row))
        row = i - lag * blocks
        if halo <= row < lines_n - halo:
            plan.append((settle, row))
            line = row - halo
            if line % 2:
                plan.append((lambda n: widen(n - 1, n + 1), line))
            elif line == count - 1:
                plan.append((lambda n: widen(n, n + 1), line))
    plan += [(lambda _: edge_pick(), 0), (raised, 0), (raised, 1), (lambda _: edge_pack(), 0), (raised, 2),
             (lifted, 0), (raised, 3), (edge_blend, 0), (edge_blend, 1), (edge_blend, 2), (raised, 4), (lifted, 1), (raised, 5),
             (lambda _: edge_lift(), 0), (lifted, 2), (raised, 6), (lambda _: edge_finish(), 0), (lifted, 3), (finished, 0),
             (raised, 7), (finished, 1), (lifted, 4), (finished, 2), (mid, 0), (finished, 3)]
    for action, n in plan:
        action(n)

    halves = group // steps
    share_out = blocks_out // group

    def step(i, u, e, last):
        n = i // halves
        shrink_at = (i % halves) * (blocks_out // halves) + u * share_out
        for o in range(share_out):
            shrink(n + 1, shrink_at + o)
        emit(n, (i % halves) * steps + u, u)
        if last is None or last + 1 < fr:
            mid((u + 1) % steps)
        if last is None or last + 4 < fr + 2:
            finish(e + 4, (u + 4) % steps)
        if last is None or last + 5 < fr + 2:
            lift((u + 5) % steps, u + 5)
        if last is None:
            raise_row(e + 8, u)

    trips = fr // steps

    def begin(i):
        @pl.when(jnp.logical_and(i % halves == 0, i >= 3 * halves))
        def _():
            flushed(i // halves - 3).wait()

    def finish_trip(i):
        @pl.when(jnp.logical_and(i % halves == halves - 1, i >= halves))
        def _():
            flushed(i // halves - 1).start()

    def trip(i, _):
        begin(i)
        for u in range(steps):
            step(i, u, i * steps + u, None)
        finish_trip(i)
        return 0

    lax.fori_loop(0, trips - 1, trip, 0)
    i = jnp.int32(trips - 1)
    begin(i)
    for u in range(steps):
        step(i, u, i * steps + u, fr - steps + u)
    finish_trip(i)
    groups = fr // group
    if groups >= 3:
        flushed(groups - 3).wait()
    for o in range(blocks_out):
        shrink(groups - 1, o)
    flushed(groups - 1).start()
    for n in range(max(groups - 2, 0), groups):
        flushed(n).wait()


def tile_program(dims, prepared):
    cin, ch, nout, fr, fl = dims
    got, lon, liftw = prepared[0], prepared[9], prepared[6]
    lines_n = got.shape[0]
    cw = lon.shape[0]
    blocks = prepared[4].shape[0]
    count = lines_n - 2 * (blocks + 1)
    group = 8
    steps = 4
    vmem = pl.BlockSpec(memory_space=pltpu.VMEM)
    slab = liftw.shape[1] // 3
    return pl.pallas_call(
        functools.partial(tile_kernel, dims),
        out_shape=jax.ShapeDtypeStruct((1, ch, fr, fl), BF16),
        in_specs=[vmem] * len(prepared),
        out_specs=pl.BlockSpec(memory_space=pl.ANY),
        scratch_shapes=[
            pltpu.VMEM((lines_n, cin, cw), F32),
            pltpu.VMEM((2, lines_n, 3 * cin, cw), F32),
            pltpu.VMEM((count, cin, cw), BF16),
            pltpu.VMEM((count, 3 * cin, fl), F32),
            pltpu.VMEM((steps, slab, fl), BF16),
            pltpu.VMEM((3 * slab, 128), BF16),
            pltpu.VMEM((steps, 3 * ch, fl), BF16),
            pltpu.VMEM((16, fl), BF16),
            pltpu.VMEM((steps, ch, fl), F32),
            pltpu.VMEM((2, ch, fl), F32),
            pltpu.VMEM((ch, 128), BF16),
            pltpu.VMEM((2, fl // 128, ch * group, 128), F32),
            pltpu.VMEM((2, ch, group, fl), BF16),
            pltpu.SemaphoreType.DMA((2,)),
        ],
        compiler_params=pltpu.CompilerParams(vmem_limit_bytes=44_000_000),
    )(*prepared)


def per_device(
    coarse, reg_gain, reg_weight, reg_bias, noisy, lift_weight, lift_bias, mid_gain, mid_weight, mid_bias,
):
    lifts = lift_weight.transpose(0, 1, 3, 2)
    prepared = first_program(
        coarse, noisy, reg_gain, reg_bias, reg_weight.reshape((-1,) + reg_weight.shape[3:]),
        lift_bias[None], mid_gain[None], mid_bias[None],
        lifts.reshape((9,) + lifts.shape[2:]), mid_weight.reshape((9,) + mid_weight.shape[2:]))
    return tile_program((coarse.shape[0], mid_weight.shape[2]) + noisy.shape[1:], prepared)


def solution(mesh):
    placed = (
        P(None, ("grp", "lat"), None),
        P(),
        P(),
        P(),
        P(("grp", "lat"), None, None, None),
        P(),
        P(),
        P(),
        P(),
        P(),
    )
    return jax.shard_map(
        per_device,
        mesh=mesh,
        in_specs=placed,
        out_specs=P(("grp", "lat"), None, None, None),
        check_vma=False,
    )
```

```python
import functools

import jax
import jax.numpy as jnp
from jax import lax
from jax.experimental import pallas as pl
from jax.experimental.pallas import tpu as pltpu
from jax.sharding import PartitionSpec as P

TILE_COLS = 4
LAT_UP = 4
LON_UP = 4
EPSILON = 1e-06
F32 = jnp.float32
BF16 = jnp.bfloat16
MESH = pl.DeviceIdType.MESH
HALF = 64


def activate(values, half_gain):
    inverse = lax.rsqrt(jnp.mean(values * values, axis=0, keepdims=True) + EPSILON)
    half = values * inverse * half_gain
    return half + half * jnp.tanh(half)


def split(numerator, factor):
    lower = numerator // (2 * factor)
    return lower, (numerator - 2 * factor * lower).astype(F32) / (2.0 * factor)


def column(row):
    n = row.shape[1]
    here = lax.broadcasted_iota(jnp.int32, (n, n), 0) == lax.broadcasted_iota(jnp.int32, (n, n), 1)
    return jnp.broadcast_to(jnp.sum(jnp.where(here, row, 0.0), axis=1, keepdims=True), (n, 128))


def thirds(values):
    high = values.astype(BF16).astype(F32)
    middle = (values - high).astype(BF16).astype(F32)
    return [high, middle, values - high - middle]


def nt_dot(a, b):
    return lax.dot_general(a, b, (((1,), (1,)), ((), ())), preferred_element_type=F32)


def lon_split(fine_col):
    lower, part = split(2 * fine_col + 1 - LON_UP + 2 * LON_UP, LON_UP)
    return lower - 1, part


def lat_split(t, top, bottom, count, start, total):
    lower, part = split(2 * (t - 2) + 1 - LAT_UP + 2 * LAT_UP, LAT_UP)
    low_line = jnp.where(top, 1, 0)
    high_line = jnp.where(bottom, count - 2, count - 1)
    row = start + t - 2
    ok = jnp.logical_and(row >= 0, row < total)
    return jnp.clip(lower, low_line, high_line), jnp.clip(lower + 1, low_line, high_line), part, ok


def gather_row(got, i, c, halo):
    cin = got.shape[1] - 16
    lane = lax.broadcasted_iota(jnp.int32, (1, 128), 1)
    span = 2 * halo * TILE_COLS
    side = got[i, cin:, :].astype(F32)
    outer = []
    for g in range(cin // 16):
        after = pltpu.roll(side, 128 - halo - g * span - 2 * halo * ((c + 1) % TILE_COLS), 1)
        before = pltpu.roll(side, 128 - halo - g * span - 2 * halo * c, 1)
        outer.append(jnp.where(lane < halo, after, jnp.where(lane >= 128 - halo, before, 0.0)))
    return jnp.concatenate([got[i, :cin, :].astype(F32), jnp.concatenate(outer, axis=0)], axis=1)


def convolve(values, half_gain, weight):
    cw = values.shape[1]
    values = activate(values, half_gain[:, :1])
    taps = jnp.concatenate(
        [pltpu.roll(values, 1, 1).astype(BF16), values.astype(BF16), pltpu.roll(values, cw - 1, 1).astype(BF16)],
        axis=0)
    return jnp.dot(weight, taps, preferred_element_type=F32)


def add_rows(values, above, here, below, bias):
    cin = values.shape[0]
    return (values + above[:cin] + here[cin:2 * cin] + below[2 * cin:] + bias[:, :1]).astype(BF16)


def first_kernel(
    coarse, noisy, gain, regb, regs, liftb, midg, midb, lifts, mids,
    got, got_cols, cols, grid, regw, regc, liftw, liftc, midw, lon, sidew, chosen, held, part, field,
    band, pieces, tile, rows, far_rows, gainv, regbv, vecs, regv, liftv, midv, liftt,
    send, recv, nsend, nrecv, local,
):
    me = lax.axis_index("lat")
    tile_rows = lax.axis_size("lat") // TILE_COLS
    r = me // TILE_COLS
    c = me % TILE_COLS
    north, south = r > 0, r < tile_rows - 1
    top, bottom = r == 0, r == tile_rows - 1
    cin, band_rows, clon = band.shape
    ch = midv.shape[1]
    nout, fr, fl = tile.shape
    blocks = regw.shape[0]
    halo = blocks + 1
    span = 2 * halo * TILE_COLS
    cw = chosen.shape[0]
    count = got.shape[0] - 2 * halo

    barrier = pltpu.get_barrier_semaphore()

    def greet(target):
        pl.semaphore_signal(barrier, inc=1, device_id={"lat": target}, device_id_type=MESH)

    for k in range(1, TILE_COLS):
        greet(r * TILE_COLS + (c + k) % TILE_COLS)

    @pl.when(north)
    def _():
        for k in range(TILE_COLS):
            greet((r - 1) * TILE_COLS + k)

    @pl.when(south)
    def _():
        for k in range(TILE_COLS):
            greet((r + 1) * TILE_COLS + k)

    loads = [
        pltpu.make_async_copy(coarse, band, local.at[0]),
        pltpu.make_async_copy(noisy.at[0], tile, local.at[1]),
        pltpu.make_async_copy(regs, regv, local.at[2]),
        pltpu.make_async_copy(mids, midv, local.at[3]),
        pltpu.make_async_copy(lifts, liftv, local.at[4]),
        pltpu.make_async_copy(gain, gainv, local.at[6]),
        pltpu.make_async_copy(regb, regbv, local.at[7]),
        pltpu.make_async_copy(liftb, vecs.at[0], local.at[8]),
        pltpu.make_async_copy(midg, vecs.at[1], local.at[9]),
        pltpu.make_async_copy(midb, vecs.at[2], local.at[10]),
    ]
    for load in loads:
        load.start()

    lane = lax.broadcasted_iota(jnp.int32, (1, 128), 1)
    both = band_rows * cin
    row_id = lax.broadcasted_iota(jnp.int32, (both, both), 0)
    sub_id = jnp.where(row_id >= cin, 1, 0)
    order = lax.broadcasted_iota(jnp.int32, (both, both), 1) == band_rows * (row_id - sub_id * cin) + sub_id
    order = jnp.where(order, 1.0, 0.0).astype(BF16)
    loads[0].wait()
    sorted_rows = jnp.dot(order, band[...].reshape(both, clon), preferred_element_type=F32)
    for sub in range(band_rows):
        row = sorted_rows[sub * cin:(sub + 1) * cin]
        parts = [row[:, b * 128:(b + 1) * 128] for b in range(TILE_COLS)]
        for b in range(TILE_COLS):
            pieces[b, sub, :cin, :] = parts[b].astype(BF16)
        side = jnp.zeros((16, 128), F32)
        for b in range(TILE_COLS):
            seam = jnp.where(lane < 64, parts[b], parts[(b + TILE_COLS - 1) % TILE_COLS])
            for g in range(cin // 16):
                at = g * span + 2 * halo * b
                moved = pltpu.roll(seam[g * 16:(g + 1) * 16], at + halo, 1)
                side = jnp.where(jnp.logical_and(lane >= at, lane < at + 2 * halo), moved, side)
        for b in range(TILE_COLS):
            pieces[b, sub, cin:, :] = side.astype(BF16)

    loads[1].wait()
    ends = []
    for n in range(nout):
        ends += [tile[n, :2, :].astype(F32), tile[n, fr - 2:, :].astype(F32)]
    rows[...] = jnp.concatenate(ends, axis=0).astype(BF16)
    pick_row = lax.broadcasted_iota(jnp.int32, (4 * nout, 128), 0)
    pick_lane = lax.broadcasted_iota(jnp.int32, (4 * nout, 128), 1)
    packed = jnp.zeros((4 * nout, fr), F32)
    for n in range(nout):
        for s, (lo, at) in enumerate(((0, 0), (0, 1), (fl - 128, 126), (fl - 128, 127))):
            if s % 2 == 0:
                hit = jnp.zeros(pick_row.shape, jnp.bool_)
            hit = jnp.logical_or(hit, jnp.logical_and(pick_row == s * nout + n, pick_lane == at))
            if s % 2:
                packed = packed + nt_dot(jnp.where(hit, 1.0, 0.0).astype(BF16), tile[n, :, lo:lo + 128])
    cols[...] = jnp.concatenate([packed, jnp.zeros((4 * nout, 128 - fr), F32)], axis=1).astype(BF16)

    peers = TILE_COLS - 1 + jnp.where(north, TILE_COLS, 0) + jnp.where(south, TILE_COLS, 0)
    pl.semaphore_wait(barrier, peers)

    def remote(src, dst, ssem, rsem, target):
        return pltpu.make_async_remote_copy(
            src_ref=src, dst_ref=dst, send_sem=ssem, recv_sem=rsem,
            device_id={"lat": target}, device_id_type=MESH)

    whole, upper, lower = (0, 2), (0, 1), (1, 1)

    def landing(slot, span_rows):
        return got.at[pl.ds(2 * slot + span_rows[0], span_rows[1])]

    def far_first(k):
        return ((c // 2) * 2 + 2 + k) % TILE_COLS

    def beside():
        return c + 1 - 2 * (c % 2)

    def band_copy(k, row, slot, ssem, span_rows=whole):
        col = far_first(k)
        return remote(pieces.at[col, pl.ds(*span_rows)], landing(slot, span_rows), send.at[ssem], recv.at[slot],
                      row * TILE_COLS + col)

    west, east = (c + TILE_COLS - 1) % TILE_COLS, (c + 1) % TILE_COLS

    def col_copy(slot, row, col):
        return remote(cols, got_cols.at[slot], nsend.at[slot], nrecv.at[slot], row * TILE_COLS + col)

    def row_copy(slot, row):
        return remote(rows, far_rows.at[slot], nsend.at[8 + slot], nrecv.at[8 + slot], row * TILE_COLS + c)

    def each_band(action):
        for col, side, row, slot, span_rows in (
            (2, south, r + 1, 0, lower), (3, south, r + 1, 1, whole),
            (0, north, r - 1, 6, whole), (1, north, r - 1, 7, upper),
        ):
            @pl.when(jnp.logical_and(side, c == col))
            def _():
                for k in range(TILE_COLS):
                    action(band_copy(k, row, slot, TILE_COLS + k, span_rows))

        for k in range(TILE_COLS - 2):
            action(band_copy(k, r, 2 + c, k))
        action(remote(pieces.at[beside(), pl.ds(0, 2)], landing(2 + c, whole), send.at[2], recv.at[2 + c],
                      r * TILE_COLS + beside()))

    def each_edge(action):
        action(col_copy(0, r, east))
        action(col_copy(1, r, west))

        @pl.when(south)
        def _():
            action(row_copy(0, r + 1))
            action(col_copy(6, r + 1, c))
            action(col_copy(2, r + 1, east))
            action(col_copy(3, r + 1, west))

        @pl.when(north)
        def _():
            action(row_copy(1, r - 1))
            action(col_copy(7, r - 1, c))
            action(col_copy(4, r - 1, east))
            action(col_copy(5, r - 1, west))

    each_band(lambda copy: copy.start())
    own = pltpu.make_async_copy(pieces.at[c], landing(2 + c, whole), local.at[5])
    own.start()

    loads[2].wait()
    for k in range(blocks):
        for p in range(3):
            for q in range(3):
                regw[k, p * cin:(p + 1) * cin, q * cin:(q + 1) * cin] = regv[9 * k + 3 * p + q]
    each_edge(lambda copy: copy.start())

    loads[3].wait()
    for tap in range(9):
        midw[:, tap * ch:(tap + 1) * ch] = midv[tap]
    for load in loads[4:]:
        load.wait()
    slab = liftt.shape[0] // 3
    for p in range(3):
        noise = []
        for q in range(3):
            base = p * slab + q * cin
            liftt[base:base + cin, :] = liftv[3 * p + q, :cin, :]
            noise.append(liftv[3 * p + q, cin:, :].astype(F32))
        spare_rows = slab - 3 * (cin + nout)
        if p == 1:
            noise += thirds(vecs[0]) + [jnp.zeros((spare_rows - 3, ch), F32)]
        else:
            noise.append(jnp.zeros((spare_rows, ch), F32))
        liftt[p * slab + 3 * cin:(p + 1) * slab, :] = jnp.concatenate(noise, axis=0).astype(BF16)
    eye = jnp.where(lax.broadcasted_iota(jnp.int32, (ch, ch), 0) == lax.broadcasted_iota(jnp.int32, (ch, ch), 1), 1.0, 0.0)
    liftw[...] = nt_dot(eye.astype(BF16), liftt[...]).astype(BF16)

    position = lax.broadcasted_iota(jnp.int32, (1, 3 * fl), 1)
    shift = jnp.where(position >= 2 * fl, 2, jnp.where(position >= fl, 1, 0))
    low, weight = lon_split(position - shift * fl + shift - 1)
    low_lane = jnp.where(low < 0, low + cw, low)
    high_lane = jnp.where(low + 1 < 0, low + 1 + cw, low + 1)
    coarse_lane = lax.broadcasted_iota(jnp.int32, (cw, 3 * fl), 0)
    lon[...] = jnp.where(coarse_lane == low_lane, 1.0 - weight,
                         jnp.where(coarse_lane == high_lane, weight, 0.0)).astype(BF16)

    for k in range(blocks):
        regc[2 * k] = column(gainv[k:k + 1, :]) * 0.5
        regc[2 * k + 1] = column(regbv[k:k + 1, :])
    liftc[...] = column(vecs[1]) * 0.5
    bias_cols = jnp.zeros((ch, 128), F32)
    for n, third in enumerate(thirds(column(vecs[2]))):
        bias_cols = jnp.where(lane == n, third, bias_cols)
    midw[:, 9 * ch:] = bias_cols[:, :16].astype(BF16)

    tall = fr + 4
    wide = fl // 128
    for n in range(nout):
        for j in range(wide):
            grid[j, n * tall + 2:n * tall + 2 + fr, :] = tile[n, :, j * 128:(j + 1) * 128].astype(F32)

    near = fl // LON_UP
    picked_cols = [-1, 0, near - 1, near]
    select_lane = lax.broadcasted_iota(jnp.int32, (cw, 128), 0)
    select_pos = lax.broadcasted_iota(jnp.int32, (cw, 128), 1)
    hits = jnp.zeros((cw, 128), jnp.bool_)
    for s, col in enumerate(picked_cols):
        hits = jnp.logical_or(hits, jnp.logical_and(select_pos == s, select_lane == col % cw))
    chosen[...] = jnp.where(hits, 1.0, 0.0).astype(BF16)
    key = lax.broadcasted_iota(jnp.int32, (128, 1), 0)
    key_line = key // 4
    key_pick = key - 4 * key_line
    key_col = jnp.where(key_pick == 0, picked_cols[0], jnp.where(
        key_pick == 1, picked_cols[1], jnp.where(key_pick == 2, picked_cols[2], picked_cols[3])))
    edge_row = jnp.where(lane < HALF, lane, lane - HALF)
    for p in range(3):
        a, b, share, ok = lat_split(edge_row + p, top, bottom, count, r * fr, fr * tile_rows)
        wa = jnp.where(ok, 1.0 - share, 0.0)
        wb = jnp.where(ok, share, 0.0)
        by_row = jnp.where(key_line == a, wa, 0.0) + jnp.where(key_line == b, wb, 0.0)
        for q in range(3):
            lower_col, share_m = lon_split(jnp.where(lane < HALF, q - 2, fl - 1 + q))
            by_col = jnp.where(key_col == lower_col, 1.0 - share_m, jnp.where(key_col == lower_col + 1, share_m, 0.0))
            sidew[3 * p + q] = (by_row * by_col).astype(BF16)

    own.wait()

    def arrived(slot, span_rows=whole):
        remote(pieces.at[0, pl.ds(*span_rows)], landing(slot, span_rows), send.at[0], recv.at[slot], me).wait_recv()

    def edge(slot):
        if slot < 8:
            remote(cols, got_cols.at[slot], nsend.at[slot], nrecv.at[slot], me).wait_recv()
        else:
            remote(rows, far_rows.at[slot - 8], nsend.at[slot], nrecv.at[slot], me).wait_recv()

    for k in range(1, TILE_COLS):
        arrived(2 + (c + k) % TILE_COLS)

    spare = got.shape[0] // 4
    inner = got.shape[0] - 2 * spare

    def enter(i):
        values = gather_row(got, spare + i, c, halo)
        held[i] = values
        part[0, i] = convolve(values, regc[0], regw[0])

    def update(k, i):
        return add_rows(held[i], part[k, i - 1], part[k, i], part[k, i + 1], regc[2 * k + 1])

    def follow(k, i):
        values = update(k - 1, i).astype(F32)
        held[i] = values
        part[k, i] = convolve(values, regc[2 * k], regw[k])

    lag = 3
    for i in range(inner + lag * blocks):
        if i < inner:
            enter(i)
        for k in range(1, blocks):
            if k <= i - lag * k < inner - k:
                follow(k, i - lag * k)
        row = i - lag * blocks
        if blocks <= row < inner - blocks:
            field[row - blocks] = update(blocks - 1, row)

    @pl.when(north)
    def _():
        arrived(0, lower)
        arrived(1)

    @pl.when(south)
    def _():
        arrived(6)
        arrived(7, upper)

    edge(0)
    edge(1)

    @pl.when(north)
    def _():
        for slot in (2, 3, 6, 8):
            edge(slot)

    @pl.when(south)
    def _():
        for slot in (4, 5, 7, 9):
            edge(slot)

    for n in range(nout):
        for j in range(wide):
            at = slice(j * 128, (j + 1) * 128)
            above = far_rows[0, :, at].astype(F32)[4 * n + 2:4 * n + 4]
            below = far_rows[1, :, at].astype(F32)[4 * n:4 * n + 2]
            grid[j, n * tall:n * tall + 2, :] = jnp.where(top, 0.0, above)
            grid[j, n * tall + 2 + fr:(n + 1) * tall, :] = jnp.where(bottom, 0.0, below)

    each_band(lambda copy: copy.wait_send())
    each_edge(lambda copy: copy.wait_send())


def first_program(coarse, noisy, gain, regb, regs, liftb, midg, midb, lifts, mids):
    hbm = pl.BlockSpec(memory_space=pltpu.HBM)
    vmem = pl.BlockSpec(memory_space=pltpu.VMEM)
    dma = pltpu.SemaphoreType.DMA
    cin, band_rows, clon = coarse.shape
    nout, fr, fl = noisy.shape[1:]
    ch = mids.shape[1]
    blocks = regs.shape[0] // 9
    slab = 3 * cin + -(-(3 * nout + 3) // 16) * 16
    lines_n = band_rows * (TILE_COLS + 4)
    ct_lon = clon // TILE_COLS
    cw = 2 * ct_lon
    assert ct_lon == 128 and cin % 16 == 0 and band_rows == 2
    assert (cin // 16) * 2 * (blocks + 1) * TILE_COLS <= 128
    shape = jax.ShapeDtypeStruct
    return pl.pallas_call(
        first_kernel,
        out_shape=(
            shape((lines_n, cin + 16, 128), BF16),
            shape((8, 4 * nout, 128), BF16),
            shape((4 * nout, 128), BF16),
            shape((fl // 128, nout * (fr + 4), 128), F32),
            shape((blocks, 3 * cin, 3 * cin), BF16),
            shape((2 * blocks, cin, 128), F32),
            shape((ch, 3 * slab), BF16),
            shape((ch, 128), F32),
            shape((ch, 9 * ch + 16), BF16),
            shape((cw, 3 * fl), BF16),
            shape((9, 128, 128), BF16),
            shape((cw, 128), BF16),
            shape((lines_n - 2 * (lines_n // 4), cin, cw), F32),
            shape((blocks, lines_n - 2 * (lines_n // 4), 3 * cin, cw), F32),
            shape((lines_n - 2 * (lines_n // 4) - 2 * blocks, cin, cw), BF16),
        ),
        in_specs=[hbm] * 10,
        out_specs=(vmem,) * 15,
        scratch_shapes=[
            pltpu.VMEM((cin, band_rows, clon), BF16),
            pltpu.VMEM((TILE_COLS, band_rows, cin + 16, 128), BF16),
            pltpu.VMEM((nout, fr, fl), BF16),
            pltpu.VMEM((4 * nout, fl), BF16),
            pltpu.VMEM((2, 4 * nout, fl), BF16),
            pltpu.VMEM(gain.shape, F32),
            pltpu.VMEM(regb.shape, F32),
            pltpu.VMEM((3, 1, ch), F32),
            pltpu.VMEM(regs.shape, BF16),
            pltpu.VMEM(lifts.shape, BF16),
            pltpu.VMEM(mids.shape, BF16),
            pltpu.VMEM((3 * slab, ch), BF16),
            dma((2 * TILE_COLS,)), dma((8,)), dma((10,)), dma((10,)), dma((11,)),
        ],
        compiler_params=pltpu.CompilerParams(
            collective_id=0, has_side_effects=True, vmem_limit_bytes=24_000_000),
    )(*[pltpu.with_memory_space_constraint(x, pltpu.HBM) for x in (
        coarse, noisy, gain, regb, regs, liftb, midg, midb, lifts, mids)])


def tile_kernel(
    dims, got, got_cols, own_cols, grid, regw, regc, liftw, gains, midw, lon, sidew, chosen, held_in, part_in, field_in, out,
    held, part, field, lines, upper, sides, bands, unit, raw, prod, edges, rows_out, stage, sems,
):
    cin, ch, nout, fr, fl = dims
    lines_n, count, cw = got.shape[0], field.shape[0], field.shape[2]
    blocks = regw.shape[0]
    halo = blocks + 1
    me = lax.axis_index("lat")
    tile_row, tile_rows = me // TILE_COLS, lax.axis_size("lat") // TILE_COLS
    c = me % TILE_COLS
    top, bottom = tile_row == 0, tile_row == tile_rows - 1
    steps = bands.shape[0]
    wide = fl // 128
    lane = lax.broadcasted_iota(jnp.int32, (1, 128), 1)
    lane_first, lane_last = lane == 0, lane == 127
    spare = lines_n // 4

    def known(i, values):
        if i < spare:
            return jnp.where(top, 0.0, values)
        if i >= lines_n - spare:
            return jnp.where(bottom, 0.0, values)
        return values

    def ready(k, i):
        return spare + k <= i < lines_n - spare - k

    def product(k, i):
        return part_in[k, i - spare] if ready(k, i) else part[k % 2, i]

    def enter(i):
        values = known(i, gather_row(got, i, c, halo))
        held[i] = values
        part[0, i] = convolve(values, regc[0], regw[0])

    def update(k, i):
        values = held_in[i - spare] if ready(k, i) else held[i]
        values = add_rows(values, product(k, i - 1), product(k, i), product(k, i + 1), regc[2 * k + 1])
        return known(i, values.astype(F32))

    def follow(k, i):
        values = update(k - 1, i)
        held[i] = values
        part[k % 2, i] = convolve(values, regc[2 * k], regw[k])

    def widen(first, last):
        coarse = field[first:last].reshape((last - first) * cin, cw)
        for q in range(3):
            lines[first:last, q * cin:(q + 1) * cin, :] = jnp.dot(
                coarse, lon[:, q * fl:(q + 1) * fl], preferred_element_type=F32).reshape(last - first, cin, fl)

    def blend(t):
        return lat_split(t, top, bottom, count, tile_row * fr, fr * tile_rows)

    def inside(t):
        row = tile_row * fr + t - 2
        return jnp.logical_and(row >= 0, row < fr * tile_rows)

    tall = fr + 4
    slab = upper.shape[1]

    def along(middle, above, below):
        above = jnp.where(top, 0.0, pltpu.roll(above.astype(F32), 128 - (fr - 2), 1))
        below = jnp.where(bottom, 0.0, pltpu.roll(below.astype(F32), fr + 2, 1))
        middle = pltpu.roll(middle.astype(F32), 2, 1)
        return jnp.where(lane < 2, above, jnp.where(lane < fr + 2, middle, below))

    west = along(got_cols[0], got_cols[2], got_cols[4])
    east = along(got_cols[1], got_cols[3], got_cols[5])
    here = along(own_cols[...], got_cols[6], got_cols[7])
    none = jnp.ones((slab - 3 * (cin + nout), 128), F32)
    left_cols = jnp.concatenate([west[2 * nout:], here[:nout], none], axis=0)
    right_cols = jnp.concatenate([here[3 * nout:], east[:2 * nout], none], axis=0)
    west_col, east_col = west[3 * nout:], east[:nout]

    def noise_rows(t):
        rows = [grid[j, pl.ds(t, nout, stride=tall), :] for j in range(wide)]
        onward = [pltpu.roll(v, 1, 1) for v in rows]
        back = [pltpu.roll(v, 127, 1) for v in rows]
        edge_l = pltpu.roll(west_col, (128 - t) % 128 if isinstance(t, int) else 128 - t, 1)
        edge_r = pltpu.roll(east_col, 127 - t, 1)
        pieces = []
        for j in range(wide):
            lo = jnp.where(lane_first, onward[j - 1] if j else edge_l, onward[j])
            hi = jnp.where(lane_last, back[j + 1] if j < wide - 1 else edge_r, back[j])
            pieces.append(jnp.concatenate([lo, rows[j], hi, none], axis=0))
        return jnp.concatenate(pieces, axis=1).astype(BF16)

    def raise_row(t, slot):
        a, b, share, ok = blend(jnp.int32(t))
        wa = jnp.where(ok, 1.0 - share, 0.0)
        wb = jnp.where(ok, share, 0.0)
        for o in range(0, 3 * cin, 16):
            upper[slot, o:o + 16, :] = (wa * lines[a, o:o + 16, :] + wb * lines[b, o:o + 16, :]).astype(BF16)
        upper[slot, 3 * cin:slab, :] = noise_rows(t)

    edge_row = jnp.where(lane < HALF, lane, lane - HALF)

    found = {}

    def edge_pick():
        found["narrow"] = jnp.dot(field[...].reshape(count * cin, cw), chosen[...], preferred_element_type=F32)

    def edge_pack():
        packed = found["narrow"][:cin]
        for i in range(1, count):
            packed = packed + pltpu.roll(found["narrow"][i * cin:(i + 1) * cin], 4 * i, 1)
        found["packed"] = packed.astype(BF16)

    def edge_blend(p):
        for q in range(3):
            base = p * slab + q * cin
            sides[base:base + cin, :] = jnp.dot(
                found["packed"], sidew[3 * p + q], preferred_element_type=F32).astype(BF16)
        sides[p * slab + 3 * cin:(p + 1) * slab, :] = jnp.where(
            lane < HALF, pltpu.roll(left_cols, (128 - p) % 128, 1), pltpu.roll(right_cols, HALF - p, 1)).astype(BF16)

    def edge_lift():
        found["lift"] = jnp.dot(liftw[...], sides[...], preferred_element_type=F32)

    def edge_finish():
        edges[...] = jnp.where(inside(edge_row + 1), activate(found["lift"], gains[...]), 0.0).astype(BF16)

    def lift(slot, target):
        window = jnp.concatenate([upper[(slot + n) % steps] for n in range(3)], axis=0)
        raw[target % steps] = jnp.dot(liftw[...], window, preferred_element_type=F32)

    def finish(l, slot):
        squares = jnp.zeros((8, fl), F32)
        for o in range(0, ch, 16):
            values = raw[slot, o:o + 16, :]
            values = values * values
            squares = squares + (values[:8] + values[8:])
        inverse = lax.rsqrt(jnp.sum(squares, axis=0, keepdims=True) * (1.0 / ch) + EPSILON)
        inverse = jnp.where(inside(l + 1), inverse, 0.0)
        for o in range(0, ch, 16):
            half_gain = jnp.concatenate([gains[o:o + 16, :]] * wide, axis=1)
            half = raw[slot, o:o + 16, :] * inverse * half_gain
            values = (half + half * jnp.tanh(half)).astype(BF16)
            edge = edges[o:o + 16, :]
            parts = [values[:, j * 128:(j + 1) * 128] for j in range(wide)]
            onward = [pltpu.roll(v, 1, 1) for v in parts]
            back = [pltpu.roll(v, 127, 1) for v in parts]
            edge_l = pltpu.roll(edge, 128 - l, 1)
            edge_r = pltpu.roll(edge, 128 + HALF - 1 - l, 1)
            bands[slot, ch + o:ch + o + 16, :] = values
            bands[slot, o:o + 16, :] = jnp.concatenate(
                [jnp.where(lane_first, onward[j - 1] if j else edge_l, onward[j]) for j in range(wide)], axis=1)
            bands[slot, 2 * ch + o:2 * ch + o + 16, :] = jnp.concatenate(
                [jnp.where(lane_last, back[j + 1] if j < wide - 1 else edge_r, back[j]) for j in range(wide)], axis=1)

    def mid(slot):
        window = jnp.concatenate([bands[(slot + n) % steps] for n in range(3)] + [unit[...]], axis=0)
        prod[slot % 2] = jnp.dot(midw[...], window, preferred_element_type=F32)

    group = stage.shape[2]
    blocks_out = ch // 8

    def flushed(n):
        return pltpu.make_async_copy(
            stage.at[n % 2], out.at[0, :, pl.ds(pl.multiple_of(n * group, group), group), :], sems.at[n % 2])

    def shrink(n, o):
        for j in range(wide):
            block = rows_out[n % 2, j, pl.ds(pl.multiple_of(o * 8 * group, 8 * group), 8 * group), :]
            stage[n % 2, pl.ds(o * 8, 8), :, j * 128:(j + 1) * 128] = block.reshape(8, group, 128).astype(BF16)

    def emit(n, spot, slot):
        for o in range(0, ch, 16):
            for j in range(wide):
                at = slice(j * 128, (j + 1) * 128)
                total = raw[(slot + 1) % steps, o:o + 16, at] + prod[slot % 2, o:o + 16, at]
                rows_out[n % 2, j, pl.ds(spot + o * group, 16, stride=group), :] = total

    unit[...] = jnp.ones(unit.shape, BF16)

    def raised(t):
        raise_row(t, t % steps)

    def lifted(l):
        lift(l % steps, l)

    def finished(l):
        finish(jnp.int32(l), l % steps)

    def settle(row):
        field[row - halo] = update(blocks - 1, row).astype(BF16)

    def spread(lines_at):
        widen(*lines_at)

    held_lines = lines_n - 2 * spare - 2 * blocks
    low = spare + blocks - halo
    for n in range(held_lines):
        field[low + n] = field_in[n]
    plan = []
    for k in range(blocks):
        for i in range(1 + k, lines_n - 1 - k):
            if not ready(k, i):
                plan.append((functools.partial(follow, k) if k else enter, i))
        if k == 0:
            plan.insert(3, (spread, (low, low + held_lines // 2)))
            plan.append((spread, (low + held_lines // 2, low + held_lines)))
    plan += [(settle, i) for i in range(halo, spare + blocks)] + [(spread, (0, low))]
    plan += [(settle, i) for i in range(lines_n - spare - blocks, lines_n - halo)] + [(spread, (low + held_lines, count))]
    plan += [(lambda _: edge_pick(), 0), (raised, 0), (raised, 1), (lambda _: edge_pack(), 0), (raised, 2),
             (lifted, 0), (raised, 3), (edge_blend, 0), (edge_blend, 1), (edge_blend, 2), (raised, 4), (lifted, 1), (raised, 5),
             (lambda _: edge_lift(), 0), (lifted, 2), (raised, 6), (lambda _: edge_finish(), 0), (lifted, 3), (finished, 0),
             (raised, 7), (finished, 1), (lifted, 4), (finished, 2), (mid, 0), (finished, 3)]
    for action, n in plan:
        action(n)

    halves = group // steps
    share_out = blocks_out // group

    def step(i, u, e, last):
        n = i // halves
        shrink_at = (i % halves) * (blocks_out // halves) + u * share_out
        for o in range(share_out):
            shrink(n + 1, shrink_at + o)
        emit(n, (i % halves) * steps + u, u)
        if last is None or last + 4 < fr + 2:
            finish(e + 4, (u + 4) % steps)
        if last is None or last + 1 < fr:
            mid((u + 1) % steps)
        if last is None or last + 5 < fr + 2:
            lift((u + 5) % steps, u + 5)
        if last is None:
            raise_row(e + 8, u)

    trips = fr // steps

    def begin(i):
        @pl.when(jnp.logical_and(i % halves == 0, i >= 3 * halves))
        def _():
            flushed(i // halves - 3).wait()

    def finish_trip(i):
        @pl.when(jnp.logical_and(i % halves == halves - 1, i >= halves))
        def _():
            flushed(i // halves - 1).start()

    def trip(i, _):
        begin(i)
        for u in range(steps):
            step(i, u, i * steps + u, None)
        finish_trip(i)
        return 0

    lax.fori_loop(0, trips - 1, trip, 0)
    i = jnp.int32(trips - 1)
    begin(i)
    for u in range(steps):
        step(i, u, i * steps + u, fr - steps + u)
    finish_trip(i)
    groups = fr // group
    if groups >= 3:
        flushed(groups - 3).wait()
    last = groups - 1
    parts = [pltpu.make_async_copy(
        stage.at[last % 2, pl.ds(h * ch // 2, ch // 2)],
        out.at[0, pl.ds(h * ch // 2, ch // 2), pl.ds(last * group, group), :], sems.at[2 + h]) for h in range(2)]
    for h in range(2):
        for o in range(blocks_out // 2):
            shrink(last, h * (blocks_out // 2) + o)
        parts[h].start()
    if groups >= 2:
        flushed(groups - 2).wait()
    for copy in parts:
        copy.wait()


def tile_program(dims, prepared):
    cin, ch, nout, fr, fl = dims
    got, lon, liftw = prepared[0], prepared[9], prepared[6]
    lines_n = got.shape[0]
    cw = lon.shape[0]
    blocks = prepared[4].shape[0]
    count = lines_n - 2 * (blocks + 1)
    group = 8
    steps = 4
    vmem = pl.BlockSpec(memory_space=pltpu.VMEM)
    slab = liftw.shape[1] // 3
    return pl.pallas_call(
        functools.partial(tile_kernel, dims),
        out_shape=jax.ShapeDtypeStruct((1, ch, fr, fl), BF16),
        in_specs=[vmem] * len(prepared),
        out_specs=pl.BlockSpec(memory_space=pl.ANY),
        scratch_shapes=[
            pltpu.VMEM((lines_n, cin, cw), F32),
            pltpu.VMEM((2, lines_n, 3 * cin, cw), F32),
            pltpu.VMEM((count, cin, cw), BF16),
            pltpu.VMEM((count, 3 * cin, fl), F32),
            pltpu.VMEM((steps, slab, fl), BF16),
            pltpu.VMEM((3 * slab, 128), BF16),
            pltpu.VMEM((steps, 3 * ch, fl), BF16),
            pltpu.VMEM((16, fl), BF16),
            pltpu.VMEM((steps, ch, fl), F32),
            pltpu.VMEM((2, ch, fl), F32),
            pltpu.VMEM((ch, 128), BF16),
            pltpu.VMEM((2, fl // 128, ch * group, 128), F32),
            pltpu.VMEM((2, ch, group, fl), BF16),
            pltpu.SemaphoreType.DMA((4,)),
        ],
        compiler_params=pltpu.CompilerParams(vmem_limit_bytes=44_000_000),
    )(*prepared)


def per_device(
    coarse, reg_gain, reg_weight, reg_bias, noisy, lift_weight, lift_bias, mid_gain, mid_weight, mid_bias,
):
    lifts = lift_weight.transpose(0, 1, 3, 2)
    prepared = first_program(
        coarse, noisy, reg_gain, reg_bias, reg_weight.reshape((-1,) + reg_weight.shape[3:]),
        lift_bias[None], mid_gain[None], mid_bias[None],
        lifts.reshape((9,) + lifts.shape[2:]), mid_weight.reshape((9,) + mid_weight.shape[2:]))
    return tile_program((coarse.shape[0], mid_weight.shape[2]) + noisy.shape[1:], prepared)


def solution(mesh):
    placed = (
        P(None, ("grp", "lat"), None),
        P(),
        P(),
        P(),
        P(("grp", "lat"), None, None, None),
        P(),
        P(),
        P(),
        P(),
        P(),
    )
    return jax.shard_map(
        per_device,
        mesh=mesh,
        in_specs=placed,
        out_specs=P(("grp", "lat"), None, None, None),
        check_vma=False,
    )
```

```python
import functools

import jax
import jax.numpy as jnp
from jax import lax
from jax.experimental import pallas as pl
from jax.experimental.pallas import tpu as pltpu
from jax.sharding import PartitionSpec as P

TILE_COLS = 4
LAT_UP = 4
LON_UP = 4
EPSILON = 1e-06
F32 = jnp.float32
BF16 = jnp.bfloat16
MESH = pl.DeviceIdType.MESH
HALF = 64


def activate(values, half_gain):
    inverse = lax.rsqrt(jnp.mean(values * values, axis=0, keepdims=True) + EPSILON)
    half = values * inverse * half_gain
    return half + half * jnp.tanh(half)


def split(numerator, factor):
    lower = numerator // (2 * factor)
    return lower, (numerator - 2 * factor * lower).astype(F32) / (2.0 * factor)


def column(row):
    n = row.shape[1]
    here = lax.broadcasted_iota(jnp.int32, (n, n), 0) == lax.broadcasted_iota(jnp.int32, (n, n), 1)
    return jnp.broadcast_to(jnp.sum(jnp.where(here, row, 0.0), axis=1, keepdims=True), (n, 128))


def thirds(values):
    high = values.astype(BF16).astype(F32)
    middle = (values - high).astype(BF16).astype(F32)
    return [high, middle, values - high - middle]


def nt_dot(a, b):
    return lax.dot_general(a, b, (((1,), (1,)), ((), ())), preferred_element_type=F32)


def lon_split(fine_col):
    lower, part = split(2 * fine_col + 1 - LON_UP + 2 * LON_UP, LON_UP)
    return lower - 1, part


def lat_split(t, top, bottom, count, start, total):
    lower, part = split(2 * (t - 2) + 1 - LAT_UP + 2 * LAT_UP, LAT_UP)
    low_line = jnp.where(top, 1, 0)
    high_line = jnp.where(bottom, count - 2, count - 1)
    row = start + t - 2
    ok = jnp.logical_and(row >= 0, row < total)
    return jnp.clip(lower, low_line, high_line), jnp.clip(lower + 1, low_line, high_line), part, ok


def gather_row(got, i, c, halo):
    cin = got.shape[1] - 16
    lane = lax.broadcasted_iota(jnp.int32, (1, 128), 1)
    span = 2 * halo * TILE_COLS
    side = got[i, cin:, :].astype(F32)
    outer = []
    for g in range(cin // 16):
        after = pltpu.roll(side, 128 - halo - g * span - 2 * halo * ((c + 1) % TILE_COLS), 1)
        before = pltpu.roll(side, 128 - halo - g * span - 2 * halo * c, 1)
        outer.append(jnp.where(lane < halo, after, jnp.where(lane >= 128 - halo, before, 0.0)))
    return jnp.concatenate([got[i, :cin, :].astype(F32), jnp.concatenate(outer, axis=0)], axis=1)


def convolve(values, half_gain, weight):
    cw = values.shape[1]
    values = activate(values, half_gain[:, :1])
    taps = jnp.concatenate(
        [pltpu.roll(values, 1, 1).astype(BF16), values.astype(BF16), pltpu.roll(values, cw - 1, 1).astype(BF16)],
        axis=0)
    return jnp.dot(weight, taps, preferred_element_type=F32)


def add_rows(values, above, here, below, bias):
    cin = values.shape[0]
    return (values + above[:cin] + here[cin:2 * cin] + below[2 * cin:] + bias[:, :1]).astype(BF16)


def first_kernel(
    coarse, noisy, gain, regb, regs, liftb, midg, midb, lifts, mids,
    got, got_cols, cols, grid, regw, regc, liftw, liftc, midw, lon, sidew, chosen, held, part, field,
    band, pieces, tile, rows, far_rows, gainv, regbv, vecs, regv, liftv, midv, liftt,
    send, recv, nsend, nrecv, local,
):
    me = lax.axis_index("lat")
    tile_rows = lax.axis_size("lat") // TILE_COLS
    r = me // TILE_COLS
    c = me % TILE_COLS
    north, south = r > 0, r < tile_rows - 1
    top, bottom = r == 0, r == tile_rows - 1
    cin, band_rows, clon = band.shape
    ch = midv.shape[1]
    nout, fr, fl = tile.shape
    blocks = regw.shape[0]
    halo = blocks + 1
    span = 2 * halo * TILE_COLS
    cw = chosen.shape[0]
    count = got.shape[0] - 2 * halo

    barrier = pltpu.get_barrier_semaphore()

    def greet(target):
        pl.semaphore_signal(barrier, inc=1, device_id={"lat": target}, device_id_type=MESH)

    for k in range(1, TILE_COLS):
        greet(r * TILE_COLS + (c + k) % TILE_COLS)

    @pl.when(north)
    def _():
        for k in range(TILE_COLS):
            greet((r - 1) * TILE_COLS + k)

    @pl.when(south)
    def _():
        for k in range(TILE_COLS):
            greet((r + 1) * TILE_COLS + k)

    loads = [
        pltpu.make_async_copy(coarse, band, local.at[0]),
        pltpu.make_async_copy(noisy.at[0], tile, local.at[1]),
        pltpu.make_async_copy(regs, regv, local.at[2]),
        pltpu.make_async_copy(mids, midv, local.at[3]),
        pltpu.make_async_copy(lifts, liftv, local.at[4]),
        pltpu.make_async_copy(gain, gainv, local.at[6]),
        pltpu.make_async_copy(regb, regbv, local.at[7]),
        pltpu.make_async_copy(liftb, vecs.at[0], local.at[8]),
        pltpu.make_async_copy(midg, vecs.at[1], local.at[9]),
        pltpu.make_async_copy(midb, vecs.at[2], local.at[10]),
    ]
    for load in loads:
        load.start()

    lane = lax.broadcasted_iota(jnp.int32, (1, 128), 1)
    both = band_rows * cin
    row_id = lax.broadcasted_iota(jnp.int32, (both, both), 0)
    sub_id = jnp.where(row_id >= cin, 1, 0)
    order = lax.broadcasted_iota(jnp.int32, (both, both), 1) == band_rows * (row_id - sub_id * cin) + sub_id
    order = jnp.where(order, 1.0, 0.0).astype(BF16)
    loads[0].wait()
    sorted_rows = jnp.dot(order, band[...].reshape(both, clon), preferred_element_type=F32)
    for sub in range(band_rows):
        row = sorted_rows[sub * cin:(sub + 1) * cin]
        parts = [row[:, b * 128:(b + 1) * 128] for b in range(TILE_COLS)]
        for b in range(TILE_COLS):
            pieces[b, sub, :cin, :] = parts[b].astype(BF16)
        side = jnp.zeros((16, 128), F32)
        for b in range(TILE_COLS):
            seam = jnp.where(lane < 64, parts[b], parts[(b + TILE_COLS - 1) % TILE_COLS])
            for g in range(cin // 16):
                at = g * span + 2 * halo * b
                moved = pltpu.roll(seam[g * 16:(g + 1) * 16], at + halo, 1)
                side = jnp.where(jnp.logical_and(lane >= at, lane < at + 2 * halo), moved, side)
        for b in range(TILE_COLS):
            pieces[b, sub, cin:, :] = side.astype(BF16)

    loads[1].wait()
    for side, first in ((0, 0), (1, fr - 2)):
        lines = jnp.concatenate([tile[n, first:first + 2, :].astype(F32) for n in range(nout)], axis=0)
        rows[side] = jnp.concatenate([lines[:, :fl // 2], lines[:, fl // 2:]], axis=0).astype(BF16)
    pick_row = lax.broadcasted_iota(jnp.int32, (4 * nout, 128), 0)
    pick_lane = lax.broadcasted_iota(jnp.int32, (4 * nout, 128), 1)
    packed = jnp.zeros((4 * nout, fr), F32)
    for n in range(nout):
        for s, (lo, at) in enumerate(((0, 0), (0, 1), (fl - 128, 126), (fl - 128, 127))):
            if s % 2 == 0:
                hit = jnp.zeros(pick_row.shape, jnp.bool_)
            hit = jnp.logical_or(hit, jnp.logical_and(pick_row == s * nout + n, pick_lane == at))
            if s % 2:
                packed = packed + nt_dot(jnp.where(hit, 1.0, 0.0).astype(BF16), tile[n, :, lo:lo + 128])
    cols[...] = jnp.concatenate([packed, jnp.zeros((4 * nout, 128 - fr), F32)], axis=1).astype(BF16)

    peers = TILE_COLS - 1 + jnp.where(north, TILE_COLS, 0) + jnp.where(south, TILE_COLS, 0)
    pl.semaphore_wait(barrier, peers)

    def remote(src, dst, ssem, rsem, target):
        return pltpu.make_async_remote_copy(
            src_ref=src, dst_ref=dst, send_sem=ssem, recv_sem=rsem,
            device_id={"lat": target}, device_id_type=MESH)

    whole, upper, lower = (0, 2), (0, 1), (1, 1)

    def landing(slot, span_rows):
        return got.at[pl.ds(2 * slot + span_rows[0], span_rows[1])]

    def far_first(k):
        return ((c // 2) * 2 + 2 + k) % TILE_COLS

    def beside():
        return c + 1 - 2 * (c % 2)

    def band_copy(k, row, slot, ssem, span_rows=whole):
        col = far_first(k)
        return remote(pieces.at[col, pl.ds(*span_rows)], landing(slot, span_rows), send.at[ssem], recv.at[slot],
                      row * TILE_COLS + col)

    west, east = (c + TILE_COLS - 1) % TILE_COLS, (c + 1) % TILE_COLS

    def col_copy(slot, row, col):
        return remote(cols, got_cols.at[slot], nsend.at[slot], nrecv.at[slot], row * TILE_COLS + col)

    def row_copy(slot, row):
        return remote(rows.at[1 - slot], far_rows.at[slot], nsend.at[8 + slot], nrecv.at[8 + slot], row * TILE_COLS + c)

    def each_band(action):
        for col, side, row, slot, span_rows in (
            (2, south, r + 1, 0, lower), (3, south, r + 1, 1, whole),
            (0, north, r - 1, 6, whole), (1, north, r - 1, 7, upper),
        ):
            @pl.when(jnp.logical_and(side, c == col))
            def _():
                for k in range(TILE_COLS):
                    action(band_copy(k, row, slot, TILE_COLS + k, span_rows))

        for k in range(TILE_COLS - 2):
            action(band_copy(k, r, 2 + c, k))
        action(remote(pieces.at[beside(), pl.ds(0, 2)], landing(2 + c, whole), send.at[2], recv.at[2 + c],
                      r * TILE_COLS + beside()))

    def each_edge(action):
        action(col_copy(0, r, east))
        action(col_copy(1, r, west))

        @pl.when(south)
        def _():
            action(row_copy(0, r + 1))
            action(col_copy(6, r + 1, c))
            action(col_copy(2, r + 1, east))
            action(col_copy(3, r + 1, west))

        @pl.when(north)
        def _():
            action(row_copy(1, r - 1))
            action(col_copy(7, r - 1, c))
            action(col_copy(4, r - 1, east))
            action(col_copy(5, r - 1, west))

    each_band(lambda copy: copy.start())
    own = pltpu.make_async_copy(pieces.at[c], landing(2 + c, whole), local.at[5])
    own.start()
    each_edge(lambda copy: copy.start())

    loads[2].wait()
    for k in range(blocks):
        for p in range(3):
            for q in range(3):
                regw[k, p * cin:(p + 1) * cin, q * cin:(q + 1) * cin] = regv[9 * k + 3 * p + q]

    loads[3].wait()
    for tap in range(9):
        midw[:, tap * ch:(tap + 1) * ch] = midv[tap]
    for load in loads[4:]:
        load.wait()
    slab = liftt.shape[0] // 3
    for p in range(3):
        noise = []
        for q in range(3):
            base = p * slab + q * cin
            liftt[base:base + cin, :] = liftv[3 * p + q, :cin, :]
            noise.append(liftv[3 * p + q, cin:, :].astype(F32))
        spare_rows = slab - 3 * (cin + nout)
        if p == 1:
            noise += thirds(vecs[0]) + [jnp.zeros((spare_rows - 3, ch), F32)]
        else:
            noise.append(jnp.zeros((spare_rows, ch), F32))
        liftt[p * slab + 3 * cin:(p + 1) * slab, :] = jnp.concatenate(noise, axis=0).astype(BF16)
    eye = jnp.where(lax.broadcasted_iota(jnp.int32, (ch, ch), 0) == lax.broadcasted_iota(jnp.int32, (ch, ch), 1), 1.0, 0.0)
    liftw[...] = nt_dot(eye.astype(BF16), liftt[...]).astype(BF16)

    low, weight = lon_split(lax.broadcasted_iota(jnp.int32, (1, fl), 1))
    low_lane = jnp.where(low < 0, low + cw, low)
    high_lane = jnp.where(low + 1 < 0, low + 1 + cw, low + 1)
    coarse_lane = lax.broadcasted_iota(jnp.int32, (cw, fl), 0)
    lon[...] = jnp.where(coarse_lane == low_lane, 1.0 - weight,
                         jnp.where(coarse_lane == high_lane, weight, 0.0)).astype(BF16)

    for k in range(blocks):
        regc[2 * k] = column(gainv[k:k + 1, :]) * 0.5
        regc[2 * k + 1] = column(regbv[k:k + 1, :])
    liftc[...] = column(vecs[1]) * 0.5
    bias_cols = jnp.zeros((ch, 128), F32)
    for n, third in enumerate(thirds(column(vecs[2]))):
        bias_cols = jnp.where(lane == n, third, bias_cols)
    midw[:, 9 * ch:] = bias_cols[:, :16].astype(BF16)

    tall = fr + 4
    wide = fl // 128
    for n in range(nout):
        for j in range(wide):
            grid[j, n * tall + 2:n * tall + 2 + fr, :] = tile[n, :, j * 128:(j + 1) * 128].astype(F32)

    near = fl // LON_UP
    picked_cols = [-1, 0, near - 1, near]
    select_lane = lax.broadcasted_iota(jnp.int32, (cw, 128), 0)
    select_pos = lax.broadcasted_iota(jnp.int32, (cw, 128), 1)
    hits = jnp.zeros((cw, 128), jnp.bool_)
    for s, col in enumerate(picked_cols):
        hits = jnp.logical_or(hits, jnp.logical_and(select_pos == s, select_lane == col % cw))
    chosen[...] = jnp.where(hits, 1.0, 0.0).astype(BF16)
    key = lax.broadcasted_iota(jnp.int32, (128, 1), 0)
    key_line = key // 4
    key_pick = key - 4 * key_line
    key_col = jnp.where(key_pick == 0, picked_cols[0], jnp.where(
        key_pick == 1, picked_cols[1], jnp.where(key_pick == 2, picked_cols[2], picked_cols[3])))
    edge_row = jnp.where(lane < HALF, lane, lane - HALF)
    for p in range(3):
        a, b, share, ok = lat_split(edge_row + p, top, bottom, count, r * fr, fr * tile_rows)
        wa = jnp.where(ok, 1.0 - share, 0.0)
        wb = jnp.where(ok, share, 0.0)
        by_row = jnp.where(key_line == a, wa, 0.0) + jnp.where(key_line == b, wb, 0.0)
        for q in range(3):
            lower_col, share_m = lon_split(jnp.where(lane < HALF, q - 2, fl - 1 + q))
            by_col = jnp.where(key_col == lower_col, 1.0 - share_m, jnp.where(key_col == lower_col + 1, share_m, 0.0))
            sidew[3 * p + q] = (by_row * by_col).astype(BF16)

    own.wait()

    def arrived(slot, span_rows=whole):
        remote(pieces.at[0, pl.ds(*span_rows)], landing(slot, span_rows), send.at[0], recv.at[slot], me).wait_recv()

    def edge(slot):
        if slot < 8:
            remote(cols, got_cols.at[slot], nsend.at[slot], nrecv.at[slot], me).wait_recv()
        else:
            remote(rows.at[0], far_rows.at[slot - 8], nsend.at[slot], nrecv.at[slot], me).wait_recv()

    for k in range(1, TILE_COLS):
        arrived(2 + (c + k) % TILE_COLS)

    spare = got.shape[0] // 4
    inner = got.shape[0] - 2 * spare

    def enter(i):
        values = gather_row(got, spare + i, c, halo)
        held[i] = values
        part[0, i] = convolve(values, regc[0], regw[0])

    def update(k, i):
        return add_rows(held[i], part[k, i - 1], part[k, i], part[k, i + 1], regc[2 * k + 1])

    def follow(k, i):
        values = update(k - 1, i).astype(F32)
        held[i] = values
        part[k, i] = convolve(values, regc[2 * k], regw[k])

    lag = 3
    for i in range(inner + lag * blocks):
        if i < inner:
            enter(i)
        for k in range(1, blocks):
            if k <= i - lag * k < inner - k:
                follow(k, i - lag * k)
        row = i - lag * blocks
        if blocks <= row < inner - blocks:
            field[row - blocks] = update(blocks - 1, row)

    @pl.when(north)
    def _():
        arrived(0, lower)
        arrived(1)

    @pl.when(south)
    def _():
        arrived(6)
        arrived(7, upper)

    edge(0)
    edge(1)

    @pl.when(north)
    def _():
        for slot in (2, 3, 6, 8):
            edge(slot)

    @pl.when(south)
    def _():
        for slot in (4, 5, 7, 9):
            edge(slot)

    for n in range(nout):
        for j in range(wide):
            at = slice(j * 128 % (fl // 2), j * 128 % (fl // 2) + 128)
            row = 2 * n + 2 * nout * (j * 128 // (fl // 2))
            above = far_rows[0, :, at].astype(F32)[row:row + 2]
            below = far_rows[1, :, at].astype(F32)[row:row + 2]
            grid[j, n * tall:n * tall + 2, :] = jnp.where(top, 0.0, above)
            grid[j, n * tall + 2 + fr:(n + 1) * tall, :] = jnp.where(bottom, 0.0, below)

    each_band(lambda copy: copy.wait_send())
    each_edge(lambda copy: copy.wait_send())


def first_program(coarse, noisy, gain, regb, regs, liftb, midg, midb, lifts, mids):
    hbm = pl.BlockSpec(memory_space=pltpu.HBM)
    vmem = pl.BlockSpec(memory_space=pltpu.VMEM)
    dma = pltpu.SemaphoreType.DMA
    cin, band_rows, clon = coarse.shape
    nout, fr, fl = noisy.shape[1:]
    ch = mids.shape[1]
    blocks = regs.shape[0] // 9
    slab = 3 * cin + -(-(3 * nout + 3) // 16) * 16
    lines_n = band_rows * (TILE_COLS + 4)
    ct_lon = clon // TILE_COLS
    cw = 2 * ct_lon
    assert ct_lon == 128 and cin % 16 == 0 and band_rows == 2
    assert (cin // 16) * 2 * (blocks + 1) * TILE_COLS <= 128
    shape = jax.ShapeDtypeStruct
    return pl.pallas_call(
        first_kernel,
        out_shape=(
            shape((lines_n, cin + 16, 128), BF16),
            shape((8, 4 * nout, 128), BF16),
            shape((4 * nout, 128), BF16),
            shape((fl // 128, nout * (fr + 4), 128), F32),
            shape((blocks, 3 * cin, 3 * cin), BF16),
            shape((2 * blocks, cin, 128), F32),
            shape((ch, 3 * slab), BF16),
            shape((ch, 128), F32),
            shape((ch, 9 * ch + 16), BF16),
            shape((cw, fl), BF16),
            shape((9, 128, 128), BF16),
            shape((cw, 128), BF16),
            shape((lines_n - 2 * (lines_n // 4), cin, cw), F32),
            shape((blocks, lines_n - 2 * (lines_n // 4), 3 * cin, cw), F32),
            shape((lines_n - 2 * (lines_n // 4) - 2 * blocks, cin, cw), BF16),
        ),
        in_specs=[hbm] * 10,
        out_specs=(vmem,) * 15,
        scratch_shapes=[
            pltpu.VMEM((cin, band_rows, clon), BF16),
            pltpu.VMEM((TILE_COLS, band_rows, cin + 16, 128), BF16),
            pltpu.VMEM((nout, fr, fl), BF16),
            pltpu.VMEM((2, 4 * nout, fl // 2), BF16),
            pltpu.VMEM((2, 4 * nout, fl // 2), BF16),
            pltpu.VMEM(gain.shape, F32),
            pltpu.VMEM(regb.shape, F32),
            pltpu.VMEM((3, 1, ch), F32),
            pltpu.VMEM(regs.shape, BF16),
            pltpu.VMEM(lifts.shape, BF16),
            pltpu.VMEM(mids.shape, BF16),
            pltpu.VMEM((3 * slab, ch), BF16),
            dma((2 * TILE_COLS,)), dma((8,)), dma((10,)), dma((10,)), dma((11,)),
        ],
        compiler_params=pltpu.CompilerParams(
            collective_id=0, has_side_effects=True, vmem_limit_bytes=24_000_000),
    )(*[pltpu.with_memory_space_constraint(x, pltpu.HBM) for x in (
        coarse, noisy, gain, regb, regs, liftb, midg, midb, lifts, mids)])


def tile_kernel(
    dims, got, got_cols, own_cols, grid, regw, regc, liftw, gains, midw, lon, sidew, chosen, held_in, part_in, field_in, out,
    held, part, field, lines, upper, sides, bands, unit, raw, prod, edges, rows_out, stage, sems,
):
    cin, ch, nout, fr, fl = dims
    lines_n, count, cw = got.shape[0], field.shape[0], field.shape[2]
    blocks = regw.shape[0]
    halo = blocks + 1
    me = lax.axis_index("lat")
    tile_row, tile_rows = me // TILE_COLS, lax.axis_size("lat") // TILE_COLS
    c = me % TILE_COLS
    top, bottom = tile_row == 0, tile_row == tile_rows - 1
    steps = bands.shape[0]
    wide = fl // 128
    lane = lax.broadcasted_iota(jnp.int32, (1, 128), 1)
    lane_first, lane_last = lane == 0, lane == 127
    spare = lines_n // 4

    def known(i, values):
        if i < spare:
            return jnp.where(top, 0.0, values)
        if i >= lines_n - spare:
            return jnp.where(bottom, 0.0, values)
        return values

    def ready(k, i):
        return spare + k <= i < lines_n - spare - k

    def product(k, i):
        return part_in[k, i - spare] if ready(k, i) else part[k % 2, i]

    def enter(i):
        values = known(i, gather_row(got, i, c, halo))
        held[i] = values
        part[0, i] = convolve(values, regc[0], regw[0])

    def update(k, i):
        values = held_in[i - spare] if ready(k, i) else held[i]
        values = add_rows(values, product(k, i - 1), product(k, i), product(k, i + 1), regc[2 * k + 1])
        return known(i, values.astype(F32))

    def follow(k, i):
        values = update(k - 1, i)
        held[i] = values
        part[k % 2, i] = convolve(values, regc[2 * k], regw[k])

    def widen(first, last):
        coarse = field[first:last].reshape((last - first) * cin, cw)
        lines[first:last] = jnp.dot(coarse, lon[...], preferred_element_type=F32).reshape(last - first, cin, fl)

    def neighbours(values, seam_l, seam_r):
        parts = [values[:, j * 128:(j + 1) * 128] for j in range(wide)]
        onward = [seam_l] + [pltpu.roll(v, 1, 1) for v in parts]
        back = [pltpu.roll(v, 127, 1) for v in parts] + [seam_r]
        return (jnp.concatenate([jnp.where(lane_first, onward[j], onward[j + 1]) for j in range(wide)], axis=1),
                jnp.concatenate([jnp.where(lane_last, back[j + 1], back[j]) for j in range(wide)], axis=1))

    def blend(t):
        return lat_split(t, top, bottom, count, tile_row * fr, fr * tile_rows)

    def inside(t):
        row = tile_row * fr + t - 2
        return jnp.logical_and(row >= 0, row < fr * tile_rows)

    tall = fr + 4
    slab = upper.shape[1]

    def along(middle, above, below):
        above = jnp.where(top, 0.0, pltpu.roll(above.astype(F32), 128 - (fr - 2), 1))
        below = jnp.where(bottom, 0.0, pltpu.roll(below.astype(F32), fr + 2, 1))
        middle = pltpu.roll(middle.astype(F32), 2, 1)
        return jnp.where(lane < 2, above, jnp.where(lane < fr + 2, middle, below))

    west = along(got_cols[0], got_cols[2], got_cols[4])
    east = along(got_cols[1], got_cols[3], got_cols[5])
    here = along(own_cols[...], got_cols[6], got_cols[7])
    none = jnp.ones((slab - 3 * (cin + nout), 128), F32)
    left_cols = jnp.concatenate([west[2 * nout:], here[:nout], none], axis=0)
    right_cols = jnp.concatenate([here[3 * nout:], east[:2 * nout], none], axis=0)
    west_col, east_col = west[3 * nout:], east[:nout]

    def noise_rows(t):
        rows = [grid[j, pl.ds(t, nout, stride=tall), :] for j in range(wide)]
        onward = [pltpu.roll(v, 1, 1) for v in rows]
        back = [pltpu.roll(v, 127, 1) for v in rows]
        edge_l = pltpu.roll(west_col, (128 - t) % 128 if isinstance(t, int) else 128 - t, 1)
        edge_r = pltpu.roll(east_col, 127 - t, 1)
        pieces = []
        for j in range(wide):
            lo = jnp.where(lane_first, onward[j - 1] if j else edge_l, onward[j])
            hi = jnp.where(lane_last, back[j + 1] if j < wide - 1 else edge_r, back[j])
            pieces.append(jnp.concatenate([lo, rows[j], hi, none], axis=0))
        return jnp.concatenate(pieces, axis=1).astype(BF16)

    def raise_row(t, slot):
        a, b, share, ok = blend(jnp.int32(t))
        wa = jnp.where(ok, 1.0 - share, 0.0)
        wb = jnp.where(ok, share, 0.0)
        static = isinstance(t, int)
        for o in range(0, cin, 16):
            values = (wa * lines[a, o:o + 16, :] + wb * lines[b, o:o + 16, :]).astype(BF16)
            seam = sides[cin + o:cin + o + 16, :]
            seam_l = pltpu.roll(seam, (128 - t) % 128 if static else 128 - t, 1)
            seam_r = pltpu.roll(seam, (127 + HALF - t) % 128 if static else 127 + HALF - t, 1)
            onward, back = neighbours(values, seam_l, seam_r)
            upper[slot, o:o + 16, :] = onward
            upper[slot, cin + o:cin + o + 16, :] = values
            upper[slot, 2 * cin + o:2 * cin + o + 16, :] = back
        upper[slot, 3 * cin:slab, :] = noise_rows(t)

    edge_row = jnp.where(lane < HALF, lane, lane - HALF)

    found = {}

    def edge_pick():
        found["narrow"] = jnp.dot(field[...].reshape(count * cin, cw), chosen[...], preferred_element_type=F32)

    def edge_pack():
        packed = found["narrow"][:cin]
        for i in range(1, count):
            packed = packed + pltpu.roll(found["narrow"][i * cin:(i + 1) * cin], 4 * i, 1)
        found["packed"] = packed.astype(BF16)

    def edge_blend(p):
        for q in range(3):
            base = p * slab + q * cin
            sides[base:base + cin, :] = jnp.dot(
                found["packed"], sidew[3 * p + q], preferred_element_type=F32).astype(BF16)
        sides[p * slab + 3 * cin:(p + 1) * slab, :] = jnp.where(
            lane < HALF, pltpu.roll(left_cols, (128 - p) % 128, 1), pltpu.roll(right_cols, HALF - p, 1)).astype(BF16)

    def edge_lift():
        found["lift"] = jnp.dot(liftw[...], sides[...], preferred_element_type=F32)

    def edge_finish():
        edges[...] = jnp.where(inside(edge_row + 1), activate(found["lift"], gains[...]), 0.0).astype(BF16)

    def lift(slot, target):
        window = jnp.concatenate([upper[(slot + n) % steps] for n in range(3)], axis=0)
        raw[target % steps] = jnp.dot(liftw[...], window, preferred_element_type=F32)

    def finish(l, slot):
        squares = jnp.zeros((8, fl), F32)
        for o in range(0, ch, 16):
            values = raw[slot, o:o + 16, :]
            values = values * values
            squares = squares + (values[:8] + values[8:])
        inverse = lax.rsqrt(jnp.sum(squares, axis=0, keepdims=True) * (1.0 / ch) + EPSILON)
        inverse = jnp.where(inside(l + 1), inverse, 0.0)
        for o in range(0, ch, 16):
            half_gain = jnp.concatenate([gains[o:o + 16, :]] * wide, axis=1)
            half = raw[slot, o:o + 16, :] * inverse * half_gain
            values = (half + half * jnp.tanh(half)).astype(BF16)
            edge = edges[o:o + 16, :]
            edge_l = pltpu.roll(edge, 128 - l, 1)
            edge_r = pltpu.roll(edge, 127 + HALF - l, 1)
            onward, back = neighbours(values, edge_l, edge_r)
            bands[slot, o:o + 16, :] = onward
            bands[slot, ch + o:ch + o + 16, :] = values
            bands[slot, 2 * ch + o:2 * ch + o + 16, :] = back

    def mid(slot):
        window = jnp.concatenate([bands[(slot + n) % steps] for n in range(3)] + [unit[...]], axis=0)
        prod[slot % 2] = jnp.dot(midw[...], window, preferred_element_type=F32)

    group = stage.shape[2]
    blocks_out = ch // 8

    def flushed(n):
        return pltpu.make_async_copy(
            stage.at[n % 2], out.at[0, :, pl.ds(n * group if isinstance(n, int) else pl.multiple_of(n * group, group), group), :], sems.at[n % 2])

    def shrink(n, o, only=None):
        for j in range(wide) if only is None else (only,):
            block = rows_out[n % 2, j, pl.ds(o * 8 * group if isinstance(o, int) else pl.multiple_of(o * 8 * group, 8 * group), 8 * group), :]
            stage[n % 2, pl.ds(o * 8, 8), :, j * 128:(j + 1) * 128] = block.reshape(8, group, 128).astype(BF16)

    def emit(n, spot, slot):
        for o in range(0, ch, 16):
            for j in range(wide):
                at = slice(j * 128, (j + 1) * 128)
                total = raw[(slot + 1) % steps, o:o + 16, at] + prod[slot % 2, o:o + 16, at]
                rows_out[n % 2, j, pl.ds(spot + o * group, 16, stride=group), :] = total

    unit[...] = jnp.ones(unit.shape, BF16)

    def raised(t):
        raise_row(t, t % steps)

    def lifted(l):
        lift(l % steps, l)

    def finished(l):
        finish(jnp.int32(l), l % steps)

    def settle(row):
        field[row - halo] = update(blocks - 1, row).astype(BF16)

    def spread(lines_at):
        widen(*lines_at)

    held_lines = lines_n - 2 * spare - 2 * blocks
    low = spare + blocks - halo
    for n in range(held_lines):
        field[low + n] = field_in[n]
    plan = []
    for k in range(blocks):
        for i in range(1 + k, lines_n - 1 - k):
            if not ready(k, i):
                plan.append((functools.partial(follow, k) if k else enter, i))
        if k == 0:
            plan.insert(3, (spread, (low, low + held_lines // 2)))
            plan.append((spread, (low + held_lines // 2, low + held_lines)))
    plan += [(settle, i) for i in range(halo, spare + blocks)] + [(spread, (0, low))]
    plan += [(settle, i) for i in range(lines_n - spare - blocks, lines_n - halo)] + [(spread, (low + held_lines, count))]
    plan += [(lambda _: edge_pick(), 0), (lambda _: edge_pack(), 0), (edge_blend, 0), (raised, 0), (edge_blend, 1), (raised, 1),
             (edge_blend, 2), (raised, 2), (lifted, 0), (raised, 3), (lambda _: edge_lift(), 0), (lifted, 1), (raised, 4),
             (lifted, 2), (raised, 5), (lambda _: edge_finish(), 0), (lifted, 3), (raised, 6), (finished, 0),
             (lifted, 4), (raised, 7), (finished, 1), (finished, 2), (mid, 0), (finished, 3)]
    for action, n in plan:
        action(n)

    halves = group // steps
    share_out = blocks_out // group

    def step(i, u, e, last):
        n = i // halves
        shrink_at = (i % halves) * (blocks_out // halves) + u * share_out
        emit(n, (i % halves) * steps + u, u)
        for o in range(share_out):
            shrink(n + 1, shrink_at + o)
        if last is None:
            raise_row(e + 8, u)
        if last is None or last + 4 < fr + 2:
            finish(e + 4, (u + 4) % steps)
        if last is None or last + 1 < fr:
            mid((u + 1) % steps)
        if last is None or last + 5 < fr + 2:
            lift((u + 5) % steps, u + 5)

    trips = fr // steps

    def begin(i):
        @pl.when(jnp.logical_and(i % halves == 0, i >= 3 * halves))
        def _():
            flushed(i // halves - 3).wait()

    def finish_trip(i):
        @pl.when(jnp.logical_and(i % halves == halves - 1, i >= halves))
        def _():
            flushed(i // halves - 1).start()

    def trip(i, _):
        begin(i)
        for u in range(steps):
            step(i, u, i * steps + u, None)
        finish_trip(i)
        return 0

    lax.fori_loop(0, trips - 1, trip, 0)
    groups = fr // group
    last = groups - 1
    if groups >= 3:
        flushed(groups - 3).wait()
    for u in range(steps):
        step(trips - 1, u, (trips - 1) * steps + u, fr - steps + u)
    if groups >= 2:
        flushed(groups - 2).start()
    parts = [pltpu.make_async_copy(
        stage.at[last % 2, :, :, pl.ds(j * 128, 128)],
        out.at[0, :, pl.ds(last * group, group), pl.ds(j * 128, 128)], sems.at[2 + j]) for j in range(wide)]
    for j in range(wide):
        for o in range(blocks_out):
            shrink(last, o, j)
        parts[j].start()
    if groups >= 2:
        flushed(groups - 2).wait()
    for copy in parts:
        copy.wait()


def tile_program(dims, prepared):
    cin, ch, nout, fr, fl = dims
    got, lon, liftw = prepared[0], prepared[9], prepared[6]
    lines_n = got.shape[0]
    cw = lon.shape[0]
    blocks = prepared[4].shape[0]
    count = lines_n - 2 * (blocks + 1)
    group = 8
    steps = 4
    vmem = pl.BlockSpec(memory_space=pltpu.VMEM)
    slab = liftw.shape[1] // 3
    return pl.pallas_call(
        functools.partial(tile_kernel, dims),
        out_shape=jax.ShapeDtypeStruct((1, ch, fr, fl), BF16),
        in_specs=[vmem] * len(prepared),
        out_specs=pl.BlockSpec(memory_space=pl.ANY),
        scratch_shapes=[
            pltpu.VMEM((lines_n, cin, cw), F32),
            pltpu.VMEM((2, lines_n, 3 * cin, cw), F32),
            pltpu.VMEM((count, cin, cw), BF16),
            pltpu.VMEM((count, cin, fl), F32),
            pltpu.VMEM((steps, slab, fl), BF16),
            pltpu.VMEM((3 * slab, 128), BF16),
            pltpu.VMEM((steps, 3 * ch, fl), BF16),
            pltpu.VMEM((16, fl), BF16),
            pltpu.VMEM((steps, ch, fl), F32),
            pltpu.VMEM((2, ch, fl), F32),
            pltpu.VMEM((ch, 128), BF16),
            pltpu.VMEM((2, fl // 128, ch * group, 128), F32),
            pltpu.VMEM((2, ch, group, fl), BF16),
            pltpu.SemaphoreType.DMA((2 + fl // 128,)),
        ],
        compiler_params=pltpu.CompilerParams(vmem_limit_bytes=44_000_000),
    )(*prepared)


def per_device(
    coarse, reg_gain, reg_weight, reg_bias, noisy, lift_weight, lift_bias, mid_gain, mid_weight, mid_bias,
):
    lifts = lift_weight.transpose(0, 1, 3, 2)
    prepared = first_program(
        coarse, noisy, reg_gain, reg_bias, reg_weight.reshape((-1,) + reg_weight.shape[3:]),
        lift_bias[None], mid_gain[None], mid_bias[None],
        lifts.reshape((9,) + lifts.shape[2:]), mid_weight.reshape((9,) + mid_weight.shape[2:]))
    return tile_program((coarse.shape[0], mid_weight.shape[2]) + noisy.shape[1:], prepared)


def solution(mesh):
    placed = (
        P(None, ("grp", "lat"), None),
        P(),
        P(),
        P(),
        P(("grp", "lat"), None, None, None),
        P(),
        P(),
        P(),
        P(),
        P(),
    )
    return jax.shard_map(
        per_device,
        mesh=mesh,
        in_specs=placed,
        out_specs=P(("grp", "lat"), None, None, None),
        check_vma=False,
    )
```

```python
import functools

import jax
import jax.numpy as jnp
from jax import lax
from jax.experimental import pallas as pl
from jax.experimental.pallas import tpu as pltpu
from jax.sharding import PartitionSpec as P

TILE_COLS = 4
LAT_UP = 4
LON_UP = 4
EPSILON = 1e-06
F32 = jnp.float32
BF16 = jnp.bfloat16
MESH = pl.DeviceIdType.MESH
HALF = 64


def activate(values, half_gain):
    inverse = lax.rsqrt(jnp.mean(values * values, axis=0, keepdims=True) + EPSILON)
    half = values * inverse * half_gain
    return half + half * jnp.tanh(half)


def split(numerator, factor):
    lower = numerator // (2 * factor)
    return lower, (numerator - 2 * factor * lower).astype(F32) / (2.0 * factor)


def column(row):
    n = row.shape[1]
    here = lax.broadcasted_iota(jnp.int32, (n, n), 0) == lax.broadcasted_iota(jnp.int32, (n, n), 1)
    return jnp.broadcast_to(jnp.sum(jnp.where(here, row, 0.0), axis=1, keepdims=True), (n, 128))


def thirds(values):
    high = values.astype(BF16).astype(F32)
    middle = (values - high).astype(BF16).astype(F32)
    return [high, middle, values - high - middle]


def nt_dot(a, b):
    return lax.dot_general(a, b, (((1,), (1,)), ((), ())), preferred_element_type=F32)


def lon_split(fine_col):
    lower, part = split(2 * fine_col + 1 - LON_UP + 2 * LON_UP, LON_UP)
    return lower - 1, part


def lat_split(t, top, bottom, count, start, total):
    lower, part = split(2 * (t - 2) + 1 - LAT_UP + 2 * LAT_UP, LAT_UP)
    low_line = jnp.where(top, 1, 0)
    high_line = jnp.where(bottom, count - 2, count - 1)
    row = start + t - 2
    ok = jnp.logical_and(row >= 0, row < total)
    return jnp.clip(lower, low_line, high_line), jnp.clip(lower + 1, low_line, high_line), part, ok


def gather_row(got, i, c, halo):
    cin = got.shape[1] - 16
    lane = lax.broadcasted_iota(jnp.int32, (1, 128), 1)
    span = 2 * halo * TILE_COLS
    side = got[i, cin:, :].astype(F32)
    outer = []
    for g in range(cin // 16):
        after = pltpu.roll(side, 128 - halo - g * span - 2 * halo * ((c + 1) % TILE_COLS), 1)
        before = pltpu.roll(side, 128 - halo - g * span - 2 * halo * c, 1)
        outer.append(jnp.where(lane < halo, after, jnp.where(lane >= 128 - halo, before, 0.0)))
    return jnp.concatenate([got[i, :cin, :].astype(F32), jnp.concatenate(outer, axis=0)], axis=1)


def convolve(values, half_gain, weight):
    cw = values.shape[1]
    values = activate(values, half_gain[:, :1])
    taps = jnp.concatenate(
        [pltpu.roll(values, 1, 1).astype(BF16), values.astype(BF16), pltpu.roll(values, cw - 1, 1).astype(BF16)],
        axis=0)
    return jnp.dot(weight, taps, preferred_element_type=F32)


def add_rows(values, above, here, below, bias):
    cin = values.shape[0]
    return (values + above[:cin] + here[cin:2 * cin] + below[2 * cin:] + bias[:, :1]).astype(BF16)


def first_kernel(
    coarse, noisy, gain, regb, regs, liftb, midg, midb, lifts, mids,
    got, got_cols, cols, grid, regw, regc, liftw, liftc, midw, lon, sidew, chosen, held, part, field,
    band, pieces, tile, rows, far_rows, gainv, regbv, vecs, regv, liftv, midv, liftt,
    send, recv, nsend, nrecv, local,
):
    me = lax.axis_index("lat")
    tile_rows = lax.axis_size("lat") // TILE_COLS
    r = me // TILE_COLS
    c = me % TILE_COLS
    north, south = r > 0, r < tile_rows - 1
    top, bottom = r == 0, r == tile_rows - 1
    cin, band_rows, clon = band.shape
    ch = midv.shape[1]
    nout, fr, fl = tile.shape
    blocks = regw.shape[0]
    halo = blocks + 1
    span = 2 * halo * TILE_COLS
    cw = chosen.shape[0]
    count = got.shape[0] - 2 * halo

    barrier = pltpu.get_barrier_semaphore()

    def greet(target):
        pl.semaphore_signal(barrier, inc=1, device_id={"lat": target}, device_id_type=MESH)

    for k in range(1, TILE_COLS):
        greet(r * TILE_COLS + (c + k) % TILE_COLS)

    @pl.when(north)
    def _():
        for k in range(TILE_COLS):
            greet((r - 1) * TILE_COLS + k)

    @pl.when(south)
    def _():
        for k in range(TILE_COLS):
            greet((r + 1) * TILE_COLS + k)

    loads = [
        pltpu.make_async_copy(coarse, band, local.at[0]),
        pltpu.make_async_copy(noisy.at[0], tile, local.at[1]),
        pltpu.make_async_copy(regs, regv, local.at[2]),
        pltpu.make_async_copy(mids, midv, local.at[3]),
        pltpu.make_async_copy(lifts, liftv, local.at[4]),
        pltpu.make_async_copy(gain, gainv, local.at[6]),
        pltpu.make_async_copy(regb, regbv, local.at[7]),
        pltpu.make_async_copy(liftb, vecs.at[0], local.at[8]),
        pltpu.make_async_copy(midg, vecs.at[1], local.at[9]),
        pltpu.make_async_copy(midb, vecs.at[2], local.at[10]),
    ]
    for load in loads:
        load.start()

    lane = lax.broadcasted_iota(jnp.int32, (1, 128), 1)
    both = band_rows * cin
    row_id = lax.broadcasted_iota(jnp.int32, (both, both), 0)
    sub_id = jnp.where(row_id >= cin, 1, 0)
    order = lax.broadcasted_iota(jnp.int32, (both, both), 1) == band_rows * (row_id - sub_id * cin) + sub_id
    order = jnp.where(order, 1.0, 0.0).astype(BF16)
    loads[0].wait()
    sorted_rows = jnp.dot(order, band[...].reshape(both, clon), preferred_element_type=F32)
    for sub in range(band_rows):
        row = sorted_rows[sub * cin:(sub + 1) * cin]
        parts = [row[:, b * 128:(b + 1) * 128] for b in range(TILE_COLS)]
        for b in range(TILE_COLS):
            pieces[b, sub, :cin, :] = parts[b].astype(BF16)
        side = jnp.zeros((16, 128), F32)
        for b in range(TILE_COLS):
            seam = jnp.where(lane < 64, parts[b], parts[(b + TILE_COLS - 1) % TILE_COLS])
            for g in range(cin // 16):
                at = g * span + 2 * halo * b
                moved = pltpu.roll(seam[g * 16:(g + 1) * 16], at + halo, 1)
                side = jnp.where(jnp.logical_and(lane >= at, lane < at + 2 * halo), moved, side)
        for b in range(TILE_COLS):
            pieces[b, sub, cin:, :] = side.astype(BF16)

    loads[1].wait()
    for side, first in ((0, 0), (1, fr - 2)):
        lines = jnp.concatenate([tile[n, first:first + 2, :].astype(F32) for n in range(nout)], axis=0)
        rows[side] = jnp.concatenate([lines[:, :fl // 2], lines[:, fl // 2:]], axis=0).astype(BF16)
    pick_row = lax.broadcasted_iota(jnp.int32, (4 * nout, 128), 0)
    pick_lane = lax.broadcasted_iota(jnp.int32, (4 * nout, 128), 1)
    packed = jnp.zeros((4 * nout, fr), F32)
    for n in range(nout):
        for s, (lo, at) in enumerate(((0, 0), (0, 1), (fl - 128, 126), (fl - 128, 127))):
            if s % 2 == 0:
                hit = jnp.zeros(pick_row.shape, jnp.bool_)
            hit = jnp.logical_or(hit, jnp.logical_and(pick_row == s * nout + n, pick_lane == at))
            if s % 2:
                packed = packed + nt_dot(jnp.where(hit, 1.0, 0.0).astype(BF16), tile[n, :, lo:lo + 128])
    cols[...] = jnp.concatenate([packed, jnp.zeros((4 * nout, 128 - fr), F32)], axis=1).astype(BF16)

    peers = TILE_COLS - 1 + jnp.where(north, TILE_COLS, 0) + jnp.where(south, TILE_COLS, 0)
    pl.semaphore_wait(barrier, peers)

    def remote(src, dst, ssem, rsem, target):
        return pltpu.make_async_remote_copy(
            src_ref=src, dst_ref=dst, send_sem=ssem, recv_sem=rsem,
            device_id={"lat": target}, device_id_type=MESH)

    whole, upper, lower = (0, 2), (0, 1), (1, 1)

    def landing(slot, span_rows):
        return got.at[pl.ds(2 * slot + span_rows[0], span_rows[1])]

    def far_first(k):
        return ((c // 2) * 2 + 2 + k) % TILE_COLS

    def beside():
        return c + 1 - 2 * (c % 2)

    def band_copy(k, row, slot, ssem, span_rows=whole):
        col = far_first(k)
        return remote(pieces.at[col, pl.ds(*span_rows)], landing(slot, span_rows), send.at[ssem], recv.at[slot],
                      row * TILE_COLS + col)

    west, east = (c + TILE_COLS - 1) % TILE_COLS, (c + 1) % TILE_COLS

    def col_copy(slot, row, col):
        return remote(cols, got_cols.at[slot], nsend.at[slot], nrecv.at[slot], row * TILE_COLS + col)

    def row_copy(slot, row):
        return remote(rows.at[1 - slot], far_rows.at[slot], nsend.at[8 + slot], nrecv.at[8 + slot], row * TILE_COLS + c)

    def each_band(action):
        for col, side, row, slot, span_rows in (
            (2, south, r + 1, 0, lower), (3, south, r + 1, 1, whole),
            (0, north, r - 1, 6, whole), (1, north, r - 1, 7, upper),
        ):
            @pl.when(jnp.logical_and(side, c == col))
            def _():
                for k in range(TILE_COLS):
                    action(band_copy(k, row, slot, TILE_COLS + k, span_rows))

        for k in range(TILE_COLS - 2):
            action(band_copy(k, r, 2 + c, k))
        action(remote(pieces.at[beside(), pl.ds(0, 2)], landing(2 + c, whole), send.at[2], recv.at[2 + c],
                      r * TILE_COLS + beside()))

    def each_edge(action):
        action(col_copy(0, r, east))
        action(col_copy(1, r, west))

        @pl.when(south)
        def _():
            action(row_copy(0, r + 1))
            action(col_copy(6, r + 1, c))
            action(col_copy(2, r + 1, east))
            action(col_copy(3, r + 1, west))

        @pl.when(north)
        def _():
            action(row_copy(1, r - 1))
            action(col_copy(7, r - 1, c))
            action(col_copy(4, r - 1, east))
            action(col_copy(5, r - 1, west))

    each_band(lambda copy: copy.start())
    own = pltpu.make_async_copy(pieces.at[c], landing(2 + c, whole), local.at[5])
    own.start()
    each_edge(lambda copy: copy.start())

    loads[2].wait()
    for k in range(blocks):
        for p in range(3):
            for q in range(3):
                regw[k, p * cin:(p + 1) * cin, q * cin:(q + 1) * cin] = regv[9 * k + 3 * p + q]

    loads[3].wait()
    for tap in range(9):
        midw[:, tap * ch:(tap + 1) * ch] = midv[tap]
    for load in loads[4:]:
        load.wait()
    slab = liftt.shape[0] // 3
    for p in range(3):
        noise = []
        for q in range(3):
            base = p * slab + q * cin
            liftt[base:base + cin, :] = liftv[3 * p + q, :cin, :]
            noise.append(liftv[3 * p + q, cin:, :].astype(F32))
        spare_rows = slab - 3 * (cin + nout)
        if p == 1:
            noise += thirds(vecs[0]) + [jnp.zeros((spare_rows - 3, ch), F32)]
        else:
            noise.append(jnp.zeros((spare_rows, ch), F32))
        liftt[p * slab + 3 * cin:(p + 1) * slab, :] = jnp.concatenate(noise, axis=0).astype(BF16)
    eye = jnp.where(lax.broadcasted_iota(jnp.int32, (ch, ch), 0) == lax.broadcasted_iota(jnp.int32, (ch, ch), 1), 1.0, 0.0)
    liftw[...] = nt_dot(eye.astype(BF16), liftt[...]).astype(BF16)

    low, weight = lon_split(lax.broadcasted_iota(jnp.int32, (1, fl), 1))
    low_lane = jnp.where(low < 0, low + cw, low)
    high_lane = jnp.where(low + 1 < 0, low + 1 + cw, low + 1)
    coarse_lane = lax.broadcasted_iota(jnp.int32, (cw, fl), 0)
    lon[...] = jnp.where(coarse_lane == low_lane, 1.0 - weight,
                         jnp.where(coarse_lane == high_lane, weight, 0.0)).astype(BF16)

    for k in range(blocks):
        regc[2 * k] = column(gainv[k:k + 1, :]) * 0.5
        regc[2 * k + 1] = column(regbv[k:k + 1, :])
    liftc[...] = column(vecs[1]) * 0.5
    bias_cols = jnp.zeros((ch, 128), F32)
    for n, third in enumerate(thirds(column(vecs[2]))):
        bias_cols = jnp.where(lane == n, third, bias_cols)
    midw[:, 9 * ch:] = bias_cols[:, :16].astype(BF16)

    tall = fr + 4
    wide = fl // 128
    for n in range(nout):
        for j in range(wide):
            grid[j, n * tall + 2:n * tall + 2 + fr, :] = tile[n, :, j * 128:(j + 1) * 128].astype(F32)

    near = fl // LON_UP
    picked_cols = [-1, 0, near - 1, near]
    select_lane = lax.broadcasted_iota(jnp.int32, (cw, 128), 0)
    select_pos = lax.broadcasted_iota(jnp.int32, (cw, 128), 1)
    hits = jnp.zeros((cw, 128), jnp.bool_)
    for s, col in enumerate(picked_cols):
        hits = jnp.logical_or(hits, jnp.logical_and(select_pos == s, select_lane == col % cw))
    chosen[...] = jnp.where(hits, 1.0, 0.0).astype(BF16)
    key = lax.broadcasted_iota(jnp.int32, (128, 1), 0)
    key_line = key // 4
    key_pick = key - 4 * key_line
    key_col = jnp.where(key_pick == 0, picked_cols[0], jnp.where(
        key_pick == 1, picked_cols[1], jnp.where(key_pick == 2, picked_cols[2], picked_cols[3])))
    edge_row = jnp.where(lane < HALF, lane, lane - HALF)
    for p in range(3):
        a, b, share, ok = lat_split(edge_row + p, top, bottom, count, r * fr, fr * tile_rows)
        wa = jnp.where(ok, 1.0 - share, 0.0)
        wb = jnp.where(ok, share, 0.0)
        by_row = jnp.where(key_line == a, wa, 0.0) + jnp.where(key_line == b, wb, 0.0)
        for q in range(3):
            lower_col, share_m = lon_split(jnp.where(lane < HALF, q - 2, fl - 1 + q))
            by_col = jnp.where(key_col == lower_col, 1.0 - share_m, jnp.where(key_col == lower_col + 1, share_m, 0.0))
            sidew[3 * p + q] = (by_row * by_col).astype(BF16)

    own.wait()

    def arrived(slot, span_rows=whole):
        remote(pieces.at[0, pl.ds(*span_rows)], landing(slot, span_rows), send.at[0], recv.at[slot], me).wait_recv()

    def edge(slot):
        if slot < 8:
            remote(cols, got_cols.at[slot], nsend.at[slot], nrecv.at[slot], me).wait_recv()
        else:
            remote(rows.at[0], far_rows.at[slot - 8], nsend.at[slot], nrecv.at[slot], me).wait_recv()

    for k in range(1, TILE_COLS):
        arrived(2 + (c + k) % TILE_COLS)

    spare = got.shape[0] // 4
    inner = got.shape[0] - 2 * spare

    def enter(i):
        values = gather_row(got, spare + i, c, halo)
        held[i] = values
        part[0, i] = convolve(values, regc[0], regw[0])

    def update(k, i):
        return add_rows(held[i], part[k, i - 1], part[k, i], part[k, i + 1], regc[2 * k + 1])

    def follow(k, i):
        values = update(k - 1, i).astype(F32)
        held[i] = values
        part[k, i] = convolve(values, regc[2 * k], regw[k])

    lag = 3
    for i in range(inner + lag * blocks):
        if i < inner:
            enter(i)
        for k in range(1, blocks):
            if k <= i - lag * k < inner - k:
                follow(k, i - lag * k)
        row = i - lag * blocks
        if blocks <= row < inner - blocks:
            field[row - blocks] = update(blocks - 1, row)

    @pl.when(north)
    def _():
        arrived(0, lower)
        arrived(1)

    @pl.when(south)
    def _():
        arrived(6)
        arrived(7, upper)

    edge(0)
    edge(1)

    @pl.when(north)
    def _():
        for slot in (2, 3, 6, 8):
            edge(slot)

    @pl.when(south)
    def _():
        for slot in (4, 5, 7, 9):
            edge(slot)

    for n in range(nout):
        for j in range(wide):
            at = slice(j * 128 % (fl // 2), j * 128 % (fl // 2) + 128)
            row = 2 * n + 2 * nout * (j * 128 // (fl // 2))
            above = far_rows[0, :, at].astype(F32)[row:row + 2]
            below = far_rows[1, :, at].astype(F32)[row:row + 2]
            grid[j, n * tall:n * tall + 2, :] = jnp.where(top, 0.0, above)
            grid[j, n * tall + 2 + fr:(n + 1) * tall, :] = jnp.where(bottom, 0.0, below)

    each_band(lambda copy: copy.wait_send())
    each_edge(lambda copy: copy.wait_send())


def first_program(coarse, noisy, gain, regb, regs, liftb, midg, midb, lifts, mids):
    hbm = pl.BlockSpec(memory_space=pltpu.HBM)
    vmem = pl.BlockSpec(memory_space=pltpu.VMEM)
    dma = pltpu.SemaphoreType.DMA
    cin, band_rows, clon = coarse.shape
    nout, fr, fl = noisy.shape[1:]
    ch = mids.shape[1]
    blocks = regs.shape[0] // 9
    slab = 3 * cin + -(-(3 * nout + 3) // 16) * 16
    lines_n = band_rows * (TILE_COLS + 4)
    ct_lon = clon // TILE_COLS
    cw = 2 * ct_lon
    assert ct_lon == 128 and cin % 16 == 0 and band_rows == 2
    assert (cin // 16) * 2 * (blocks + 1) * TILE_COLS <= 128
    shape = jax.ShapeDtypeStruct
    return pl.pallas_call(
        first_kernel,
        out_shape=(
            shape((lines_n, cin + 16, 128), BF16),
            shape((8, 4 * nout, 128), BF16),
            shape((4 * nout, 128), BF16),
            shape((fl // 128, nout * (fr + 4), 128), F32),
            shape((blocks, 3 * cin, 3 * cin), BF16),
            shape((2 * blocks, cin, 128), F32),
            shape((ch, 3 * slab), BF16),
            shape((ch, 128), F32),
            shape((ch, 9 * ch + 16), BF16),
            shape((cw, fl), BF16),
            shape((9, 128, 128), BF16),
            shape((cw, 128), BF16),
            shape((lines_n - 2 * (lines_n // 4), cin, cw), F32),
            shape((blocks, lines_n - 2 * (lines_n // 4), 3 * cin, cw), F32),
            shape((lines_n - 2 * (lines_n // 4) - 2 * blocks, cin, cw), BF16),
        ),
        in_specs=[hbm] * 10,
        out_specs=(vmem,) * 15,
        scratch_shapes=[
            pltpu.VMEM((cin, band_rows, clon), BF16),
            pltpu.VMEM((TILE_COLS, band_rows, cin + 16, 128), BF16),
            pltpu.VMEM((nout, fr, fl), BF16),
            pltpu.VMEM((2, 4 * nout, fl // 2), BF16),
            pltpu.VMEM((2, 4 * nout, fl // 2), BF16),
            pltpu.VMEM(gain.shape, F32),
            pltpu.VMEM(regb.shape, F32),
            pltpu.VMEM((3, 1, ch), F32),
            pltpu.VMEM(regs.shape, BF16),
            pltpu.VMEM(lifts.shape, BF16),
            pltpu.VMEM(mids.shape, BF16),
            pltpu.VMEM((3 * slab, ch), BF16),
            dma((2 * TILE_COLS,)), dma((8,)), dma((10,)), dma((10,)), dma((11,)),
        ],
        compiler_params=pltpu.CompilerParams(
            collective_id=0, has_side_effects=True, vmem_limit_bytes=24_000_000),
    )(*[pltpu.with_memory_space_constraint(x, pltpu.HBM) for x in (
        coarse, noisy, gain, regb, regs, liftb, midg, midb, lifts, mids)])


def tile_kernel(
    dims, got, got_cols, own_cols, grid, regw, regc, liftw, gains, midw, lon, sidew, chosen, held_in, part_in, field_in, out,
    held, part, field, lines, upper, sides, bands, unit, raw, prod, edges, rows_out, stage, sems,
):
    cin, ch, nout, fr, fl = dims
    lines_n, count, cw = got.shape[0], field.shape[0], field.shape[2]
    blocks = regw.shape[0]
    halo = blocks + 1
    me = lax.axis_index("lat")
    tile_row, tile_rows = me // TILE_COLS, lax.axis_size("lat") // TILE_COLS
    c = me % TILE_COLS
    top, bottom = tile_row == 0, tile_row == tile_rows - 1
    steps = bands.shape[0]
    wide = fl // 128
    lane = lax.broadcasted_iota(jnp.int32, (1, 128), 1)
    lane_first, lane_last = lane == 0, lane == 127
    spare = lines_n // 4

    def known(i, values):
        if i < spare:
            return jnp.where(top, 0.0, values)
        if i >= lines_n - spare:
            return jnp.where(bottom, 0.0, values)
        return values

    def ready(k, i):
        return spare + k <= i < lines_n - spare - k

    def product(k, i):
        return part_in[k, i - spare] if ready(k, i) else part[k % 2, i]

    def enter(i):
        values = known(i, gather_row(got, i, c, halo))
        held[i] = values
        part[0, i] = convolve(values, regc[0], regw[0])

    def update(k, i):
        values = held_in[i - spare] if ready(k, i) else held[i]
        values = add_rows(values, product(k, i - 1), product(k, i), product(k, i + 1), regc[2 * k + 1])
        return known(i, values.astype(F32))

    def follow(k, i):
        values = update(k - 1, i)
        held[i] = values
        part[k % 2, i] = convolve(values, regc[2 * k], regw[k])

    def widen(first, last):
        coarse = field[first:last].reshape((last - first) * cin, cw)
        lines[first:last] = jnp.dot(coarse, lon[...], preferred_element_type=F32).reshape(last - first, cin, fl)

    def neighbours(values, seam_l, seam_r):
        parts = [values[:, j * 128:(j + 1) * 128] for j in range(wide)]
        onward = [seam_l] + [pltpu.roll(v, 1, 1) for v in parts]
        back = [pltpu.roll(v, 127, 1) for v in parts] + [seam_r]
        return (jnp.concatenate([jnp.where(lane_first, onward[j], onward[j + 1]) for j in range(wide)], axis=1),
                jnp.concatenate([jnp.where(lane_last, back[j + 1], back[j]) for j in range(wide)], axis=1))

    def blend(t):
        return lat_split(t, top, bottom, count, tile_row * fr, fr * tile_rows)

    def inside(t):
        row = tile_row * fr + t - 2
        return jnp.logical_and(row >= 0, row < fr * tile_rows)

    tall = fr + 4
    slab = upper.shape[1]

    def along(middle, above, below):
        above = jnp.where(top, 0.0, pltpu.roll(above.astype(F32), 128 - (fr - 2), 1))
        below = jnp.where(bottom, 0.0, pltpu.roll(below.astype(F32), fr + 2, 1))
        middle = pltpu.roll(middle.astype(F32), 2, 1)
        return jnp.where(lane < 2, above, jnp.where(lane < fr + 2, middle, below))

    west = along(got_cols[0], got_cols[2], got_cols[4])
    east = along(got_cols[1], got_cols[3], got_cols[5])
    here = along(own_cols[...], got_cols[6], got_cols[7])
    none = jnp.ones((slab - 3 * (cin + nout), 128), F32)
    left_cols = jnp.concatenate([west[2 * nout:], here[:nout], none], axis=0)
    right_cols = jnp.concatenate([here[3 * nout:], east[:2 * nout], none], axis=0)
    west_col, east_col = west[3 * nout:], east[:nout]

    def noise_rows(t):
        rows = [grid[j, pl.ds(t, nout, stride=tall), :] for j in range(wide)]
        onward = [pltpu.roll(v, 1, 1) for v in rows]
        back = [pltpu.roll(v, 127, 1) for v in rows]
        edge_l = pltpu.roll(west_col, (128 - t) % 128 if isinstance(t, int) else 128 - t, 1)
        edge_r = pltpu.roll(east_col, 127 - t, 1)
        pieces = []
        for j in range(wide):
            lo = jnp.where(lane_first, onward[j - 1] if j else edge_l, onward[j])
            hi = jnp.where(lane_last, back[j + 1] if j < wide - 1 else edge_r, back[j])
            pieces.append(jnp.concatenate([lo, rows[j], hi, none], axis=0))
        return jnp.concatenate(pieces, axis=1).astype(BF16)

    def raise_row(t, slot):
        a, b, share, ok = blend(jnp.int32(t))
        wa = jnp.where(ok, 1.0 - share, 0.0)
        wb = jnp.where(ok, share, 0.0)
        static = isinstance(t, int)
        for o in range(0, cin, 16):
            values = (wa * lines[a, o:o + 16, :] + wb * lines[b, o:o + 16, :]).astype(BF16)
            seam = sides[cin + o:cin + o + 16, :]
            seam_l = pltpu.roll(seam, (128 - t) % 128 if static else 128 - t, 1)
            seam_r = pltpu.roll(seam, (127 + HALF - t) % 128 if static else 127 + HALF - t, 1)
            onward, back = neighbours(values, seam_l, seam_r)
            upper[slot, o:o + 16, :] = onward
            upper[slot, cin + o:cin + o + 16, :] = values
            upper[slot, 2 * cin + o:2 * cin + o + 16, :] = back
        upper[slot, 3 * cin:slab, :] = noise_rows(t)

    edge_row = jnp.where(lane < HALF, lane, lane - HALF)

    found = {}

    def edge_pick():
        found["narrow"] = jnp.dot(field[...].reshape(count * cin, cw), chosen[...], preferred_element_type=F32)

    def edge_pack():
        packed = found["narrow"][:cin]
        for i in range(1, count):
            packed = packed + pltpu.roll(found["narrow"][i * cin:(i + 1) * cin], 4 * i, 1)
        found["packed"] = packed.astype(BF16)

    def edge_blend(p):
        for q in range(3):
            base = p * slab + q * cin
            sides[base:base + cin, :] = jnp.dot(
                found["packed"], sidew[3 * p + q], preferred_element_type=F32).astype(BF16)
        sides[p * slab + 3 * cin:(p + 1) * slab, :] = jnp.where(
            lane < HALF, pltpu.roll(left_cols, (128 - p) % 128, 1), pltpu.roll(right_cols, HALF - p, 1)).astype(BF16)

    def edge_lift():
        found["lift"] = jnp.dot(liftw[...], sides[...], preferred_element_type=F32)

    def edge_finish():
        edges[...] = jnp.where(inside(edge_row + 1), activate(found["lift"], gains[...]), 0.0).astype(BF16)

    def lift(slot, target):
        window = jnp.concatenate([upper[(slot + n) % steps] for n in range(3)], axis=0)
        raw[target % steps] = jnp.dot(liftw[...], window, preferred_element_type=F32)

    def finish(l, slot):
        squares = jnp.zeros((8, fl), F32)
        for o in range(0, ch, 16):
            values = raw[slot, o:o + 16, :]
            values = values * values
            squares = squares + (values[:8] + values[8:])
        inverse = lax.rsqrt(jnp.sum(squares, axis=0, keepdims=True) * (1.0 / ch) + EPSILON)
        inverse = jnp.where(inside(l + 1), inverse, 0.0)
        for o in range(0, ch, 16):
            half_gain = jnp.concatenate([gains[o:o + 16, :]] * wide, axis=1)
            half = raw[slot, o:o + 16, :] * inverse * half_gain
            values = (half + half * jnp.tanh(half)).astype(BF16)
            edge = edges[o:o + 16, :]
            edge_l = pltpu.roll(edge, 128 - l, 1)
            edge_r = pltpu.roll(edge, 127 + HALF - l, 1)
            onward, back = neighbours(values, edge_l, edge_r)
            bands[slot, o:o + 16, :] = onward
            bands[slot, ch + o:ch + o + 16, :] = values
            bands[slot, 2 * ch + o:2 * ch + o + 16, :] = back

    def mid(slot):
        window = jnp.concatenate([bands[(slot + n) % steps] for n in range(3)] + [unit[...]], axis=0)
        prod[slot % 2] = jnp.dot(midw[...], window, preferred_element_type=F32)

    group = stage.shape[2]
    blocks_out = ch // 8

    def flushed(n):
        return pltpu.make_async_copy(
            stage.at[n % 2], out.at[0, :, pl.ds(n * group if isinstance(n, int) else pl.multiple_of(n * group, group), group), :], sems.at[n % 2])

    def shrink(n, o, only=None):
        for j in range(wide) if only is None else (only,):
            block = rows_out[n % 2, j, pl.ds(o * 8 * group if isinstance(o, int) else pl.multiple_of(o * 8 * group, 8 * group), 8 * group), :]
            stage[n % 2, pl.ds(o * 8, 8), :, j * 128:(j + 1) * 128] = block.reshape(8, group, 128).astype(BF16)

    def emit(n, spot, slot):
        for o in range(0, ch, 16):
            for j in range(wide):
                at = slice(j * 128, (j + 1) * 128)
                total = raw[(slot + 1) % steps, o:o + 16, at] + prod[slot % 2, o:o + 16, at]
                rows_out[n % 2, j, pl.ds(spot + o * group, 16, stride=group), :] = total

    unit[...] = jnp.ones(unit.shape, BF16)

    def raised(t):
        raise_row(t, t % steps)

    def lifted(l):
        lift(l % steps, l)

    def finished(l):
        finish(jnp.int32(l), l % steps)

    def settle(row):
        field[row - halo] = update(blocks - 1, row).astype(BF16)

    def spread(lines_at):
        widen(*lines_at)

    held_lines = lines_n - 2 * spare - 2 * blocks
    low = spare + blocks - halo
    for n in range(held_lines):
        field[low + n] = field_in[n]
    plan = []
    for k in range(blocks):
        for i in range(1 + k, lines_n - 1 - k):
            if not ready(k, i):
                plan.append((functools.partial(follow, k) if k else enter, i))
        if k == 0:
            plan.insert(3, (spread, (low, low + held_lines // 2)))
            plan.append((spread, (low + held_lines // 2, low + held_lines)))
    plan += [(settle, i) for i in range(halo, spare + blocks)] + [(spread, (0, low))]
    plan += [(settle, i) for i in range(lines_n - spare - blocks, lines_n - halo)] + [(spread, (low + held_lines, count))]
    plan += [(lambda _: edge_pick(), 0), (lambda _: edge_pack(), 0), (edge_blend, 0), (raised, 0), (edge_blend, 1), (raised, 1),
             (edge_blend, 2), (raised, 2), (lifted, 0), (raised, 3), (lambda _: edge_lift(), 0), (lifted, 1), (raised, 4),
             (lifted, 2), (raised, 5), (lambda _: edge_finish(), 0), (lifted, 3), (raised, 6), (finished, 0),
             (lifted, 4), (raised, 7), (finished, 1), (finished, 2), (mid, 0), (finished, 3)]
    for action, n in plan:
        action(n)

    halves = group // steps
    share_out = blocks_out // group

    def step(i, u, e, last):
        n = i // halves
        shrink_at = (i % halves) * (blocks_out // halves) + u * share_out
        emit(n, (i % halves) * steps + u, u)
        for o in range(share_out):
            shrink(n + 1, shrink_at + o)
        if last is None:
            raise_row(e + 8, u)
        if last is None or last + 4 < fr + 2:
            finish(e + 4, (u + 4) % steps)
        if last is None or last + 1 < fr:
            mid((u + 1) % steps)
        if last is None or last + 5 < fr + 2:
            lift((u + 5) % steps, u + 5)

    trips = fr // steps

    def begin(i):
        @pl.when(jnp.logical_and(i % halves == 0, i >= 3 * halves))
        def _():
            flushed(i // halves - 3).wait()

    def finish_trip(i):
        @pl.when(jnp.logical_and(i % halves == halves - 1, i >= halves))
        def _():
            flushed(i // halves - 1).start()

    def trip(i, _):
        begin(i)
        for u in range(steps):
            step(i, u, i * steps + u, None)
        finish_trip(i)
        return 0

    lax.fori_loop(0, trips - 1, trip, 0)
    groups = fr // group
    last = groups - 1
    if groups >= 3:
        flushed(groups - 3).wait()
    for u in range(steps):
        step(trips - 1, u, (trips - 1) * steps + u, fr - steps + u)
    if groups >= 2:
        flushed(groups - 2).start()
    parts = [pltpu.make_async_copy(
        stage.at[last % 2, pl.ds(h * ch // 4, ch // 4)],
        out.at[0, pl.ds(h * ch // 4, ch // 4), pl.ds(last * group, group), :], sems.at[2 + h]) for h in range(4)]
    for h in range(4):
        for o in range(blocks_out // 4):
            shrink(last, h * (blocks_out // 4) + o)
        parts[h].start()
    if groups >= 2:
        flushed(groups - 2).wait()
    for copy in parts:
        copy.wait()


def tile_program(dims, prepared):
    cin, ch, nout, fr, fl = dims
    got, lon, liftw = prepared[0], prepared[9], prepared[6]
    lines_n = got.shape[0]
    cw = lon.shape[0]
    blocks = prepared[4].shape[0]
    count = lines_n - 2 * (blocks + 1)
    group = 8
    steps = 4
    vmem = pl.BlockSpec(memory_space=pltpu.VMEM)
    slab = liftw.shape[1] // 3
    return pl.pallas_call(
        functools.partial(tile_kernel, dims),
        out_shape=jax.ShapeDtypeStruct((1, ch, fr, fl), BF16),
        in_specs=[vmem] * len(prepared),
        out_specs=pl.BlockSpec(memory_space=pl.ANY),
        scratch_shapes=[
            pltpu.VMEM((lines_n, cin, cw), F32),
            pltpu.VMEM((2, lines_n, 3 * cin, cw), F32),
            pltpu.VMEM((count, cin, cw), BF16),
            pltpu.VMEM((count, cin, fl), F32),
            pltpu.VMEM((steps, slab, fl), BF16),
            pltpu.VMEM((3 * slab, 128), BF16),
            pltpu.VMEM((steps, 3 * ch, fl), BF16),
            pltpu.VMEM((16, fl), BF16),
            pltpu.VMEM((steps, ch, fl), F32),
            pltpu.VMEM((2, ch, fl), F32),
            pltpu.VMEM((ch, 128), BF16),
            pltpu.VMEM((2, fl // 128, ch * group, 128), F32),
            pltpu.VMEM((2, ch, group, fl), BF16),
            pltpu.SemaphoreType.DMA((6,)),
        ],
        compiler_params=pltpu.CompilerParams(vmem_limit_bytes=44_000_000),
    )(*prepared)


def per_device(
    coarse, reg_gain, reg_weight, reg_bias, noisy, lift_weight, lift_bias, mid_gain, mid_weight, mid_bias,
):
    lifts = lift_weight.transpose(0, 1, 3, 2)
    prepared = first_program(
        coarse, noisy, reg_gain, reg_bias, reg_weight.reshape((-1,) + reg_weight.shape[3:]),
        lift_bias[None], mid_gain[None], mid_bias[None],
        lifts.reshape((9,) + lifts.shape[2:]), mid_weight.reshape((9,) + mid_weight.shape[2:]))
    return tile_program((coarse.shape[0], mid_weight.shape[2]) + noisy.shape[1:], prepared)


def solution(mesh):
    placed = (
        P(None, ("grp", "lat"), None),
        P(),
        P(),
        P(),
        P(("grp", "lat"), None, None, None),
        P(),
        P(),
        P(),
        P(),
        P(),
    )
    return jax.shard_map(
        per_device,
        mesh=mesh,
        in_specs=placed,
        out_specs=P(("grp", "lat"), None, None, None),
        check_vma=False,
    )
```

```python
import functools

import jax
import jax.numpy as jnp
from jax import lax
from jax.experimental import pallas as pl
from jax.experimental.pallas import tpu as pltpu
from jax.sharding import PartitionSpec as P

TILE_COLS = 4
LAT_UP = 4
LON_UP = 4
EPSILON = 1e-06
F32 = jnp.float32
BF16 = jnp.bfloat16
MESH = pl.DeviceIdType.MESH
HALF = 64


def activate(values, half_gain):
    inverse = lax.rsqrt(jnp.mean(values * values, axis=0, keepdims=True) + EPSILON)
    half = values * inverse * half_gain
    return half + half * jnp.tanh(half)


def split(numerator, factor):
    lower = numerator // (2 * factor)
    return lower, (numerator - 2 * factor * lower).astype(F32) / (2.0 * factor)


def column(row):
    n = row.shape[1]
    here = lax.broadcasted_iota(jnp.int32, (n, n), 0) == lax.broadcasted_iota(jnp.int32, (n, n), 1)
    return jnp.broadcast_to(jnp.sum(jnp.where(here, row, 0.0), axis=1, keepdims=True), (n, 128))


def thirds(values):
    high = values.astype(BF16).astype(F32)
    middle = (values - high).astype(BF16).astype(F32)
    return [high, middle, values - high - middle]


def nt_dot(a, b):
    return lax.dot_general(a, b, (((1,), (1,)), ((), ())), preferred_element_type=F32)


def lon_split(fine_col):
    lower, part = split(2 * fine_col + 1 - LON_UP + 2 * LON_UP, LON_UP)
    return lower - 1, part


def lat_split(t, top, bottom, count, start, total):
    lower, part = split(2 * (t - 2) + 1 - LAT_UP + 2 * LAT_UP, LAT_UP)
    low_line = jnp.where(top, 1, 0)
    high_line = jnp.where(bottom, count - 2, count - 1)
    row = start + t - 2
    ok = jnp.logical_and(row >= 0, row < total)
    return jnp.clip(lower, low_line, high_line), jnp.clip(lower + 1, low_line, high_line), part, ok


def gather_row(got, i, c, halo):
    cin = got.shape[1] - 16
    lane = lax.broadcasted_iota(jnp.int32, (1, 128), 1)
    span = 2 * halo * TILE_COLS
    side = got[i, cin:, :].astype(F32)
    outer = []
    for g in range(cin // 16):
        after = pltpu.roll(side, 128 - halo - g * span - 2 * halo * ((c + 1) % TILE_COLS), 1)
        before = pltpu.roll(side, 128 - halo - g * span - 2 * halo * c, 1)
        outer.append(jnp.where(lane < halo, after, jnp.where(lane >= 128 - halo, before, 0.0)))
    return jnp.concatenate([got[i, :cin, :].astype(F32), jnp.concatenate(outer, axis=0)], axis=1)


def convolve(values, half_gain, weight):
    cw = values.shape[1]
    values = activate(values, half_gain[:, :1])
    taps = jnp.concatenate(
        [pltpu.roll(values, 1, 1).astype(BF16), values.astype(BF16), pltpu.roll(values, cw - 1, 1).astype(BF16)],
        axis=0)
    return jnp.dot(weight, taps, preferred_element_type=F32)


def add_rows(values, above, here, below, bias):
    cin = values.shape[0]
    return (values + above[:cin] + here[cin:2 * cin] + below[2 * cin:] + bias[:, :1]).astype(BF16)


def first_kernel(
    coarse, noisy, gain, regb, regs, liftb, midg, midb, lifts, mids,
    got, got_cols, cols, grid, regw, regc, liftw, liftc, midw, lon, sidew, chosen, held, part, field,
    band, pieces, tile, rows, far_rows, gainv, regbv, vecs, regv, liftv, midv, liftt,
    send, recv, nsend, nrecv, local,
):
    me = lax.axis_index("lat")
    tile_rows = lax.axis_size("lat") // TILE_COLS
    r = me // TILE_COLS
    c = me % TILE_COLS
    north, south = r > 0, r < tile_rows - 1
    top, bottom = r == 0, r == tile_rows - 1
    cin, band_rows, clon = band.shape
    ch = midv.shape[1]
    nout, fr, fl = tile.shape
    blocks = regw.shape[0]
    halo = blocks + 1
    span = 2 * halo * TILE_COLS
    cw = chosen.shape[0]
    count = got.shape[0] - 2 * halo

    barrier = pltpu.get_barrier_semaphore()

    def greet(target):
        pl.semaphore_signal(barrier, inc=1, device_id={"lat": target}, device_id_type=MESH)

    for k in range(1, TILE_COLS):
        greet(r * TILE_COLS + (c + k) % TILE_COLS)

    @pl.when(north)
    def _():
        for k in range(TILE_COLS):
            greet((r - 1) * TILE_COLS + k)

    @pl.when(south)
    def _():
        for k in range(TILE_COLS):
            greet((r + 1) * TILE_COLS + k)

    loads = [
        pltpu.make_async_copy(coarse, band, local.at[0]),
        pltpu.make_async_copy(noisy.at[0], tile, local.at[1]),
        pltpu.make_async_copy(regs, regv, local.at[2]),
        pltpu.make_async_copy(mids, midv, local.at[3]),
        pltpu.make_async_copy(lifts, liftv, local.at[4]),
        pltpu.make_async_copy(gain, gainv, local.at[6]),
        pltpu.make_async_copy(regb, regbv, local.at[7]),
        pltpu.make_async_copy(liftb, vecs.at[0], local.at[8]),
        pltpu.make_async_copy(midg, vecs.at[1], local.at[9]),
        pltpu.make_async_copy(midb, vecs.at[2], local.at[10]),
    ]
    for load in loads:
        load.start()

    lane = lax.broadcasted_iota(jnp.int32, (1, 128), 1)
    both = band_rows * cin
    row_id = lax.broadcasted_iota(jnp.int32, (both, both), 0)
    sub_id = jnp.where(row_id >= cin, 1, 0)
    order = lax.broadcasted_iota(jnp.int32, (both, both), 1) == band_rows * (row_id - sub_id * cin) + sub_id
    order = jnp.where(order, 1.0, 0.0).astype(BF16)
    loads[0].wait()
    sorted_rows = jnp.dot(order, band[...].reshape(both, clon), preferred_element_type=F32)
    for sub in range(band_rows):
        row = sorted_rows[sub * cin:(sub + 1) * cin]
        parts = [row[:, b * 128:(b + 1) * 128] for b in range(TILE_COLS)]
        for b in range(TILE_COLS):
            pieces[b, sub, :cin, :] = parts[b].astype(BF16)
        side = jnp.zeros((16, 128), F32)
        for b in range(TILE_COLS):
            seam = jnp.where(lane < 64, parts[b], parts[(b + TILE_COLS - 1) % TILE_COLS])
            for g in range(cin // 16):
                at = g * span + 2 * halo * b
                moved = pltpu.roll(seam[g * 16:(g + 1) * 16], at + halo, 1)
                side = jnp.where(jnp.logical_and(lane >= at, lane < at + 2 * halo), moved, side)
        for b in range(TILE_COLS):
            pieces[b, sub, cin:, :] = side.astype(BF16)

    loads[1].wait()
    for side, first in ((0, 0), (1, fr - 2)):
        lines = jnp.concatenate([tile[n, first:first + 2, :].astype(F32) for n in range(nout)], axis=0)
        rows[side] = jnp.concatenate([lines[:, :fl // 2], lines[:, fl // 2:]], axis=0).astype(BF16)
    pick_row = lax.broadcasted_iota(jnp.int32, (4 * nout, 128), 0)
    pick_lane = lax.broadcasted_iota(jnp.int32, (4 * nout, 128), 1)
    packed = jnp.zeros((4 * nout, fr), F32)
    for n in range(nout):
        for s, (lo, at) in enumerate(((0, 0), (0, 1), (fl - 128, 126), (fl - 128, 127))):
            if s % 2 == 0:
                hit = jnp.zeros(pick_row.shape, jnp.bool_)
            hit = jnp.logical_or(hit, jnp.logical_and(pick_row == s * nout + n, pick_lane == at))
            if s % 2:
                packed = packed + nt_dot(jnp.where(hit, 1.0, 0.0).astype(BF16), tile[n, :, lo:lo + 128])
    cols[...] = jnp.concatenate([packed, jnp.zeros((4 * nout, 128 - fr), F32)], axis=1).astype(BF16)

    peers = TILE_COLS - 1 + jnp.where(north, TILE_COLS, 0) + jnp.where(south, TILE_COLS, 0)
    pl.semaphore_wait(barrier, peers)

    def remote(src, dst, ssem, rsem, target):
        return pltpu.make_async_remote_copy(
            src_ref=src, dst_ref=dst, send_sem=ssem, recv_sem=rsem,
            device_id={"lat": target}, device_id_type=MESH)

    whole, upper, lower = (0, 2), (0, 1), (1, 1)

    def landing(slot, span_rows):
        return got.at[pl.ds(2 * slot + span_rows[0], span_rows[1])]

    def far_first(k):
        return ((c // 2) * 2 + 2 + k) % TILE_COLS

    def beside():
        return c + 1 - 2 * (c % 2)

    def band_copy(k, row, slot, ssem, span_rows=whole):
        col = far_first(k)
        return remote(pieces.at[col, pl.ds(*span_rows)], landing(slot, span_rows), send.at[ssem], recv.at[slot],
                      row * TILE_COLS + col)

    west, east = (c + TILE_COLS - 1) % TILE_COLS, (c + 1) % TILE_COLS

    def col_copy(slot, row, col):
        return remote(cols, got_cols.at[slot], nsend.at[slot], nrecv.at[slot], row * TILE_COLS + col)

    def row_copy(slot, row):
        return remote(rows.at[1 - slot], far_rows.at[slot], nsend.at[8 + slot], nrecv.at[8 + slot], row * TILE_COLS + c)

    def each_band(action):
        for col, side, row, slot, span_rows in (
            (2, south, r + 1, 0, lower), (3, south, r + 1, 1, whole),
            (0, north, r - 1, 6, whole), (1, north, r - 1, 7, upper),
        ):
            @pl.when(jnp.logical_and(side, c == col))
            def _():
                for k in range(TILE_COLS):
                    action(band_copy(k, row, slot, TILE_COLS + k, span_rows))

        for k in range(TILE_COLS - 2):
            action(band_copy(k, r, 2 + c, k))
        action(remote(pieces.at[beside(), pl.ds(0, 2)], landing(2 + c, whole), send.at[2], recv.at[2 + c],
                      r * TILE_COLS + beside()))

    def each_edge(action):
        action(col_copy(0, r, east))
        action(col_copy(1, r, west))

        @pl.when(south)
        def _():
            action(row_copy(0, r + 1))
            action(col_copy(6, r + 1, c))
            action(col_copy(2, r + 1, east))
            action(col_copy(3, r + 1, west))

        @pl.when(north)
        def _():
            action(row_copy(1, r - 1))
            action(col_copy(7, r - 1, c))
            action(col_copy(4, r - 1, east))
            action(col_copy(5, r - 1, west))

    each_band(lambda copy: copy.start())
    own = pltpu.make_async_copy(pieces.at[c], landing(2 + c, whole), local.at[5])
    own.start()
    each_edge(lambda copy: copy.start())

    loads[2].wait()
    for k in range(blocks):
        for p in range(3):
            for q in range(3):
                regw[k, p * cin:(p + 1) * cin, q * cin:(q + 1) * cin] = regv[9 * k + 3 * p + q]

    loads[3].wait()
    for tap in range(9):
        midw[:, tap * ch:(tap + 1) * ch] = midv[tap]
    for load in loads[4:]:
        load.wait()
    slab = liftt.shape[0] // 3
    for p in range(3):
        noise = []
        for q in range(3):
            base = p * slab + q * cin
            liftt[base:base + cin, :] = liftv[3 * p + q, :cin, :]
            noise.append(liftv[3 * p + q, cin:, :].astype(F32))
        spare_rows = slab - 3 * (cin + nout)
        if p == 1:
            noise += thirds(vecs[0]) + [jnp.zeros((spare_rows - 3, ch), F32)]
        else:
            noise.append(jnp.zeros((spare_rows, ch), F32))
        liftt[p * slab + 3 * cin:(p + 1) * slab, :] = jnp.concatenate(noise, axis=0).astype(BF16)
    eye = jnp.where(lax.broadcasted_iota(jnp.int32, (ch, ch), 0) == lax.broadcasted_iota(jnp.int32, (ch, ch), 1), 1.0, 0.0)
    liftw[...] = nt_dot(eye.astype(BF16), liftt[...]).astype(BF16)

    low, weight = lon_split(lax.broadcasted_iota(jnp.int32, (1, fl), 1))
    low_lane = jnp.where(low < 0, low + cw, low)
    high_lane = jnp.where(low + 1 < 0, low + 1 + cw, low + 1)
    coarse_lane = lax.broadcasted_iota(jnp.int32, (cw, fl), 0)
    lon[...] = jnp.where(coarse_lane == low_lane, 1.0 - weight,
                         jnp.where(coarse_lane == high_lane, weight, 0.0)).astype(BF16)

    for k in range(blocks):
        regc[2 * k] = column(gainv[k:k + 1, :]) * 0.5
        regc[2 * k + 1] = column(regbv[k:k + 1, :])
    liftc[...] = column(vecs[1]) * 0.5
    bias_cols = jnp.zeros((ch, 128), F32)
    for n, third in enumerate(thirds(column(vecs[2]))):
        bias_cols = jnp.where(lane == n, third, bias_cols)
    midw[:, 9 * ch:] = bias_cols[:, :16].astype(BF16)

    tall = fr + 4
    wide = fl // 128
    for n in range(nout):
        for j in range(wide):
            grid[j, n * tall + 2:n * tall + 2 + fr, :] = tile[n, :, j * 128:(j + 1) * 128].astype(F32)

    near = fl // LON_UP
    picked_cols = [-1, 0, near - 1, near]
    select_lane = lax.broadcasted_iota(jnp.int32, (cw, 128), 0)
    select_pos = lax.broadcasted_iota(jnp.int32, (cw, 128), 1)
    hits = jnp.zeros((cw, 128), jnp.bool_)
    for s, col in enumerate(picked_cols):
        hits = jnp.logical_or(hits, jnp.logical_and(select_pos == s, select_lane == col % cw))
    chosen[...] = jnp.where(hits, 1.0, 0.0).astype(BF16)
    key = lax.broadcasted_iota(jnp.int32, (128, 1), 0)
    key_line = key // 4
    key_pick = key - 4 * key_line
    key_col = jnp.where(key_pick == 0, picked_cols[0], jnp.where(
        key_pick == 1, picked_cols[1], jnp.where(key_pick == 2, picked_cols[2], picked_cols[3])))
    edge_row = jnp.where(lane < HALF, lane, lane - HALF)
    for p in range(3):
        a, b, share, ok = lat_split(edge_row + p, top, bottom, count, r * fr, fr * tile_rows)
        wa = jnp.where(ok, 1.0 - share, 0.0)
        wb = jnp.where(ok, share, 0.0)
        by_row = jnp.where(key_line == a, wa, 0.0) + jnp.where(key_line == b, wb, 0.0)
        for q in range(3):
            lower_col, share_m = lon_split(jnp.where(lane < HALF, q - 2, fl - 1 + q))
            by_col = jnp.where(key_col == lower_col, 1.0 - share_m, jnp.where(key_col == lower_col + 1, share_m, 0.0))
            sidew[3 * p + q] = (by_row * by_col).astype(BF16)

    own.wait()

    def arrived(slot, span_rows=whole):
        remote(pieces.at[0, pl.ds(*span_rows)], landing(slot, span_rows), send.at[0], recv.at[slot], me).wait_recv()

    def edge(slot):
        if slot < 8:
            remote(cols, got_cols.at[slot], nsend.at[slot], nrecv.at[slot], me).wait_recv()
        else:
            remote(rows.at[0], far_rows.at[slot - 8], nsend.at[slot], nrecv.at[slot], me).wait_recv()

    for k in range(1, TILE_COLS):
        arrived(2 + (c + k) % TILE_COLS)

    spare = got.shape[0] // 4
    inner = got.shape[0] - 2 * spare

    def enter(i):
        values = gather_row(got, spare + i, c, halo)
        held[i] = values
        part[0, i] = convolve(values, regc[0], regw[0])

    def update(k, i):
        return add_rows(held[i], part[k, i - 1], part[k, i], part[k, i + 1], regc[2 * k + 1])

    def follow(k, i):
        values = update(k - 1, i).astype(F32)
        held[i] = values
        part[k, i] = convolve(values, regc[2 * k], regw[k])

    lag = 3
    for i in range(inner + lag * blocks):
        if i < inner:
            enter(i)
        for k in range(1, blocks):
            if k <= i - lag * k < inner - k:
                follow(k, i - lag * k)
        row = i - lag * blocks
        if blocks <= row < inner - blocks:
            field[row - blocks] = update(blocks - 1, row)

    each_band(lambda copy: copy.wait_send())
    each_edge(lambda copy: copy.wait_send())

    @pl.when(north)
    def _():
        arrived(0, lower)
        arrived(1)

    @pl.when(south)
    def _():
        arrived(6)
        arrived(7, upper)

    edge(0)
    edge(1)

    @pl.when(north)
    def _():
        for slot in (2, 3, 6, 8):
            edge(slot)

    @pl.when(south)
    def _():
        for slot in (4, 5, 7, 9):
            edge(slot)

    for n in range(nout):
        for j in range(wide):
            at = slice(j * 128 % (fl // 2), j * 128 % (fl // 2) + 128)
            row = 2 * n + 2 * nout * (j * 128 // (fl // 2))
            above = far_rows[0, :, at].astype(F32)[row:row + 2]
            below = far_rows[1, :, at].astype(F32)[row:row + 2]
            grid[j, n * tall:n * tall + 2, :] = jnp.where(top, 0.0, above)
            grid[j, n * tall + 2 + fr:(n + 1) * tall, :] = jnp.where(bottom, 0.0, below)


def first_program(coarse, noisy, gain, regb, regs, liftb, midg, midb, lifts, mids):
    hbm = pl.BlockSpec(memory_space=pltpu.HBM)
    vmem = pl.BlockSpec(memory_space=pltpu.VMEM)
    dma = pltpu.SemaphoreType.DMA
    cin, band_rows, clon = coarse.shape
    nout, fr, fl = noisy.shape[1:]
    ch = mids.shape[1]
    blocks = regs.shape[0] // 9
    slab = 3 * cin + -(-(3 * nout + 3) // 16) * 16
    lines_n = band_rows * (TILE_COLS + 4)
    ct_lon = clon // TILE_COLS
    cw = 2 * ct_lon
    assert ct_lon == 128 and cin % 16 == 0 and band_rows == 2
    assert (cin // 16) * 2 * (blocks + 1) * TILE_COLS <= 128
    shape = jax.ShapeDtypeStruct
    return pl.pallas_call(
        first_kernel,
        out_shape=(
            shape((lines_n, cin + 16, 128), BF16),
            shape((8, 4 * nout, 128), BF16),
            shape((4 * nout, 128), BF16),
            shape((fl // 128, nout * (fr + 4), 128), F32),
            shape((blocks, 3 * cin, 3 * cin), BF16),
            shape((2 * blocks, cin, 128), F32),
            shape((ch, 3 * slab), BF16),
            shape((ch, 128), F32),
            shape((ch, 9 * ch + 16), BF16),
            shape((cw, fl), BF16),
            shape((9, 128, 128), BF16),
            shape((cw, 128), BF16),
            shape((lines_n - 2 * (lines_n // 4), cin, cw), F32),
            shape((blocks, lines_n - 2 * (lines_n // 4), 3 * cin, cw), F32),
            shape((lines_n - 2 * (lines_n // 4) - 2 * blocks, cin, cw), BF16),
        ),
        in_specs=[hbm] * 10,
        out_specs=(vmem,) * 15,
        scratch_shapes=[
            pltpu.VMEM((cin, band_rows, clon), BF16),
            pltpu.VMEM((TILE_COLS, band_rows, cin + 16, 128), BF16),
            pltpu.VMEM((nout, fr, fl), BF16),
            pltpu.VMEM((2, 4 * nout, fl // 2), BF16),
            pltpu.VMEM((2, 4 * nout, fl // 2), BF16),
            pltpu.VMEM(gain.shape, F32),
            pltpu.VMEM(regb.shape, F32),
            pltpu.VMEM((3, 1, ch), F32),
            pltpu.VMEM(regs.shape, BF16),
            pltpu.VMEM(lifts.shape, BF16),
            pltpu.VMEM(mids.shape, BF16),
            pltpu.VMEM((3 * slab, ch), BF16),
            dma((2 * TILE_COLS,)), dma((8,)), dma((10,)), dma((10,)), dma((11,)),
        ],
        compiler_params=pltpu.CompilerParams(
            collective_id=0, has_side_effects=True, vmem_limit_bytes=24_000_000),
    )(*[pltpu.with_memory_space_constraint(x, pltpu.HBM) for x in (
        coarse, noisy, gain, regb, regs, liftb, midg, midb, lifts, mids)])


def tile_kernel(
    dims, got, got_cols, own_cols, grid, regw, regc, liftw, gains, midw, lon, sidew, chosen, held_in, part_in, field_in, out,
    held, part, field, lines, upper, sides, bands, unit, raw, prod, edges, rows_out, stage, sems,
):
    cin, ch, nout, fr, fl = dims
    lines_n, count, cw = got.shape[0], field.shape[0], field.shape[2]
    blocks = regw.shape[0]
    halo = blocks + 1
    me = lax.axis_index("lat")
    tile_row, tile_rows = me // TILE_COLS, lax.axis_size("lat") // TILE_COLS
    c = me % TILE_COLS
    top, bottom = tile_row == 0, tile_row == tile_rows - 1
    steps = bands.shape[0]
    wide = fl // 128
    lane = lax.broadcasted_iota(jnp.int32, (1, 128), 1)
    lane_first, lane_last = lane == 0, lane == 127
    spare = lines_n // 4

    def known(i, values):
        if i < spare:
            return jnp.where(top, 0.0, values)
        if i >= lines_n - spare:
            return jnp.where(bottom, 0.0, values)
        return values

    def ready(k, i):
        return spare + k <= i < lines_n - spare - k

    def product(k, i):
        return part_in[k, i - spare] if ready(k, i) else part[k % 2, i]

    def enter(i):
        values = known(i, gather_row(got, i, c, halo))
        held[i] = values
        part[0, i] = convolve(values, regc[0], regw[0])

    def update(k, i):
        values = held_in[i - spare] if ready(k, i) else held[i]
        values = add_rows(values, product(k, i - 1), product(k, i), product(k, i + 1), regc[2 * k + 1])
        return known(i, values.astype(F32))

    def follow(k, i):
        values = update(k - 1, i)
        held[i] = values
        part[k % 2, i] = convolve(values, regc[2 * k], regw[k])

    def widen(first, last):
        coarse = field[first:last].reshape((last - first) * cin, cw)
        lines[first:last] = jnp.dot(coarse, lon[...], preferred_element_type=F32).reshape(last - first, cin, fl)

    def neighbours(values, seam_l, seam_r):
        parts = [values[:, j * 128:(j + 1) * 128] for j in range(wide)]
        onward = [seam_l] + [pltpu.roll(v, 1, 1) for v in parts]
        back = [pltpu.roll(v, 127, 1) for v in parts] + [seam_r]
        return (jnp.concatenate([jnp.where(lane_first, onward[j], onward[j + 1]) for j in range(wide)], axis=1),
                jnp.concatenate([jnp.where(lane_last, back[j + 1], back[j]) for j in range(wide)], axis=1))

    def blend(t):
        return lat_split(t, top, bottom, count, tile_row * fr, fr * tile_rows)

    def inside(t):
        row = tile_row * fr + t - 2
        return jnp.logical_and(row >= 0, row < fr * tile_rows)

    tall = fr + 4
    slab = upper.shape[1]

    def along(middle, above, below):
        above = jnp.where(top, 0.0, pltpu.roll(above.astype(F32), 128 - (fr - 2), 1))
        below = jnp.where(bottom, 0.0, pltpu.roll(below.astype(F32), fr + 2, 1))
        middle = pltpu.roll(middle.astype(F32), 2, 1)
        return jnp.where(lane < 2, above, jnp.where(lane < fr + 2, middle, below))

    west = along(got_cols[0], got_cols[2], got_cols[4])
    east = along(got_cols[1], got_cols[3], got_cols[5])
    here = along(own_cols[...], got_cols[6], got_cols[7])
    none = jnp.ones((slab - 3 * (cin + nout), 128), F32)
    left_cols = jnp.concatenate([west[2 * nout:], here[:nout], none], axis=0)
    right_cols = jnp.concatenate([here[3 * nout:], east[:2 * nout], none], axis=0)
    west_col, east_col = west[3 * nout:], east[:nout]

    def noise_rows(t):
        rows = [grid[j, pl.ds(t, nout, stride=tall), :] for j in range(wide)]
        onward = [pltpu.roll(v, 1, 1) for v in rows]
        back = [pltpu.roll(v, 127, 1) for v in rows]
        edge_l = pltpu.roll(west_col, (128 - t) % 128 if isinstance(t, int) else 128 - t, 1)
        edge_r = pltpu.roll(east_col, 127 - t, 1)
        pieces = []
        for j in range(wide):
            lo = jnp.where(lane_first, onward[j - 1] if j else edge_l, onward[j])
            hi = jnp.where(lane_last, back[j + 1] if j < wide - 1 else edge_r, back[j])
            pieces.append(jnp.concatenate([lo, rows[j], hi, none], axis=0))
        return jnp.concatenate(pieces, axis=1).astype(BF16)

    def raise_row(t, slot):
        a, b, share, ok = blend(jnp.int32(t))
        wa = jnp.where(ok, 1.0 - share, 0.0)
        wb = jnp.where(ok, share, 0.0)
        static = isinstance(t, int)
        for o in range(0, cin, 16):
            values = (wa * lines[a, o:o + 16, :] + wb * lines[b, o:o + 16, :]).astype(BF16)
            seam = sides[cin + o:cin + o + 16, :]
            seam_l = pltpu.roll(seam, (128 - t) % 128 if static else 128 - t, 1)
            seam_r = pltpu.roll(seam, (127 + HALF - t) % 128 if static else 127 + HALF - t, 1)
            onward, back = neighbours(values, seam_l, seam_r)
            upper[slot, o:o + 16, :] = onward
            upper[slot, cin + o:cin + o + 16, :] = values
            upper[slot, 2 * cin + o:2 * cin + o + 16, :] = back
        upper[slot, 3 * cin:slab, :] = noise_rows(t)

    edge_row = jnp.where(lane < HALF, lane, lane - HALF)

    found = {}

    def edge_pick():
        found["narrow"] = jnp.dot(field[...].reshape(count * cin, cw), chosen[...], preferred_element_type=F32)

    def edge_pack():
        packed = found["narrow"][:cin]
        for i in range(1, count):
            packed = packed + pltpu.roll(found["narrow"][i * cin:(i + 1) * cin], 4 * i, 1)
        found["packed"] = packed.astype(BF16)

    def edge_blend(p):
        for q in range(3):
            base = p * slab + q * cin
            sides[base:base + cin, :] = jnp.dot(
                found["packed"], sidew[3 * p + q], preferred_element_type=F32).astype(BF16)
        sides[p * slab + 3 * cin:(p + 1) * slab, :] = jnp.where(
            lane < HALF, pltpu.roll(left_cols, (128 - p) % 128, 1), pltpu.roll(right_cols, HALF - p, 1)).astype(BF16)

    def edge_lift():
        found["lift"] = jnp.dot(liftw[...], sides[...], preferred_element_type=F32)

    def edge_finish():
        edges[...] = jnp.where(inside(edge_row + 1), activate(found["lift"], gains[...]), 0.0).astype(BF16)

    def lift(slot, target):
        window = jnp.concatenate([upper[(slot + n) % steps] for n in range(3)], axis=0)
        raw[target % steps] = jnp.dot(liftw[...], window, preferred_element_type=F32)

    def finish(l, slot):
        squares = jnp.zeros((8, fl), F32)
        for o in range(0, ch, 16):
            values = raw[slot, o:o + 16, :]
            values = values * values
            squares = squares + (values[:8] + values[8:])
        inverse = lax.rsqrt(jnp.sum(squares, axis=0, keepdims=True) * (1.0 / ch) + EPSILON)
        inverse = jnp.where(inside(l + 1), inverse, 0.0)
        for o in range(0, ch, 16):
            half_gain = jnp.concatenate([gains[o:o + 16, :]] * wide, axis=1)
            half = raw[slot, o:o + 16, :] * inverse * half_gain
            values = (half + half * jnp.tanh(half)).astype(BF16)
            edge = edges[o:o + 16, :]
            edge_l = pltpu.roll(edge, 128 - l, 1)
            edge_r = pltpu.roll(edge, 127 + HALF - l, 1)
            onward, back = neighbours(values, edge_l, edge_r)
            bands[slot, o:o + 16, :] = onward
            bands[slot, ch + o:ch + o + 16, :] = values
            bands[slot, 2 * ch + o:2 * ch + o + 16, :] = back

    def mid(slot):
        window = jnp.concatenate([bands[(slot + n) % steps] for n in range(3)] + [unit[...]], axis=0)
        prod[slot % 2] = jnp.dot(midw[...], window, preferred_element_type=F32)

    group = stage.shape[2]
    blocks_out = ch // 8

    def flushed(n):
        return pltpu.make_async_copy(
            stage.at[n % 2], out.at[0, :, pl.ds(n * group if isinstance(n, int) else pl.multiple_of(n * group, group), group), :], sems.at[n % 2])

    def shrink(n, o, only=None):
        for j in range(wide) if only is None else (only,):
            block = rows_out[n % 2, j, pl.ds(o * 8 * group if isinstance(o, int) else pl.multiple_of(o * 8 * group, 8 * group), 8 * group), :]
            stage[n % 2, pl.ds(o * 8, 8), :, j * 128:(j + 1) * 128] = block.reshape(8, group, 128).astype(BF16)

    def emit(n, spot, slot):
        for o in range(0, ch, 16):
            for j in range(wide):
                at = slice(j * 128, (j + 1) * 128)
                total = raw[(slot + 1) % steps, o:o + 16, at] + prod[slot % 2, o:o + 16, at]
                rows_out[n % 2, j, pl.ds(spot + o * group, 16, stride=group), :] = total

    unit[...] = jnp.ones(unit.shape, BF16)

    def raised(t):
        raise_row(t, t % steps)

    def lifted(l):
        lift(l % steps, l)

    def finished(l):
        finish(jnp.int32(l), l % steps)

    def settle(row):
        field[row - halo] = update(blocks - 1, row).astype(BF16)

    def spread(lines_at):
        widen(*lines_at)

    held_lines = lines_n - 2 * spare - 2 * blocks
    low = spare + blocks - halo
    for n in range(held_lines):
        field[low + n] = field_in[n]
    plan = []
    for k in range(blocks):
        for i in range(1 + k, lines_n - 1 - k):
            if not ready(k, i):
                plan.append((functools.partial(follow, k) if k else enter, i))
        if k == 0:
            plan.insert(3, (spread, (low, low + held_lines // 2)))
            plan.append((spread, (low + held_lines // 2, low + held_lines)))
    plan += [(settle, i) for i in range(halo, spare + blocks)] + [(spread, (0, low))]
    plan += [(settle, i) for i in range(lines_n - spare - blocks, lines_n - halo)] + [(spread, (low + held_lines, count))]
    plan += [(lambda _: edge_pick(), 0), (lambda _: edge_pack(), 0), (edge_blend, 0), (raised, 0), (edge_blend, 1), (raised, 1),
             (edge_blend, 2), (raised, 2), (lifted, 0), (raised, 3), (lambda _: edge_lift(), 0), (lifted, 1), (raised, 4),
             (lifted, 2), (raised, 5), (lambda _: edge_finish(), 0), (lifted, 3), (raised, 6), (finished, 0),
             (lifted, 4), (raised, 7), (finished, 1), (finished, 2), (mid, 0), (finished, 3)]
    for action, n in plan:
        action(n)

    halves = group // steps
    share_out = blocks_out // group

    def step(i, u, e, last):
        n = i // halves
        shrink_at = (i % halves) * (blocks_out // halves) + u * share_out
        emit(n, (i % halves) * steps + u, u)
        for o in range(share_out):
            shrink(n + 1, shrink_at + o)
        if last is None:
            raise_row(e + 8, u)
        if last is None or last + 4 < fr + 2:
            finish(e + 4, (u + 4) % steps)
        if last is None or last + 1 < fr:
            mid((u + 1) % steps)
        if last is None or last + 5 < fr + 2:
            lift((u + 5) % steps, u + 5)

    trips = fr // steps

    def begin(i):
        @pl.when(jnp.logical_and(i % halves == 0, i >= 3 * halves))
        def _():
            flushed(i // halves - 3).wait()

    def finish_trip(i):
        @pl.when(jnp.logical_and(i % halves == halves - 1, i >= halves))
        def _():
            flushed(i // halves - 1).start()

    def trip(i, _):
        begin(i)
        for u in range(steps):
            step(i, u, i * steps + u, None)
        finish_trip(i)
        return 0

    lax.fori_loop(0, trips - 1, trip, 0)
    groups = fr // group
    last = groups - 1
    if groups >= 3:
        flushed(groups - 3).wait()
    for u in range(steps):
        step(trips - 1, u, (trips - 1) * steps + u, fr - steps + u)
    if groups >= 2:
        flushed(groups - 2).start()
    parts = [pltpu.make_async_copy(
        stage.at[last % 2, pl.ds(h * ch // 4, ch // 4)],
        out.at[0, pl.ds(h * ch // 4, ch // 4), pl.ds(last * group, group), :], sems.at[2 + h]) for h in range(4)]
    for h in range(4):
        for o in range(blocks_out // 4):
            shrink(last, h * (blocks_out // 4) + o)
        parts[h].start()
    if groups >= 2:
        flushed(groups - 2).wait()
    for copy in parts:
        copy.wait()


def tile_program(dims, prepared):
    cin, ch, nout, fr, fl = dims
    got, lon, liftw = prepared[0], prepared[9], prepared[6]
    lines_n = got.shape[0]
    cw = lon.shape[0]
    blocks = prepared[4].shape[0]
    count = lines_n - 2 * (blocks + 1)
    group = 8
    steps = 4
    vmem = pl.BlockSpec(memory_space=pltpu.VMEM)
    slab = liftw.shape[1] // 3
    return pl.pallas_call(
        functools.partial(tile_kernel, dims),
        out_shape=jax.ShapeDtypeStruct((1, ch, fr, fl), BF16),
        in_specs=[vmem] * len(prepared),
        out_specs=pl.BlockSpec(memory_space=pl.ANY),
        scratch_shapes=[
            pltpu.VMEM((lines_n, cin, cw), F32),
            pltpu.VMEM((2, lines_n, 3 * cin, cw), F32),
            pltpu.VMEM((count, cin, cw), BF16),
            pltpu.VMEM((count, cin, fl), F32),
            pltpu.VMEM((steps, slab, fl), BF16),
            pltpu.VMEM((3 * slab, 128), BF16),
            pltpu.VMEM((steps, 3 * ch, fl), BF16),
            pltpu.VMEM((16, fl), BF16),
            pltpu.VMEM((steps, ch, fl), F32),
            pltpu.VMEM((2, ch, fl), F32),
            pltpu.VMEM((ch, 128), BF16),
            pltpu.VMEM((2, fl // 128, ch * group, 128), F32),
            pltpu.VMEM((2, ch, group, fl), BF16),
            pltpu.SemaphoreType.DMA((6,)),
        ],
        compiler_params=pltpu.CompilerParams(vmem_limit_bytes=44_000_000),
    )(*prepared)


def per_device(
    coarse, reg_gain, reg_weight, reg_bias, noisy, lift_weight, lift_bias, mid_gain, mid_weight, mid_bias,
):
    lifts = lift_weight.transpose(0, 1, 3, 2)
    prepared = first_program(
        coarse, noisy, reg_gain, reg_bias, reg_weight.reshape((-1,) + reg_weight.shape[3:]),
        lift_bias[None], mid_gain[None], mid_bias[None],
        lifts.reshape((9,) + lifts.shape[2:]), mid_weight.reshape((9,) + mid_weight.shape[2:]))
    return tile_program((coarse.shape[0], mid_weight.shape[2]) + noisy.shape[1:], prepared)


def solution(mesh):
    placed = (
        P(None, ("grp", "lat"), None),
        P(),
        P(),
        P(),
        P(("grp", "lat"), None, None, None),
        P(),
        P(),
        P(),
        P(),
        P(),
    )
    return jax.shard_map(
        per_device,
        mesh=mesh,
        in_specs=placed,
        out_specs=P(("grp", "lat"), None, None, None),
        check_vma=False,
    )
```
